1024 devices in a mesh: gx: 16 (over z), gy: 8 (over y), gz: 8 (over x, core).
Axes of the slice: x: 4, y: 8, z: 16, core: 2. Of those that a mesh axis runs over, the one named last changes fastest.
Arguments:
- residual: float32 [256, 128, 1024], P('gx', 'gy', 'gz'), may hold values from -6 to 6
- solution: float32 [256, 128, 1024], P('gx', 'gy', 'gz'), may hold values from -6 to 6
- direction: float32 [256, 128, 1024], P('gx', 'gy', 'gz'), may hold values from -6 to 6
- conductance: float32 [3, 256, 128, 1024], P(None, 'gx', 'gy', 'gz'), may hold values from 0.3 to 3
- mass_term: float32 [256, 128, 1024], P('gx', 'gy', 'gz'), may hold values from 0.2 to 1
- eigen_basis: float32 [10, 10], replicated, may hold values from -2 to 2
- inverse_eigen_sums: float32 [320, 160, 1280], P('gx', 'gy', 'gz'), may hold values from 0.1 to 1
- element_coarse_index: int32 [32, 16, 128], P('gx', 'gy', 'gz'), may hold values from 0 to 63
- xxt_values: float32 [8192, 64, 128], P(('gx', 'gy', 'gz')), may hold values from -0.0625 to 0.0625
- xxt_blocks: int32 [8192], P(('gx', 'gy', 'gz')), may hold values from 0 to 511
- prior_inner: float32 [1], replicated, may hold values from 13107200 to 52428800
Outputs:
- new_solution: float32 [256, 128, 1024], P('gx', 'gy', 'gz')
- new_residual: float32 [256, 128, 1024], P('gx', 'gy', 'gz')
- new_direction: float32 [256, 128, 1024], P('gx', 'gy', 'gz')
The draws below stay inside these ranges and needn't reach their ends.
Inputs may be any that keep to these rules, and one draw needn't show every extreme that they name: `element_coarse_index`: an element's coarse unknown is one of the 64 of the device that holds the element. `xxt_blocks`: block numbers of the coarse vector, repeats allowed.
All inputs are finite; a program needn't handle non-finite values.
Results may differ from the reference program's by a relative error of at most 0.00011.
Values sent between devices are 32-bit elements; how exact they have to be, the bound alone decides.
No kernel may reach another device: no remote copies, remote signals or barrier semaphores. Data moves between devices by JAX's collectives and lax.ppermute only.
A program may use at most 32 MiB of HBM per device.

```python
import math
import jax
import jax.numpy as jnp
import numpy as np
from jax import lax

ELEMENT_NODES = 8
EX = 2
EY = 2
DEVICE_DEPTH_ELS = 16
DEVICE_COARSE = 64
BS = 128
XB = 8
LENGTH_ELEMENTS = 32
ACROSS_ELEMENTS = 16
DEPTH_ELEMENTS = 128
LENGTH_NODES = 256
ACROSS_NODES = 128
DEPTH_NODES = 1024
NC = 65536
NB = 512
N_GX = 16
N_GY = 8
N_GZ = 8
DEVICES = 1024


def touch_ends(values, own_key, least, largest):
    place = [jax.random.randint(jax.random.fold_in(own_key, axis), (), 0, length) for axis, length in enumerate(values.shape)]
    main_axis = values.shape.index(max(values.shape))
    neighbour = place[:main_axis] + [(place[main_axis] + 1) % values.shape[main_axis]] + place[main_axis + 1:]
    return values.at[tuple(place)].set(least).at[tuple(neighbour)].set(largest)


def shard_levels(rng, dims, pieces, smallest, top_value):
    loudness = 1.0
    for axis_at, shards_of in pieces:
        steps = jax.random.uniform(jax.random.fold_in(jax.random.fold_in(rng, 6), axis_at), (shards_of,), jnp.float32, smallest / len(pieces), top_value / len(pieces))
        loudness = loudness * jnp.repeat(jnp.exp(steps), dims[axis_at] // shards_of).reshape((-1,) + (1,) * (len(dims) - 1 - axis_at))
    return loudness


def normal_values(key, extent, width, limit, split=(), kind=jnp.bfloat16):
    drawn = jax.random.normal(key, extent, jnp.float32) * width
    if len(split) > 0:
        drawn = shard_levels(key, extent, split, -0.22, 0.18) * drawn
    return jnp.clip(drawn, min=-limit, max=limit).astype(kind)


def setup_inputs(seed: int = 0) -> dict:
    seeds = jax.random.split(jax.random.key(seed), 12)
    return {
        "residual": normal_values(seeds[0], (LENGTH_NODES, ACROSS_NODES, DEPTH_NODES), 1.0, 6.0, ((0, 16), (1, 8), (2, 8)), jnp.float32),
        "solution": normal_values(seeds[1], (LENGTH_NODES, ACROSS_NODES, DEPTH_NODES), 1.0, 6.0, ((0, 16), (1, 8), (2, 8)), jnp.float32),
        "direction": normal_values(seeds[2], (LENGTH_NODES, ACROSS_NODES, DEPTH_NODES), 1.0, 6.0, ((0, 16), (1, 8), (2, 8)), jnp.float32),
        "conductance": jnp.clip(jnp.exp(math.log(3.0) - 2.3025851 * jax.random.uniform(seeds[3], (3, LENGTH_NODES, ACROSS_NODES, DEPTH_NODES), jnp.float32) ** shard_levels(seeds[3], (3, LENGTH_NODES, ACROSS_NODES, DEPTH_NODES), ((1, 16), (2, 8), (3, 8)), -0.2, 0.2)), 0.3, 3.0),
        "mass_term": jnp.clip(0.2 + 0.8 * jax.random.uniform(seeds[4], (LENGTH_NODES, ACROSS_NODES, DEPTH_NODES), jnp.float32) ** shard_levels(seeds[4], (LENGTH_NODES, ACROSS_NODES, DEPTH_NODES), ((0, 16), (1, 8), (2, 8)), -0.2, 0.2), 0.2, 1.0),
        "eigen_basis": normal_values(seeds[5], (ELEMENT_NODES + 2, ELEMENT_NODES + 2), (ELEMENT_NODES + 2) ** -0.5, 2.0, (), jnp.float32),
        "inverse_eigen_sums": jnp.clip(jnp.exp(math.log(1.0) - 2.3025851 * jax.random.uniform(seeds[6], ((ELEMENT_NODES + 2) * LENGTH_ELEMENTS, (ELEMENT_NODES + 2) * ACROSS_ELEMENTS, (ELEMENT_NODES + 2) * DEPTH_ELEMENTS), jnp.float32) ** shard_levels(seeds[6], ((ELEMENT_NODES + 2) * LENGTH_ELEMENTS, (ELEMENT_NODES + 2) * ACROSS_ELEMENTS, (ELEMENT_NODES + 2) * DEPTH_ELEMENTS), ((0, 16), (1, 8), (2, 8)), -0.2, 0.2)), 0.1, 1.0),
        "element_coarse_index": touch_ends(jax.random.randint(seeds[7], (LENGTH_ELEMENTS, ACROSS_ELEMENTS, DEPTH_ELEMENTS), 0, DEVICE_COARSE), jax.random.fold_in(seeds[7], 1), 0, DEVICE_COARSE - 1).astype(jnp.int32),
        "xxt_values": normal_values(seeds[8], (XB * DEVICES, DEVICE_COARSE, BS), (DEVICE_COARSE * 128) ** -0.5, 0.0625, ((0, 1024),), jnp.float32),
        "xxt_blocks": touch_ends(jax.random.randint(seeds[9], (XB * DEVICES,), 0, NB), jax.random.fold_in(seeds[9], 1), 0, NB - 1).astype(jnp.int32),
        "prior_inner": jnp.clip(jnp.exp(jax.random.uniform(seeds[10], (1,), jnp.float32, math.log(13107200), math.log(52428800))), 13107200, 52428800),
    }


HIGH = lax.Precision.HIGHEST


def cheb_matrix():
    count = 8
    points = np.cos(np.pi * np.arange(count) / (count - 1))
    signs = np.array([2.0, 1, 1, 1, 1, 1, 1, 2.0]) * (-1.0) ** np.arange(count)
    differ = points[:, None] - points[None, :] + np.eye(count)
    matrix = np.outer(signs, 1.0 / signs) / differ
    matrix = matrix - np.eye(count) * np.sum(matrix, axis=1)[:, None]
    return (0.25 * matrix).astype(np.float32)


def extended_index(count):
    parts = [np.array([8 * element] + list(range(8 * element + 2, 8 * element + 10)) + [8 * element + 11]) for element in range(count)]
    return np.concatenate(parts).astype(np.int32)


def inside_index(count):
    parts = [np.arange(10 * element + 1, 10 * element + 9) for element in range(count)]
    return np.concatenate(parts).astype(np.int32)


def assemble_padded(padded):
    result = padded
    for which_axis in range(3):
        length = result.shape[which_axis] - 2
        position = np.arange(length) % 8
        shape_list = [1, 1, 1]
        shape_list[which_axis] = length
        upper = jnp.asarray((position == 7).astype(np.float32).reshape(shape_list))
        lower = jnp.asarray((position == 0).astype(np.float32).reshape(shape_list))
        centre = lax.slice_in_dim(result, 1, length + 1, axis=which_axis)
        above = lax.slice_in_dim(result, 2, length + 2, axis=which_axis)
        below = lax.slice_in_dim(result, 0, length, axis=which_axis)
        result = centre + upper * above + lower * below
    return result


def along_axis(matrix, values, which_axis):
    moved = jnp.moveaxis(values, which_axis, -1)
    width_one = matrix.shape[1]
    blocks = moved.reshape(moved.shape[:-1] + (moved.shape[-1] // width_one, width_one))
    mapped = jnp.einsum('ij,...ej->...ei', matrix, blocks, precision=HIGH)
    return jnp.moveaxis(mapped.reshape(moved.shape), -1, which_axis)


def local_operator(values, conductance, mass_term, matrix):
    total = mass_term * values
    for which_axis in range(3):
        grad = along_axis(matrix, values, which_axis)
        total = total + along_axis(matrix.T, conductance[which_axis] * grad, which_axis)
    return total


def reference(residual, solution, direction, conductance, mass_term, eigen_basis, inverse_eigen_sums, element_coarse_index, xxt_values, xxt_blocks, prior_inner):
    matrix = jnp.asarray(cheb_matrix())
    devices_all = N_GX * N_GY * N_GZ
    padded = jnp.pad(residual, 2)
    extended_element = jnp.take(padded, jnp.asarray(extended_index(LENGTH_ELEMENTS)), axis=0)
    extended_element = jnp.take(extended_element, jnp.asarray(extended_index(ACROSS_ELEMENTS)), axis=1)
    extended_element = jnp.take(extended_element, jnp.asarray(extended_index(DEPTH_ELEMENTS)), axis=2)
    spectral = extended_element
    for which_axis in range(3):
        spectral = along_axis(eigen_basis.T, spectral, which_axis)
    spectral = inverse_eigen_sums * spectral
    for which_axis in range(3):
        spectral = along_axis(eigen_basis, spectral, which_axis)
    local_solution = spectral
    device_portion = jnp.take(local_solution, jnp.asarray(inside_index(LENGTH_ELEMENTS)), axis=0)
    device_portion = jnp.take(device_portion, jnp.asarray(inside_index(ACROSS_ELEMENTS)), axis=1)
    device_portion = jnp.take(device_portion, jnp.asarray(inside_index(DEPTH_ELEMENTS)), axis=2)
    element_sum = residual.reshape(LENGTH_ELEMENTS, 8, ACROSS_ELEMENTS, 8, DEPTH_ELEMENTS, 8).sum(axis=(1, 3, 5))
    dev_x = (jnp.arange(LENGTH_ELEMENTS) // EX).astype(jnp.int32)
    dev_y = (jnp.arange(ACROSS_ELEMENTS) // EY).astype(jnp.int32)
    device_depth = (jnp.arange(DEPTH_ELEMENTS) // DEVICE_DEPTH_ELS).astype(jnp.int32)
    owner = (dev_x[:, None, None] * N_GY + dev_y[None, :, None]) * N_GZ + device_depth[None, None, :]
    global_ids = (owner * DEVICE_COARSE + element_coarse_index).astype(jnp.int32)
    coarse_residual = jnp.zeros((NC,), jnp.float32).at[global_ids.ravel()].add(element_sum.ravel())
    values_four = xxt_values.reshape(devices_all, XB, DEVICE_COARSE, BS)
    contrib = jnp.einsum('dknb,dn->dkb', values_four, coarse_residual.reshape(devices_all, DEVICE_COARSE), precision=HIGH)
    coarse_inner = jnp.zeros((NB, BS), jnp.float32).at[xxt_blocks].add(contrib.reshape(devices_all * XB, BS))
    picked = coarse_inner[xxt_blocks].reshape(devices_all, XB, BS)
    coarse_solution = jnp.einsum('dknb,dkb->dn', values_four, picked, precision=HIGH).ravel()
    element_coarse = coarse_solution[global_ids]
    spread_values = jnp.broadcast_to(element_coarse[:, None, :, None, :, None], (LENGTH_ELEMENTS, 8, ACROSS_ELEMENTS, 8, DEPTH_ELEMENTS, 8)).reshape(LENGTH_NODES, ACROSS_NODES, DEPTH_NODES)
    preconditioned = device_portion + spread_values
    inner = jnp.sum(extended_element * local_solution) + jnp.sum(coarse_inner * coarse_inner)
    new_direction = preconditioned + (inner / prior_inner[0]) * direction
    image = local_operator(new_direction, conductance, mass_term, matrix)
    curvature = jnp.sum(new_direction * image)
    alpha = inner / curvature
    new_solution = solution + alpha * new_direction
    new_residual = residual - alpha * assemble_padded(jnp.pad(image, 1))
    return new_solution, new_residual, new_direction
```

```python
import jax
import jax.numpy as jnp
import numpy as np
from jax import lax
from jax.sharding import PartitionSpec as P

HIGH = lax.Precision.HIGHEST
N = 8
E = 10


def cheb_matrix():
    count = 8
    points = np.cos(np.pi * np.arange(count) / (count - 1))
    signs = np.array([2.0, 1, 1, 1, 1, 1, 1, 2.0]) * (-1.0) ** np.arange(count)
    differ = points[:, None] - points[None, :] + np.eye(count)
    matrix = np.outer(signs, 1.0 / signs) / differ
    matrix = matrix - np.eye(count) * np.sum(matrix, axis=1)[:, None]
    return (0.25 * matrix).astype(np.float32)


def extended_positions(count):
    length = N * count
    result = []
    for element in range(count):
        for node in [N * element - 2, *range(N * element, N * element + N), N * element + N + 1]:
            result.append(length if node < 0 else length + 1 if node >= length else node)
    return np.array(result)


def one_hot(index, size):
    return (np.asarray(index)[:, None] == np.arange(size)[None, :]).astype(np.float32)


def dot(a, b):
    return jnp.dot(a, b, precision=HIGH)


def shifts(axis):
    count = lax.axis_size(axis)
    forward = [(i, i + 1) for i in range(count - 1)]
    return forward, [(b, a) for a, b in forward]


def exchange(to_high, to_low, axis):
    forward, backward = shifts(axis)
    return lax.ppermute(to_high, axis, forward), lax.ppermute(to_low, axis, backward)


def spread(values, axes):
    return lax.all_to_all(values, axes, 0, 0, tiled=False)


def broadcast_sum(values, axes):
    count = lax.axis_size(axes)
    return jnp.sum(spread(jnp.broadcast_to(values[None], (count, *values.shape)), axes), axis=0)


def local_operator(values, conductance, mass_term, cheb, kx, ky, kz):
    rows = values.shape[0] * values.shape[1]
    flat = values.reshape(rows, -1)
    along_xy = dot(jnp.asarray(np.concatenate([kx, ky], axis=0)), flat)
    along_xy = along_xy * conductance[:2].reshape(2 * rows, -1)
    along_z = dot(flat, jnp.asarray(kz.T)) * conductance[2].reshape(rows, -1)
    total = mass_term.reshape(rows, -1) * flat
    total = total + dot(jnp.asarray(np.concatenate([kx.T, ky.T], axis=1)), along_xy)
    total = total + dot(along_z, jnp.asarray(kz))
    return total.reshape(values.shape)


def assemble_inside(values, axis, low, high):
    length = values.shape[axis]
    above = jnp.concatenate([lax.slice_in_dim(values, 1, length, axis=axis), high], axis=axis)
    below = jnp.concatenate([low, lax.slice_in_dim(values, 0, length - 1, axis=axis)], axis=axis)
    position = lax.broadcasted_iota(jnp.int32, values.shape, axis) % N
    return values + jnp.where(position == N - 1, above, jnp.where(position == 0, below, 0.0))


def body(
    residual,
    solution,
    direction,
    conductance,
    mass_term,
    eigen_basis,
    inverse_eigen_sums,
    element_coarse_index,
    xxt_values,
    xxt_blocks,
    prior_inner,
):
    nx, ny, nz = residual.shape
    ex, ey, ez = nx // N, ny // N, nz // N
    rows = nx * ny
    plane = ("gy", "gz")
    n_plane = lax.axis_size(plane)
    coarse_count, block = xxt_values.shape[1:]
    n_blocks = coarse_count * lax.axis_size(("gx", "gy", "gz")) // block
    own_blocks = n_blocks // n_plane
    flat = residual.reshape(rows, nz)

    x_low, x_high = exchange(residual[nx - 2], residual[1], "gx")

    agg_xy = one_hot((np.arange(rows) // ny // N) * ey + (np.arange(rows) % ny) // N, ex * ey)
    agg_z = one_hot(np.arange(nz) // N, ez)
    element_sum = dot(dot(jnp.asarray(agg_xy.T), flat), jnp.asarray(agg_z))
    ids = element_coarse_index.reshape(ex * ey, ez)
    onehot_ids = (ids[..., None] == jnp.arange(coarse_count, dtype=jnp.int32)).astype(jnp.float32)
    coarse_residual = jnp.sum(onehot_ids * element_sum[..., None], axis=(0, 1))
    contrib = jnp.sum(xxt_values * coarse_residual[None, :, None], axis=1)
    place = (xxt_blocks[None, :] == jnp.arange(n_blocks, dtype=jnp.int32)[:, None]).astype(
        jnp.float32
    )
    partial_inner = dot(place, contrib).reshape(n_plane, own_blocks, block)

    y_low, y_high = exchange(
        jnp.concatenate([residual[:, ny - 2], x_low[ny - 2][None], x_high[ny - 2][None]]),
        jnp.concatenate([residual[:, 1], x_low[1][None], x_high[1][None]]),
        "gy",
    )
    partial_inner = jnp.sum(spread(partial_inner, plane), axis=0)

    every = jnp.concatenate([flat, x_low, x_high, y_low, y_high])
    picks = one_hot([nz - 2, 1], nz)
    ends = jnp.einsum("kl,rl->kr", jnp.asarray(picks), every, precision=HIGH)
    z_low, z_high = exchange(ends[:1], ends[1:], "gz")
    partial_inner = broadcast_sum(partial_inner, "gx")
    coarse_inner = spread(
        jnp.broadcast_to(partial_inner[None], (n_plane, own_blocks, block)), plane
    ).reshape(n_blocks, block)

    cols_x = np.concatenate(
        [np.repeat(np.arange(nx), ny), np.full(ny, nx), np.full(ny, nx + 1), *[np.arange(nx + 2)] * 2]
    )
    cols_y = np.concatenate(
        [
            np.tile(np.arange(ny), nx),
            *[np.arange(ny)] * 2,
            np.full(nx + 2, ny),
            np.full(nx + 2, ny + 1),
        ]
    )

    def blocks_of(count, matrix):
        mask = np.kron(np.eye(count), np.ones((E, E))).astype(np.float32)
        return jnp.tile(matrix, (count, count)) * mask

    pos_x, pos_y, pos_z = extended_positions(ex), extended_positions(ey), extended_positions(ez)
    n_ext_x, n_ext_y, n_ext_z = E * ex, E * ey, E * ez
    row_x = one_hot(np.repeat(np.arange(n_ext_x), n_ext_y), n_ext_x)
    row_y = one_hot(np.tile(np.arange(n_ext_y), n_ext_x), n_ext_y)
    col_x = (pos_x[:, None] == cols_x[None, :]).astype(np.float32)
    col_y = (pos_y[:, None] == cols_y[None, :]).astype(np.float32)
    basis_x, basis_y = blocks_of(ex, eigen_basis), blocks_of(ey, eigen_basis)
    basis_z = blocks_of(ez, eigen_basis)
    to_x = dot(jnp.asarray(row_x), dot(basis_x.T, jnp.asarray(col_x)))
    to_y = dot(jnp.asarray(row_y), dot(basis_y.T, jnp.asarray(col_y)))
    to_spectral = to_x * to_y
    inside_x = np.concatenate([np.arange(E * e + 1, E * e + N + 1) for e in range(ex)])
    inside_y = np.concatenate([np.arange(E * e + 1, E * e + N + 1) for e in range(ey)])
    inside_z = np.concatenate([np.arange(E * e + 1, E * e + N + 1) for e in range(ez)])
    out_x = one_hot(np.repeat(inside_x, ny), n_ext_x)
    out_y = one_hot(np.tile(inside_y, nx), n_ext_y)
    from_spectral = dot(dot(jnp.asarray(out_x), basis_x), jnp.asarray(row_x.T)) * dot(
        dot(jnp.asarray(out_y), basis_y), jnp.asarray(row_y.T)
    )
    col_z = one_hot(pos_z, nz + 2)
    to_z = dot(jnp.asarray(col_z.T), basis_z)
    from_z = dot(basis_z.T, jnp.asarray(one_hot(inside_z, n_ext_z).T))
    ends_in = jnp.concatenate([z_low, z_high])
    spectral = dot(dot(to_spectral, every), to_z[:nz])
    ends_spectral = jnp.einsum("sr,kr->sk", to_spectral, ends_in, precision=HIGH)
    spectral = spectral + dot(ends_spectral, to_z[nz:])
    weighted = inverse_eigen_sums.reshape(n_ext_x * n_ext_y, n_ext_z) * spectral
    inner_local = jnp.sum(weighted * spectral)
    local_part = dot(dot(from_spectral, weighted), from_z)

    picked = dot(place.T, coarse_inner)
    coarse_solution = jnp.sum(xxt_values * picked[:, None, :], axis=(0, 2))
    element_coarse = jnp.sum(onehot_ids * coarse_solution, axis=-1)
    spread_values = dot(dot(jnp.asarray(agg_xy), element_coarse), jnp.asarray(agg_z.T))
    preconditioned = (local_part + spread_values).reshape(residual.shape)

    cheb = cheb_matrix()
    kx = np.kron(np.kron(np.eye(ex, dtype=np.float32), cheb), np.eye(ny, dtype=np.float32))
    ky = np.kron(np.eye(nx, dtype=np.float32), np.kron(np.eye(ey, dtype=np.float32), cheb))
    kz = np.kron(np.eye(ez, dtype=np.float32), cheb)
    image_direction = local_operator(direction, conductance, mass_term, cheb, kx, ky, kz)
    image = local_operator(preconditioned, conductance, mass_term, cheb, kx, ky, kz)

    images = jnp.stack([image, image_direction])
    low, high = exchange(images[:, nx - 1 :], images[:, :1], "gx")
    terms = jnp.stack(
        [
            inner_local,
            jnp.sum(preconditioned * image),
            jnp.sum(preconditioned * image_direction + direction * image),
            jnp.sum(direction * image_direction),
        ]
    )
    terms = broadcast_sum(jnp.broadcast_to(terms[:, None], (4, 128)), plane)
    images = assemble_inside(images, 1, low, high)
    low, high = exchange(images[:, :, ny - 1 :], images[:, :, :1], "gy")
    terms = broadcast_sum(terms, "gx")[:, 0]
    images = assemble_inside(images, 2, low, high)
    low, high = exchange(images[:, :, :, nz - 1], images[:, :, :, 0], "gz")
    images = assemble_inside(images, 3, low[..., None], high[..., None])

    inner = terms[0] + jnp.sum(coarse_inner * coarse_inner)
    ratio = inner / prior_inner[0]
    curvature = terms[1] + ratio * terms[2] + ratio * ratio * terms[3]
    alpha = inner / curvature
    new_direction = preconditioned + ratio * direction
    new_solution = solution + alpha * new_direction
    new_residual = residual - alpha * (images[0] + ratio * images[1])
    return (new_solution, new_residual, new_direction)


def solution(mesh):
    whole = P("gx", "gy", "gz")
    in_specs = (
        whole,
        whole,
        whole,
        P(None, "gx", "gy", "gz"),
        whole,
        P(),
        whole,
        whole,
        P(("gx", "gy", "gz"), None, None),
        P(("gx", "gy", "gz")),
        P(),
    )
    return jax.shard_map(
        body, mesh=mesh, in_specs=in_specs, out_specs=(whole, whole, whole), check_vma=False
    )
```

```python
import jax
import jax.numpy as jnp
import numpy as np
from jax import lax
from jax.experimental import pallas as pl
from jax.experimental.pallas import tpu as pltpu
from jax.sharding import PartitionSpec as P

HIGH = lax.Precision.HIGHEST
N = 8
E = 10
F32 = jnp.float32


def cheb_matrix():
    count = 8
    points = np.cos(np.pi * np.arange(count) / (count - 1))
    signs = np.array([2.0, 1, 1, 1, 1, 1, 1, 2.0]) * (-1.0) ** np.arange(count)
    differ = points[:, None] - points[None, :] + np.eye(count)
    matrix = np.outer(signs, 1.0 / signs) / differ
    matrix = matrix - np.eye(count) * np.sum(matrix, axis=1)[:, None]
    return (0.25 * matrix).astype(np.float32)


def extended_positions(count):
    length = N * count
    result = []
    for element in range(count):
        for node in [N * element - 2, *range(N * element, N * element + N), N * element + N + 1]:
            result.append(length if node < 0 else length + 1 if node >= length else node)
    return np.array(result)


def inside_positions(count):
    return np.concatenate([np.arange(E * e + 1, E * e + N + 1) for e in range(count)])


def one_hot(index, size):
    return (np.asarray(index)[:, None] == np.arange(size)[None, :]).astype(np.float32)


def up8(count):
    return -(-count // 8) * 8


def mm(a, b, ca=1, cb=0):
    return lax.dot_general(
        a, b, (((ca,), (cb,)), ((), ())), precision=HIGH, preferred_element_type=F32
    )


def call(kernel, name, outs, *args, smem=(), flops=0):
    specs = [
        pl.BlockSpec(memory_space=pltpu.SMEM if i in smem else pltpu.VMEM)
        for i in range(len(args))
    ]
    moved = sum(int(np.prod(a.shape)) * 4 for a in args)
    moved += sum(int(np.prod(s)) * 4 for s in outs)
    return pl.pallas_call(
        kernel,
        out_shape=[jax.ShapeDtypeStruct(s, F32) for s in outs],
        in_specs=specs,
        out_specs=[pl.BlockSpec(memory_space=pltpu.VMEM)] * len(outs),
        cost_estimate=pl.CostEstimate(flops=flops, bytes_accessed=moved, transcendentals=0),
        compiler_params=pltpu.CompilerParams(vmem_limit_bytes=16 * 2**20),
        name=name,
    )(*args)


def coarse_kernel(blocks, residual, ids, values, out, ids_wide):
    nx, ny, nz = residual.shape
    ex, ey = nx // N, ny // N
    ez = ids.shape[1]
    n_stored, coarse, _ = values.shape
    widen = (
        lax.broadcasted_iota(jnp.int32, (ez, nz), 1) // N
        == lax.broadcasted_iota(jnp.int32, (ez, nz), 0)
    ).astype(F32)
    wide = mm(ids[...].astype(F32), widen)
    ids_wide[...] = wide
    unknown = lax.broadcasted_iota(jnp.int32, (coarse, nz), 0).astype(F32)
    total = jnp.zeros((coarse, nz), F32)
    for a in range(ex):
        for b in range(ey):
            part = jnp.sum(residual[a * N : a * N + N, b * N : b * N + N, :], axis=(0, 1))[None]
            q = a * ey + b
            total = total + jnp.where(jnp.abs(unknown - wide[q : q + 1]) < 0.5, part, 0.0)
    coarse_residual = jnp.sum(total, axis=1, keepdims=True)
    out[...] = jnp.zeros_like(out)
    for k in range(n_stored):
        row = jnp.sum(values[k] * coarse_residual, axis=0, keepdims=True)
        at = pl.ds(blocks[k], 1)
        out[at, :] = out[at, :] + row


def sum_spread_kernel(parts, out):
    total = jnp.sum(parts[...], axis=0)
    for i in range(out.shape[0]):
        out[i] = total


def across_faces_kernel(residual, low, high, to_high, to_low):
    nx, ny, nz = residual.shape
    for out, y in ((to_high, ny - 2), (to_low, 1)):
        out[...] = jnp.zeros_like(out)
        out[:nx] = residual[:, y, :]
        out[nx : nx + 1] = low[y : y + 1]
        out[nx + 1 : nx + 2] = high[y : y + 1]


def depth_faces_kernel(residual, x_low, x_high, y_low, y_high, every, to_high, to_low):
    nx, ny, nz = residual.shape
    at = 0
    for ref, count in ((None, nx * ny), (x_low, ny), (x_high, ny), (y_low, None), (y_high, None)):
        block = residual[...].reshape(nx * ny, nz) if ref is None else ref[...]
        every[at : at + block.shape[0]] = block
        at += block.shape[0]
    row = lax.broadcasted_iota(jnp.int32, (8, nz), 0)
    lane = lax.broadcasted_iota(jnp.int32, (8, nz), 1)
    pick = ((row == 0) & (lane == nz - 2)) | ((row == 1) & (lane == 1))
    ends = mm(pick.astype(F32), every[...], 1, 1)
    to_high[...] = ends[0:1]
    to_low[...] = ends[1:2]


def matrices_kernel(
    basis, tile2, mask2, tilez, maskz, row_x, row_y, col_x, col_y, out_x, out_y, col_z, in_z,
    to_spectral, from_spectral, to_z, from_z,
):
    flat2 = mm(mm(tile2[...], basis[...]), tile2[...], 1, 1) * mask2[...]
    flatz = mm(mm(tilez[...], basis[...]), tilez[...], 1, 1) * maskz[...]
    to_x = mm(row_x[...], mm(flat2, col_x[...], 0, 0))
    to_y = mm(row_y[...], mm(flat2, col_y[...], 0, 0))
    to_spectral[...] = to_x * to_y
    from_x = mm(mm(out_x[...], flat2), row_x[...], 1, 1)
    from_y = mm(mm(out_y[...], flat2), row_y[...], 1, 1)
    from_spectral[...] = from_x * from_y
    to_z[...] = mm(col_z[...], flatz)
    from_z[...] = mm(flatz, in_z[...], 0, 0)


def solve_kernel(
    every, z_low, z_high, to_spectral, from_spectral, to_z, from_z, sums, local_part, inner, wide
):
    nz = every.shape[1]
    n_x, n_y, n_z = sums.shape
    wide[...] = jnp.zeros_like(wide)
    wide[:, :n_y, :] = sums[...]
    weights = wide[...].reshape(-1, n_z)
    row = lax.broadcasted_iota(jnp.int32, (8, every.shape[0]), 0)
    ends = jnp.where(row == 0, z_low[...], jnp.where(row == 1, z_high[...], 0.0))
    spectral = mm(mm(to_spectral[...], every[...]), to_z[:nz, :])
    spectral = spectral + mm(mm(to_spectral[...], ends, 1, 1), to_z[nz:, :])
    weighted = weights * spectral
    inner[...] = jnp.sum(jnp.sum(weighted * spectral, axis=0, keepdims=True), axis=1, keepdims=True)
    local_part[...] = mm(mm(from_spectral[...], weighted), from_z[...])


def operator(flat, conductance, mass, kxy, kz):
    rows = flat.shape[0]
    along = mm(kxy[...], flat)
    along_x = along[:rows] * conductance[0].reshape(rows, -1)
    along_y = along[rows:] * conductance[1].reshape(rows, -1)
    along_z = mm(flat, kz[...], 1, 1) * conductance[2].reshape(rows, -1)
    total = mass[...].reshape(rows, -1) * flat + mm(along_z, kz[...])
    total = total + mm(kxy[:rows, :], along_x, 0, 0)
    return total + mm(kxy[rows:, :], along_y, 0, 0)


def operator_kernel(direction, conductance, mass, kxy, kz, image):
    rows = kxy.shape[1]
    flat = direction[...].reshape(rows, -1)
    image[...] = operator(flat, conductance, mass, kxy, kz).reshape(image.shape)


def total_of(values):
    return jnp.sum(jnp.sum(values, axis=0, keepdims=True), axis=1, keepdims=True)


def correct_kernel(
    blocks, coarse_inner, values, ids_wide, local_part, inner_local, direction, image_direction,
    conductance, mass, kxy, kz,
    z_out, image_out, to_high, to_low, terms, square,
):
    nx, ny, nz = direction.shape
    rows = nx * ny
    n_stored, coarse, block = values.shape
    total = jnp.zeros((coarse, block), F32)
    for k in range(n_stored):
        total = total + values[k] * coarse_inner[pl.ds(blocks[k], 1), :]
    solution = jnp.sum(total, axis=1, keepdims=True)
    unknown = lax.broadcasted_iota(jnp.int32, (coarse, nz), 0).astype(F32)
    ey = ny // N
    for a in range(nx // N):
        for b in range(ey):
            q = a * ey + b
            hit = jnp.abs(unknown - ids_wide[q : q + 1, :]) < 0.5
            line = jnp.sum(jnp.where(hit, solution, 0.0), axis=0, keepdims=True)
            for x in range(N):
                at = (a * N + x) * ny + b * N
                z_out[a * N + x, b * N : b * N + N, :] = local_part[at : at + N, :] + line
    flat = z_out[...].reshape(rows, nz)
    image = operator(flat, conductance, mass, kxy, kz)
    image_out[...] = image.reshape(nx, ny, nz)
    to_high[0] = image[rows - ny :]
    to_high[1] = image_direction[nx - 1]
    to_low[0] = image[:ny]
    to_low[1] = image_direction[0]
    old = direction[...].reshape(rows, nz)
    old_image = image_direction[...].reshape(rows, nz)
    first = total_of(flat * image)
    second = total_of(flat * old_image + old * image)
    third = total_of(old * old_image)
    lane = lax.broadcasted_iota(jnp.int32, (1, nz), 1)
    line = jnp.where(
        lane == 0,
        inner_local[...],
        jnp.where(lane == 1, first, jnp.where(lane == 2, second, jnp.where(lane == 3, third, 0.0))),
    )
    for i in range(terms.shape[0]):
        terms[i] = line
    square[...] = total_of(coarse_inner[...] * coarse_inner[...])


def assemble_length_kernel(image, image_direction, low, high, out, to_high, to_low):
    nx, ny, nz = image.shape
    for i, ref in ((0, image), (1, image_direction)):
        out[i] = ref[...]
        for x in range(nx):
            if x % N == N - 1:
                out[i, x] = ref[x] + (ref[x + 1] if x + 1 < nx else high[i])
            elif x % N == 0:
                out[i, x] = ref[x] + (ref[x - 1] if x else low[i])
        to_high[i] = out[i, :, ny - 1, :]
        to_low[i] = out[i, :, 0, :]


def assemble_across_kernel(images, low, high, out, to_high, to_low):
    _, nx, ny, nz = images.shape
    out[...] = images[...]
    for i in range(2):
        for y in range(ny):
            if y % N == N - 1:
                other = images[i, :, y + 1, :] if y + 1 < ny else high[i]
            elif y % N == 0:
                other = images[i, :, y - 1, :] if y else low[i]
            else:
                continue
            out[i, :, y, :] = images[i, :, y, :] + other
    row = lax.broadcasted_iota(jnp.int32, (8, nz), 0)
    lane = lax.broadcasted_iota(jnp.int32, (8, nz), 1)
    pick = ((row == 0) & (lane == nz - 1)) | ((row == 1) & (lane == 0))
    ends = mm(pick.astype(F32), out[...].reshape(2 * nx * ny, nz), 1, 1)
    to_high[...] = ends[0:1]
    to_low[...] = ends[1:2]


def update_kernel(
    prior, terms, square, images, low, high, residual, solution, direction, z,
    new_solution, new_residual, new_direction,
):
    nx, ny, nz = residual.shape
    rows = nx * ny
    lane1 = lax.broadcasted_iota(jnp.int32, (1, nz), 1)
    sums = jnp.sum(terms[...], axis=0)

    def term(i):
        return jnp.sum(jnp.where(lane1 == i, sums, 0.0), axis=1, keepdims=True)

    inner = term(0) + square[...]
    ratio = inner / prior[0]
    alpha = inner / (term(1) + ratio * term(2) + ratio * ratio * term(3))
    new = z[...].reshape(rows, nz) + ratio * direction[...].reshape(rows, nz)
    new_direction[...] = new.reshape(nx, ny, nz)
    new_solution[...] = (solution[...].reshape(rows, nz) + alpha * new).reshape(nx, ny, nz)
    image = images[0].reshape(rows, nz) + ratio * images[1].reshape(rows, nz)
    row = lax.broadcasted_iota(jnp.int32, (8, rows), 0)
    low_line = low[:, :rows] + ratio * low[:, rows:]
    high_line = high[:, :rows] + ratio * high[:, rows:]
    ends = jnp.where(row == 0, low_line, jnp.where(row == 1, high_line, 0.0))
    row = lax.broadcasted_iota(jnp.int32, (8, nz), 0)
    lane = lax.broadcasted_iota(jnp.int32, (8, nz), 1)
    place = ((row == 0) & (lane == 0)) | ((row == 1) & (lane == nz - 1))
    outer = mm(jnp.transpose(ends), place.astype(F32))
    lane = lax.broadcasted_iota(jnp.int32, (rows, nz), 1)
    above = pltpu.roll(image, nz - 1, 1)
    below = pltpu.roll(image, 1, 1)
    above = jnp.where((lane % N == N - 1) & (lane < nz - 1), above, 0.0)
    below = jnp.where((lane % N == 0) & (lane > 0), below, 0.0)
    image = image + above + below + outer
    new_residual[...] = (residual[...].reshape(rows, nz) - alpha * image).reshape(nx, ny, nz)


def shifts(axis):
    count = lax.axis_size(axis)
    forward = [(i, i + 1) for i in range(count - 1)]
    return forward, [(b, a) for a, b in forward]


def exchange(to_high, to_low, axis):
    forward, backward = shifts(axis)
    return lax.ppermute(to_high, axis, forward), lax.ppermute(to_low, axis, backward)


def spread(values, axes):
    return lax.all_to_all(values, axes, 0, 0, tiled=False)


def body(
    residual,
    solution,
    direction,
    conductance,
    mass_term,
    eigen_basis,
    inverse_eigen_sums,
    element_coarse_index,
    xxt_values,
    xxt_blocks,
    prior_inner,
):
    nx, ny, nz = residual.shape
    ex, ey, ez = nx // N, ny // N, nz // N
    rows = nx * ny
    plane = ("gy", "gz")
    n_plane, n_line = lax.axis_size(plane), lax.axis_size("gx")
    coarse_count, block = xxt_values.shape[1:]
    n_blocks = coarse_count * n_plane * n_line // block
    own = n_blocks // n_plane

    x_low, x_high = exchange(residual[nx - 2], residual[1], "gx")

    ids = element_coarse_index.reshape(ex * ey, ez)
    partial_inner, ids_wide = call(
        coarse_kernel, "coarse_restrict", [(n_blocks, block), (ex * ey, nz)],
        xxt_blocks, residual, ids, xxt_values, smem=(0,),
    )
    parts = spread(partial_inner.reshape(n_plane, own, block), plane)
    to_high, to_low = call(
        across_faces_kernel, "across_faces", [(up8(nx + 2), nz)] * 2, residual, x_low, x_high
    )
    y_low, y_high = exchange(to_high, to_low, "gy")

    face = up8(nx + 2)
    n_every = rows + 2 * ny + 2 * face
    pad = [-1] * (face - nx - 2)
    line = [*range(nx), nx, nx + 1, *pad]
    cols_x = np.array([*np.repeat(np.arange(nx), ny), *[nx] * ny, *[nx + 1] * ny, *line, *line])
    cols_y = np.array(
        [*np.tile(np.arange(ny), nx), *range(ny), *range(ny), *[ny] * face, *[ny + 1] * face]
    )
    n_x, n_y, n_z = inverse_eigen_sums.shape
    high_y = up8(n_y)
    place_y = np.tile(np.arange(high_y), n_x)
    row_x = one_hot(np.repeat(np.arange(n_x), high_y), n_x) * (place_y < n_y)[:, None]
    row_y = one_hot(place_y, n_y)
    col_x = (extended_positions(ex)[:, None] == cols_x[None, :]).astype(np.float32)
    col_y = (extended_positions(ey)[:, None] == cols_y[None, :]).astype(np.float32)
    assert ex == ey
    to_spectral, from_spectral, to_z, from_z = call(
        matrices_kernel, "basis_matrices",
        [(n_x * high_y, n_every), (rows, n_x * high_y), (nz + 8, n_z), (n_z, nz)],
        eigen_basis,
        *map(
            jnp.asarray,
            (
                np.tile(np.eye(E, dtype=np.float32), (ex, 1)),
                np.kron(np.eye(ex), np.ones((E, E))).astype(np.float32),
                np.tile(np.eye(E, dtype=np.float32), (ez, 1)),
                np.kron(np.eye(ez), np.ones((E, E))).astype(np.float32),
                row_x.astype(np.float32),
                row_y,
                col_x,
                col_y,
                one_hot(np.repeat(inside_positions(ex), ny), n_x),
                one_hot(np.tile(inside_positions(ey), nx), n_y),
                np.ascontiguousarray(one_hot(extended_positions(ez), nz + 8).T),
                np.ascontiguousarray(one_hot(inside_positions(ez), n_z).T),
            ),
        ),
    )

    cheb = cheb_matrix()
    kx = np.kron(np.kron(np.eye(ex, dtype=np.float32), cheb), np.eye(ny, dtype=np.float32))
    ky = np.kron(np.eye(nx, dtype=np.float32), np.kron(np.eye(ey, dtype=np.float32), cheb))
    kxy = jnp.asarray(np.concatenate([kx, ky]))
    kz = jnp.asarray(np.kron(np.eye(ez, dtype=np.float32), cheb))
    (image_direction,) = call(
        operator_kernel, "operator_direction", [direction.shape],
        direction, conductance, mass_term, kxy, kz,
    )

    every, to_high, to_low = call(
        depth_faces_kernel, "depth_faces", [(n_every, nz), (1, n_every), (1, n_every)],
        residual, x_low, x_high, y_low, y_high,
    )
    z_low, z_high = exchange(to_high, to_low, "gz")
    (owned,) = call(sum_spread_kernel, "sum_plane", [(n_line, own, block)], parts)
    parts = spread(owned, "gx")
    local_part, inner_local = pl.pallas_call(
        solve_kernel,
        out_shape=[jax.ShapeDtypeStruct((rows, nz), F32), jax.ShapeDtypeStruct((1, 1), F32)],
        in_specs=[pl.BlockSpec(memory_space=pltpu.VMEM)] * 8,
        out_specs=[pl.BlockSpec(memory_space=pltpu.VMEM)] * 2,
        scratch_shapes=[pltpu.VMEM((n_x, high_y, n_z), F32)],
        cost_estimate=pl.CostEstimate(flops=10**8, bytes_accessed=3 * 10**6, transcendentals=0),
        compiler_params=pltpu.CompilerParams(vmem_limit_bytes=16 * 2**20),
        name="element_solve",
    )(every, z_low, z_high, to_spectral, from_spectral, to_z, from_z, inverse_eigen_sums)
    (owned,) = call(sum_spread_kernel, "sum_line", [(n_plane, own, block)], parts)
    coarse_inner = spread(owned, plane).reshape(n_blocks, block)

    z, image, to_high, to_low, terms, square = call(
        correct_kernel, "coarse_correct",
        [direction.shape, direction.shape, (2, ny, nz), (2, ny, nz), (n_plane, 1, nz), (1, 1)],
        xxt_blocks, coarse_inner, xxt_values, ids_wide, local_part, inner_local, direction,
        image_direction, conductance, mass_term, kxy, kz, smem=(0,),
    )
    low, high = exchange(to_high, to_low, "gx")
    parts = spread(terms, plane)
    images, to_high, to_low = call(
        assemble_length_kernel, "assemble_length", [(2, nx, ny, nz), (2, nx, nz), (2, nx, nz)],
        image, image_direction, low, high,
    )
    low, high = exchange(to_high, to_low, "gy")
    (terms,) = call(sum_spread_kernel, "sum_terms", [(n_line, 1, nz)], parts)
    parts = spread(terms, "gx")
    images, to_high, to_low = call(
        assemble_across_kernel, "assemble_across", [(2, nx, ny, nz), (1, 2 * rows), (1, 2 * rows)],
        images, low, high,
    )
    low, high = exchange(to_high, to_low, "gz")
    return tuple(
        call(
            update_kernel, "update", [direction.shape] * 3,
            prior_inner, parts, square, images, low, high, residual, solution, direction, z,
            smem=(0,),
        )
    )


def solution(mesh):
    whole = P("gx", "gy", "gz")
    in_specs = (
        whole,
        whole,
        whole,
        P(None, "gx", "gy", "gz"),
        whole,
        P(),
        whole,
        whole,
        P(("gx", "gy", "gz"), None, None),
        P(("gx", "gy", "gz")),
        P(),
    )
    return jax.shard_map(
        body, mesh=mesh, in_specs=in_specs, out_specs=(whole, whole, whole), check_vma=False
    )
```

```python
import jax
import jax.numpy as jnp
import numpy as np
from jax import lax
from jax.experimental import pallas as pl
from jax.experimental.pallas import tpu as pltpu
from jax.sharding import PartitionSpec as P

HIGH = lax.Precision.HIGHEST
N = 8
E = 10
F32 = jnp.float32


def cheb_matrix():
    count = 8
    points = np.cos(np.pi * np.arange(count) / (count - 1))
    signs = np.array([2.0, 1, 1, 1, 1, 1, 1, 2.0]) * (-1.0) ** np.arange(count)
    differ = points[:, None] - points[None, :] + np.eye(count)
    matrix = np.outer(signs, 1.0 / signs) / differ
    matrix = matrix - np.eye(count) * np.sum(matrix, axis=1)[:, None]
    return (0.25 * matrix).astype(np.float32)


def extended_positions(count):
    length = N * count
    result = []
    for element in range(count):
        for node in [N * element - 2, *range(N * element, N * element + N), N * element + N + 1]:
            result.append(length if node < 0 else length + 1 if node >= length else node)
    return np.array(result)


def inside_positions(count):
    return np.concatenate([np.arange(E * e + 1, E * e + N + 1) for e in range(count)])


def one_hot(index, size):
    return (np.asarray(index)[:, None] == np.arange(size)[None, :]).astype(np.float32)


def up8(count):
    return -(-count // 8) * 8


def mm(a, b, ca=1, cb=0):
    return lax.dot_general(
        a, b, (((ca,), (cb,)), ((), ())), precision=HIGH, preferred_element_type=F32
    )


def call(kernel, name, outs, *args, smem=(), flops=0):
    specs = [
        pl.BlockSpec(memory_space=pltpu.SMEM if i in smem else pltpu.VMEM)
        for i in range(len(args))
    ]
    moved = sum(int(np.prod(a.shape)) * 4 for a in args)
    moved += sum(int(np.prod(s)) * 4 for s in outs)
    return pl.pallas_call(
        kernel,
        out_shape=[jax.ShapeDtypeStruct(s, F32) for s in outs],
        in_specs=specs,
        out_specs=[pl.BlockSpec(memory_space=pltpu.VMEM)] * len(outs),
        cost_estimate=pl.CostEstimate(flops=flops, bytes_accessed=moved, transcendentals=0),
        compiler_params=pltpu.CompilerParams(vmem_limit_bytes=16 * 2**20),
        name=name,
    )(*args)


def coarse_kernel(
    blocks, residual_hbm, ids_hbm, values_hbm, out, ids_wide, to_high, to_low, residual, ids, values, sems
):
    copies = [
        pltpu.make_async_copy(source, target, sems.at[i])
        for i, (source, target) in enumerate(
            ((residual_hbm, residual), (ids_hbm, ids), (values_hbm, values))
        )
    ]
    for copy in copies:
        copy.start()
    out[...] = jnp.zeros_like(out)
    nx, ny, nz = residual.shape
    ex, ey = nx // N, ny // N
    ez = ids.shape[1]
    n_stored, coarse, _ = values.shape
    widen = (
        lax.broadcasted_iota(jnp.int32, (ez, nz), 1) // N
        == lax.broadcasted_iota(jnp.int32, (ez, nz), 0)
    ).astype(F32)
    copies[1].wait()
    wide = mm(ids[...].astype(F32), widen)
    ids_wide[...] = wide
    unknown = lax.broadcasted_iota(jnp.int32, (coarse, nz), 0).astype(F32)
    total = jnp.zeros((coarse, nz), F32)
    copies[0].wait()
    to_high[...] = residual[nx - 2]
    to_low[...] = residual[1]
    for a in range(ex):
        for b in range(ey):
            part = jnp.sum(residual[a * N : a * N + N, b * N : b * N + N, :], axis=(0, 1))[None]
            q = a * ey + b
            total = total + jnp.where(jnp.abs(unknown - wide[q : q + 1]) < 0.5, part, 0.0)
    coarse_residual = jnp.sum(total, axis=1, keepdims=True)
    copies[2].wait()
    for k in range(n_stored):
        row = jnp.sum(values[k] * coarse_residual, axis=0, keepdims=True)
        at = pl.ds(blocks[k], 1)
        out[at, :] = out[at, :] + row


def sum_spread_kernel(parts, after, out):
    total = jnp.sum(parts[...], axis=0)
    for i in range(out.shape[0]):
        out[i] = total


def across_faces_kernel(residual, low, high, after, to_high, to_low):
    nx, ny, nz = residual.shape
    for out, y in ((to_high, ny - 2), (to_low, 1)):
        out[...] = jnp.zeros_like(out)
        out[:nx] = residual[:, y, :]
        out[nx : nx + 1] = low[y : y + 1]
        out[nx + 1 : nx + 2] = high[y : y + 1]


def depth_faces_kernel(
    residual, x_low, x_high, y_low, y_high, after, every, to_high, to_low
):
    nx, ny, nz = residual.shape
    at = 0
    for ref, count in ((None, nx * ny), (x_low, ny), (x_high, ny), (y_low, None), (y_high, None)):
        block = residual[...].reshape(nx * ny, nz) if ref is None else ref[...]
        every[at : at + block.shape[0]] = block
        at += block.shape[0]
    row = lax.broadcasted_iota(jnp.int32, (8, nz), 0)
    lane = lax.broadcasted_iota(jnp.int32, (8, nz), 1)
    pick = ((row == 0) & (lane == nz - 2)) | ((row == 1) & (lane == 1))
    ends = mm(pick.astype(F32), every[...], 1, 1)
    to_high[...] = ends[0:1]
    to_low[...] = ends[1:2]


def matrices_kernel(
    basis, tile2, mask2, tilez, maskz, row_x, row_y, col_x, col_y, out_x, out_y, col_z, in_z,
    to_spectral, from_spectral, to_z, from_z,
):
    flat2 = mm(mm(tile2[...], basis[...]), tile2[...], 1, 1) * mask2[...]
    flatz = mm(mm(tilez[...], basis[...]), tilez[...], 1, 1) * maskz[...]
    to_x = mm(row_x[...], mm(flat2, col_x[...], 0, 0))
    to_y = mm(row_y[...], mm(flat2, col_y[...], 0, 0))
    to_spectral[...] = to_x * to_y
    from_x = mm(mm(out_x[...], flat2), row_x[...], 1, 1)
    from_y = mm(mm(out_y[...], flat2), row_y[...], 1, 1)
    from_spectral[...] = from_x * from_y
    to_z[...] = mm(col_z[...], flatz)
    from_z[...] = mm(flatz, in_z[...], 0, 0)


def solve_kernel(
    every, z_low, z_high, to_spectral, from_spectral, to_z, from_z, sums, local_part, inner, wide
):
    nz = every.shape[1]
    n_x, n_y, n_z = sums.shape
    wide[...] = jnp.zeros_like(wide)
    wide[:, :n_y, :] = sums[...]
    weights = wide[...].reshape(-1, n_z)
    row = lax.broadcasted_iota(jnp.int32, (8, every.shape[0]), 0)
    ends = jnp.where(row == 0, z_low[...], jnp.where(row == 1, z_high[...], 0.0))
    spectral = mm(mm(to_spectral[...], every[...]), to_z[:nz, :])
    spectral = spectral + mm(mm(to_spectral[...], ends, 1, 1), to_z[nz:, :])
    weighted = weights * spectral
    inner[...] = jnp.sum(jnp.sum(weighted * spectral, axis=0, keepdims=True), axis=1, keepdims=True)
    local_part[...] = mm(mm(from_spectral[...], weighted), from_z[...])


def derive(matrix, slabs):
    result = []
    for first in range(0, len(slabs), N):
        for i in range(N):
            terms = [float(matrix[i, j]) * slabs[first + j] for j in range(N)]
            while len(terms) > 1:
                terms = [a + b for a, b in zip(terms[::2], terms[1::2])]
            result.append(terms[0])
    return result


def operator(source, conductance, mass, ky, ky_t, kz, kz_t, target):
    nx, ny, nz = source.shape
    rows = nx * ny
    cheb = cheb_matrix()
    flat = source[...].reshape(rows, nz)
    along_y = mm(ky[...], flat) * conductance[1].reshape(rows, nz)
    along_z = mm(flat, kz_t[...]) * conductance[2].reshape(rows, nz)
    along_x = [g * conductance[0, x] for x, g in enumerate(derive(cheb, [source[x] for x in range(nx)]))]
    yz = mm(ky_t[...], along_y) + mm(along_z, kz[...])
    for x, value in enumerate(derive(cheb.T, along_x)):
        target[x] = mass[x] * source[x] + value + yz[x * ny : (x + 1) * ny]


def operator_kernel(direction, conductance, mass, ky, ky_t, kz, kz_t, image):
    operator(direction, conductance, mass, ky, ky_t, kz, kz_t, image)


def total_of(values):
    return jnp.sum(jnp.sum(values, axis=0, keepdims=True), axis=1, keepdims=True)


def correct_kernel(
    blocks, coarse_inner, values, ids_wide, local_part, inner_local, direction, image_direction,
    conductance, mass, ky, ky_t, kz, kz_t,
    z_out, image_out, to_high, to_low, terms, square,
):
    nx, ny, nz = direction.shape
    rows = nx * ny
    n_stored, coarse, block = values.shape
    total = jnp.zeros((coarse, block), F32)
    for k in range(n_stored):
        total = total + values[k] * coarse_inner[pl.ds(blocks[k], 1), :]
    solution = jnp.sum(total, axis=1, keepdims=True)
    unknown = lax.broadcasted_iota(jnp.int32, (coarse, nz), 0).astype(F32)
    ey = ny // N
    for a in range(nx // N):
        for b in range(ey):
            q = a * ey + b
            hit = jnp.abs(unknown - ids_wide[q : q + 1, :]) < 0.5
            line = jnp.sum(jnp.where(hit, solution, 0.0), axis=0, keepdims=True)
            for x in range(N):
                at = (a * N + x) * ny + b * N
                z_out[a * N + x, b * N : b * N + N, :] = local_part[at : at + N, :] + line
    operator(z_out, conductance, mass, ky, ky_t, kz, kz_t, image_out)
    flat = z_out[...].reshape(rows, nz)
    image = image_out[...].reshape(rows, nz)
    to_high[0] = image_out[nx - 1]
    to_high[1] = image_direction[nx - 1]
    to_low[0] = image_out[0]
    to_low[1] = image_direction[0]
    old = direction[...].reshape(rows, nz)
    old_image = image_direction[...].reshape(rows, nz)
    first = total_of(flat * image)
    second = total_of(flat * old_image + old * image)
    third = total_of(old * old_image)
    lane = lax.broadcasted_iota(jnp.int32, (1, nz), 1)
    line = jnp.where(
        lane == 0,
        inner_local[...],
        jnp.where(lane == 1, first, jnp.where(lane == 2, second, jnp.where(lane == 3, third, 0.0))),
    )
    for i in range(terms.shape[0]):
        terms[i] = line
    square[...] = total_of(coarse_inner[...] * coarse_inner[...])


def assemble_length_kernel(image, image_direction, low, high, out, to_high, to_low):
    nx, ny, nz = image.shape
    for i, ref in ((0, image), (1, image_direction)):
        out[i] = ref[...]
        for x in range(nx):
            if x % N == N - 1:
                out[i, x] = ref[x] + (ref[x + 1] if x + 1 < nx else high[i])
            elif x % N == 0:
                out[i, x] = ref[x] + (ref[x - 1] if x else low[i])
        to_high[i] = out[i, :, ny - 1, :]
        to_low[i] = out[i, :, 0, :]


def assemble_across_kernel(images, low, high, out, to_high, to_low):
    _, nx, ny, nz = images.shape
    out[...] = images[...]
    for i in range(2):
        for y in range(ny):
            if y % N == N - 1:
                other = images[i, :, y + 1, :] if y + 1 < ny else high[i]
            elif y % N == 0:
                other = images[i, :, y - 1, :] if y else low[i]
            else:
                continue
            out[i, :, y, :] = images[i, :, y, :] + other
    row = lax.broadcasted_iota(jnp.int32, (8, nz), 0)
    lane = lax.broadcasted_iota(jnp.int32, (8, nz), 1)
    pick = ((row == 0) & (lane == nz - 1)) | ((row == 1) & (lane == 0))
    ends = mm(pick.astype(F32), out[...].reshape(2 * nx * ny, nz), 1, 1)
    to_high[...] = ends[0:1]
    to_low[...] = ends[1:2]


def update_kernel(
    prior, terms, square, images, low, high, residual, solution, direction, z,
    new_solution, new_residual, new_direction,
):
    nx, ny, nz = residual.shape
    rows = nx * ny
    lane1 = lax.broadcasted_iota(jnp.int32, (1, nz), 1)
    sums = jnp.sum(terms[...], axis=0)

    def term(i):
        return jnp.sum(jnp.where(lane1 == i, sums, 0.0), axis=1, keepdims=True)

    inner = term(0) + square[...]
    ratio = inner / prior[0]
    alpha = inner / (term(1) + ratio * term(2) + ratio * ratio * term(3))
    new = z[...].reshape(rows, nz) + ratio * direction[...].reshape(rows, nz)
    new_direction[...] = new.reshape(nx, ny, nz)
    new_solution[...] = (solution[...].reshape(rows, nz) + alpha * new).reshape(nx, ny, nz)
    image = images[0].reshape(rows, nz) + ratio * images[1].reshape(rows, nz)
    row = lax.broadcasted_iota(jnp.int32, (8, rows), 0)
    low_line = low[:, :rows] + ratio * low[:, rows:]
    high_line = high[:, :rows] + ratio * high[:, rows:]
    ends = jnp.where(row == 0, low_line, jnp.where(row == 1, high_line, 0.0))
    row = lax.broadcasted_iota(jnp.int32, (8, nz), 0)
    lane = lax.broadcasted_iota(jnp.int32, (8, nz), 1)
    place = ((row == 0) & (lane == 0)) | ((row == 1) & (lane == nz - 1))
    outer = mm(jnp.transpose(ends), place.astype(F32))
    lane = lax.broadcasted_iota(jnp.int32, (rows, nz), 1)
    above = pltpu.roll(image, nz - 1, 1)
    below = pltpu.roll(image, 1, 1)
    above = jnp.where((lane % N == N - 1) & (lane < nz - 1), above, 0.0)
    below = jnp.where((lane % N == 0) & (lane > 0), below, 0.0)
    image = image + above + below + outer
    new_residual[...] = (residual[...].reshape(rows, nz) - alpha * image).reshape(nx, ny, nz)


def shifts(axis):
    count = lax.axis_size(axis)
    forward = [(i, i + 1) for i in range(count - 1)]
    return forward, [(b, a) for a, b in forward]


def exchange(to_high, to_low, axis):
    forward, backward = shifts(axis)
    return lax.ppermute(to_high, axis, forward), lax.ppermute(to_low, axis, backward)


def spread(values, axes):
    return lax.all_to_all(values, axes, 0, 0, tiled=False)


def body(
    residual,
    solution,
    direction,
    conductance,
    mass_term,
    eigen_basis,
    inverse_eigen_sums,
    element_coarse_index,
    xxt_values,
    xxt_blocks,
    prior_inner,
):
    nx, ny, nz = residual.shape
    ex, ey, ez = nx // N, ny // N, nz // N
    rows = nx * ny
    plane = ("gy", "gz")
    n_plane, n_line = lax.axis_size(plane), lax.axis_size("gx")
    coarse_count, block = xxt_values.shape[1:]
    n_blocks = coarse_count * n_plane * n_line // block
    own = n_blocks // n_plane

    ids = element_coarse_index.reshape(ex * ey, ez)
    vmem, hbm = pl.BlockSpec(memory_space=pltpu.VMEM), pl.BlockSpec(memory_space=pl.ANY)
    partial_inner, ids_wide, to_high, to_low = pl.pallas_call(
        coarse_kernel,
        out_shape=[
            jax.ShapeDtypeStruct(shape, F32)
            for shape in ((n_blocks, block), (ex * ey, nz), (ny, nz), (ny, nz))
        ],
        in_specs=[pl.BlockSpec(memory_space=pltpu.SMEM), hbm, hbm, hbm],
        out_specs=[vmem] * 4,
        scratch_shapes=[
            pltpu.VMEM(residual.shape, F32),
            pltpu.VMEM(ids.shape, jnp.int32),
            pltpu.VMEM(xxt_values.shape, F32),
            pltpu.SemaphoreType.DMA((3,)),
        ],
        cost_estimate=pl.CostEstimate(flops=10**6, bytes_accessed=10**6, transcendentals=0),
        compiler_params=pltpu.CompilerParams(vmem_limit_bytes=16 * 2**20),
        name="coarse_restrict",
    )(xxt_blocks, residual, ids, xxt_values)
    parts = spread(partial_inner.reshape(n_plane, own, block), plane)
    x_low, x_high = exchange(to_high, to_low, "gx")
    cheb = cheb_matrix()
    ky = np.kron(np.eye(nx, dtype=np.float32), np.kron(np.eye(ey, dtype=np.float32), cheb))
    kz = np.kron(np.eye(ez, dtype=np.float32), cheb)
    tables = [jnp.asarray(np.ascontiguousarray(t)) for t in (ky, ky.T, kz, kz.T)]
    (image_direction,) = call(
        operator_kernel, "operator_direction", [direction.shape],
        direction, conductance, mass_term, *tables,
    )

    to_high, to_low = call(
        across_faces_kernel, "across_faces", [(up8(nx + 2), nz)] * 2, residual, x_low, x_high,
        image_direction,
    )
    y_low, y_high = exchange(to_high, to_low, "gy")

    face = up8(nx + 2)
    n_every = rows + 2 * ny + 2 * face
    pad = [-1] * (face - nx - 2)
    line = [*range(nx), nx, nx + 1, *pad]
    cols_x = np.array([*np.repeat(np.arange(nx), ny), *[nx] * ny, *[nx + 1] * ny, *line, *line])
    cols_y = np.array(
        [*np.tile(np.arange(ny), nx), *range(ny), *range(ny), *[ny] * face, *[ny + 1] * face]
    )
    n_x, n_y, n_z = inverse_eigen_sums.shape
    high_y = up8(n_y)
    place_y = np.tile(np.arange(high_y), n_x)
    row_x = one_hot(np.repeat(np.arange(n_x), high_y), n_x) * (place_y < n_y)[:, None]
    row_y = one_hot(place_y, n_y)
    col_x = (extended_positions(ex)[:, None] == cols_x[None, :]).astype(np.float32)
    col_y = (extended_positions(ey)[:, None] == cols_y[None, :]).astype(np.float32)
    assert ex == ey
    to_spectral, from_spectral, to_z, from_z = call(
        matrices_kernel, "basis_matrices",
        [(n_x * high_y, n_every), (rows, n_x * high_y), (nz + 8, n_z), (n_z, nz)],
        eigen_basis,
        *map(
            jnp.asarray,
            (
                np.tile(np.eye(E, dtype=np.float32), (ex, 1)),
                np.kron(np.eye(ex), np.ones((E, E))).astype(np.float32),
                np.tile(np.eye(E, dtype=np.float32), (ez, 1)),
                np.kron(np.eye(ez), np.ones((E, E))).astype(np.float32),
                row_x.astype(np.float32),
                row_y,
                col_x,
                col_y,
                one_hot(np.repeat(inside_positions(ex), ny), n_x),
                one_hot(np.tile(inside_positions(ey), nx), n_y),
                np.ascontiguousarray(one_hot(extended_positions(ez), nz + 8).T),
                np.ascontiguousarray(one_hot(inside_positions(ez), n_z).T),
            ),
        ),
    )

    (owned,) = call(sum_spread_kernel, "sum_plane", [(n_line, own, block)], parts, to_high)
    parts = spread(owned, "gx")
    every, to_high, to_low = call(
        depth_faces_kernel, "depth_faces", [(n_every, nz), (1, n_every), (1, n_every)],
        residual, x_low, x_high, y_low, y_high, from_z,
    )
    (owned,) = call(sum_spread_kernel, "sum_line", [(n_plane, own, block)], parts, to_high)
    coarse_inner = spread(owned, plane).reshape(n_blocks, block)
    z_low, z_high = exchange(to_high, to_low, "gz")
    local_part, inner_local = pl.pallas_call(
        solve_kernel,
        out_shape=[jax.ShapeDtypeStruct((rows, nz), F32), jax.ShapeDtypeStruct((1, 1), F32)],
        in_specs=[pl.BlockSpec(memory_space=pltpu.VMEM)] * 8,
        out_specs=[pl.BlockSpec(memory_space=pltpu.VMEM)] * 2,
        scratch_shapes=[pltpu.VMEM((n_x, high_y, n_z), F32)],
        cost_estimate=pl.CostEstimate(flops=10**8, bytes_accessed=3 * 10**6, transcendentals=0),
        compiler_params=pltpu.CompilerParams(vmem_limit_bytes=16 * 2**20),
        name="element_solve",
    )(every, z_low, z_high, to_spectral, from_spectral, to_z, from_z, inverse_eigen_sums)
    z, image, to_high, to_low, terms, square = call(
        correct_kernel, "coarse_correct",
        [direction.shape, direction.shape, (2, ny, nz), (2, ny, nz), (n_plane, 1, nz), (1, 1)],
        xxt_blocks, coarse_inner, xxt_values, ids_wide, local_part, inner_local, direction,
        image_direction, conductance, mass_term, *tables, smem=(0,),
    )
    low, high = exchange(to_high, to_low, "gx")
    parts = spread(terms, plane)
    images, to_high, to_low = call(
        assemble_length_kernel, "assemble_length", [(2, nx, ny, nz), (2, nx, nz), (2, nx, nz)],
        image, image_direction, low, high,
    )
    across = to_high, to_low
    (terms,) = call(sum_spread_kernel, "sum_terms", [(n_line, 1, nz)], parts, to_high)
    parts = spread(terms, "gx")
    low, high = exchange(*across, "gy")
    images, to_high, to_low = call(
        assemble_across_kernel, "assemble_across", [(2, nx, ny, nz), (1, 2 * rows), (1, 2 * rows)],
        images, low, high,
    )
    low, high = exchange(to_high, to_low, "gz")
    return tuple(
        call(
            update_kernel, "update", [direction.shape] * 3,
            prior_inner, parts, square, images, low, high, residual, solution, direction, z,
            smem=(0,),
        )
    )


def solution(mesh):
    whole = P("gx", "gy", "gz")
    in_specs = (
        whole,
        whole,
        whole,
        P(None, "gx", "gy", "gz"),
        whole,
        P(),
        whole,
        whole,
        P(("gx", "gy", "gz"), None, None),
        P(("gx", "gy", "gz")),
        P(),
    )
    return jax.shard_map(
        body, mesh=mesh, in_specs=in_specs, out_specs=(whole, whole, whole), check_vma=False
    )
```

```python
import jax
import jax.numpy as jnp
import numpy as np
from jax import lax
from jax.experimental import pallas as pl
from jax.experimental.pallas import tpu as pltpu
from jax.sharding import PartitionSpec as P

HIGH = lax.Precision.HIGHEST
N = 8
E = 10
F32 = jnp.float32


def cheb_matrix():
    count = 8
    points = np.cos(np.pi * np.arange(count) / (count - 1))
    signs = np.array([2.0, 1, 1, 1, 1, 1, 1, 2.0]) * (-1.0) ** np.arange(count)
    differ = points[:, None] - points[None, :] + np.eye(count)
    matrix = np.outer(signs, 1.0 / signs) / differ
    matrix = matrix - np.eye(count) * np.sum(matrix, axis=1)[:, None]
    return (0.25 * matrix).astype(np.float32)


def extended_positions(count):
    length = N * count
    result = []
    for element in range(count):
        for node in [N * element - 2, *range(N * element, N * element + N), N * element + N + 1]:
            result.append(length if node < 0 else length + 1 if node >= length else node)
    return np.array(result)


def inside_positions(count):
    return np.concatenate([np.arange(E * e + 1, E * e + N + 1) for e in range(count)])


def one_hot(index, size):
    return (np.asarray(index)[:, None] == np.arange(size)[None, :]).astype(np.float32)


def up8(count):
    return -(-count // 8) * 8


def mm(a, b, ca=1, cb=0):
    return lax.dot_general(
        a, b, (((ca,), (cb,)), ((), ())), precision=HIGH, preferred_element_type=F32
    )


def call(kernel, name, outs, *args, smem=(), load=(), keep=(), scratch=(), pin=()):
    count, n_out, n_keep = len(args), len(outs), len(keep)
    moved = sorted((*load, *keep))
    vmem = pl.BlockSpec(memory_space=pltpu.VMEM)

    def whole(*refs):
        inside, results = list(refs[:count]), refs[count : count + n_out]
        kept = refs[count + n_out : count + n_out + n_keep]
        rest = list(refs[count + n_out + n_keep :])
        sems = rest.pop() if moved else None
        copies = {}
        for at, i in enumerate(moved):
            target = kept[keep.index(i)] if i in keep else rest.pop()
            copies[i] = pltpu.make_async_copy(inside[i], target, sems.at[at])
            copies[i].start()
            inside[i] = target
        waiting = dict(copies)

        def ready(*which):
            for i in which:
                if i in waiting:
                    waiting.pop(i).wait()

        kernel(ready, *inside, *results, *rest)
        ready(*moved)

    buffers = [pltpu.VMEM(args[i].shape, args[i].dtype) for i in moved if i not in keep]
    specs = []
    for i in range(count):
        space = pltpu.SMEM if i in smem else pltpu.HBM if i in moved else pltpu.VMEM
        specs.append(pl.BlockSpec(memory_space=space))
    args = [
        pltpu.with_memory_space_constraint(a, pltpu.HBM) if i in moved else a
        for i, a in enumerate(args)
    ]
    size = sum(int(np.prod(a.shape)) * 4 for a in args) + sum(int(np.prod(o)) * 4 for o in outs)
    return pl.pallas_call(
        whole,
        out_shape=[
            pltpu.VMEM(o, F32) if i in pin else jax.ShapeDtypeStruct(o, F32)
            for i, o in enumerate(outs)
        ]
        + [pltpu.VMEM(args[i].shape, args[i].dtype) for i in keep],
        in_specs=specs,
        out_specs=[vmem] * (n_out + n_keep),
        scratch_shapes=[
            *scratch,
            *buffers[::-1],
            *([pltpu.SemaphoreType.DMA((len(moved),))] if moved else []),
        ],
        cost_estimate=pl.CostEstimate(flops=0, bytes_accessed=size, transcendentals=0),
        compiler_params=pltpu.CompilerParams(vmem_limit_bytes=24 * 2**20),
        name=name,
    )(*args)


def coarse_kernel(ready, blocks, me, residual, ids, values, payload, ids_wide):
    nx, ny, nz = residual.shape
    ex, ey = nx // N, ny // N
    ez = ids.shape[1]
    n_stored, coarse, _ = values.shape
    n_line, head = payload.shape[0], payload.shape[1] - ny
    widen = (
        lax.broadcasted_iota(jnp.int32, (ez, nz), 1) // N
        == lax.broadcasted_iota(jnp.int32, (ez, nz), 0)
    ).astype(F32)
    payload[...] = jnp.zeros_like(payload)
    at = me[0]
    lane = lax.broadcasted_iota(jnp.int32, (1, nz), 1)
    numbers = jnp.zeros((1, nz), F32)
    for k in range(n_stored):
        numbers = jnp.where(lane == n_stored * at + k, blocks[k].astype(F32), numbers)
    ready(3)
    wide = mm(ids[...].astype(F32), widen)
    ids_wide[...] = wide
    unknown = lax.broadcasted_iota(jnp.int32, (coarse, nz), 0).astype(F32)
    total = jnp.zeros((coarse, nz), F32)
    ready(2)

    @pl.when(at + 1 < n_line)
    def _():
        payload[at + 1, head:, :] = residual[nx - 2]

    @pl.when(at > 0)
    def _():
        payload[at - 1, head:, :] = residual[1]

    for a in range(ex):
        for b in range(ey):
            part = jnp.sum(residual[a * N : a * N + N, b * N : b * N + N, :], axis=(0, 1))[None]
            q = a * ey + b
            total = total + jnp.where(jnp.abs(unknown - wide[q : q + 1]) < 0.5, part, 0.0)
    coarse_residual = jnp.sum(total, axis=1, keepdims=True)
    ready(4)
    row = lax.broadcasted_iota(jnp.int32, (head, nz), 0)
    lines = jnp.where(row == n_stored, numbers, 0.0)
    for k in range(n_stored):
        lines = jnp.where(
            row == k, jnp.sum(values[k] * coarse_residual, axis=0, keepdims=True), lines
        )
    for i in range(n_line):
        payload[i, :head, :] = lines


def line_kernel(ready, me, parts, residual, after1, after2, dense, x_low, x_high, to_high, to_low):
    nx, ny, nz = residual.shape
    n_line = parts.shape[0]
    head, n_stored = parts.shape[1] - ny, 8
    at = me[0]
    rows = parts[:, :n_stored, :].reshape(n_line * n_stored, nz)
    rows = jnp.concatenate([rows] + [jnp.zeros((nz - n_line * n_stored, nz), F32)]) if n_line * n_stored < nz else rows
    numbers = jnp.sum(parts[:, n_stored : n_stored + 1, :], axis=0)
    n_blocks = dense.shape[0] * dense.shape[1]
    block = lax.broadcasted_iota(jnp.int32, (n_blocks, nz), 0).astype(F32)
    place = (jnp.abs(block - numbers) < 0.5).astype(F32)
    dense[...] = mm(place, rows).reshape(dense.shape)
    before, behind = jnp.maximum(at - 1, 0), jnp.minimum(at + 1, n_line - 1)
    x_low[...] = jnp.where(at > 0, parts[before, head:, :], 0.0)
    x_high[...] = jnp.where(at + 1 < n_line, parts[behind, head:, :], 0.0)
    for out, y in ((to_high, ny - 2), (to_low, 1)):
        out[...] = jnp.zeros_like(out)
        out[:nx] = residual[:, y, :]
        out[nx : nx + 1] = x_low[y : y + 1]
        out[nx + 1 : nx + 2] = x_high[y : y + 1]


def plane_kernel(
    ready, parts, residual, x_low, x_high, y_low, y_high, owned, every, to_high, to_low
):
    total = jnp.sum(parts[...], axis=0)
    for i in range(owned.shape[0]):
        owned[i] = total
    nx, ny, nz = residual.shape
    at = 0
    for ref in (None, x_low, x_high, y_low, y_high):
        block = residual[...].reshape(nx * ny, nz) if ref is None else ref[...]
        every[at : at + block.shape[0]] = block
        at += block.shape[0]
    row = lax.broadcasted_iota(jnp.int32, (8, nz), 0)
    lane = lax.broadcasted_iota(jnp.int32, (8, nz), 1)
    pick = ((row == 0) & (lane == nz - 2)) | ((row == 1) & (lane == 1))
    ends = mm(pick.astype(F32), every[...], 1, 1)
    to_high[...] = ends[0:1]
    to_low[...] = ends[1:2]


def matrices_kernel(
    ready, basis, tile2, mask2, tilez, maskz, row_x, row_y, col_x, col_y, out_x, out_y, col_z, in_z,
    to_spectral, from_spectral, to_z, from_z,
):
    ready(*range(13))
    flat2 = mm(mm(tile2[...], basis[...]), tile2[...], 1, 1) * mask2[...]
    flatz = mm(mm(tilez[...], basis[...]), tilez[...], 1, 1) * maskz[...]
    to_x = mm(row_x[...], mm(flat2, col_x[...], 0, 0))
    to_y = mm(row_y[...], mm(flat2, col_y[...], 0, 0))
    to_spectral[...] = to_x * to_y
    from_x = mm(mm(out_x[...], flat2), row_x[...], 1, 1)
    from_y = mm(mm(out_y[...], flat2), row_y[...], 1, 1)
    from_spectral[...] = from_x * from_y
    to_z[...] = mm(col_z[...], flatz)
    from_z[...] = mm(flatz, in_z[...], 0, 0)


def solve_kernel(
    ready, every, z_low, z_high, to_spectral, from_spectral, to_z, from_z, sums, local_part, inner, wide
):
    nz = every.shape[1]
    n_x, n_y, n_z = sums.shape
    wide[...] = jnp.zeros_like(wide)
    row = lax.broadcasted_iota(jnp.int32, (8, every.shape[0]), 0)
    ends = jnp.where(row == 0, z_low[...], jnp.where(row == 1, z_high[...], 0.0))
    ready(3, 4, 5, 6)
    spectral = mm(mm(to_spectral[...], every[...]), to_z[:nz, :])
    spectral = spectral + mm(mm(to_spectral[...], ends, 1, 1), to_z[nz:, :])
    ready(7)
    wide[:, :n_y, :] = sums[...]
    weighted = wide[...].reshape(-1, n_z) * spectral
    inner[...] = jnp.sum(jnp.sum(weighted * spectral, axis=0, keepdims=True), axis=1, keepdims=True)
    local_part[...] = mm(mm(from_spectral[...], weighted), from_z[...])


def derive(matrix, slabs):
    result = []
    for first in range(0, len(slabs), N):
        for i in range(N):
            terms = [float(matrix[i, j]) * slabs[first + j] for j in range(N)]
            while len(terms) > 1:
                terms = [a + b for a, b in zip(terms[::2], terms[1::2])]
            result.append(terms[0])
    return result


def operator(source, conductance, mass, ky, ky_t, kz, kz_t, target):
    nx, ny, nz = source.shape
    rows = nx * ny
    cheb = cheb_matrix()
    flat = source[...].reshape(rows, nz)
    along_y = mm(ky[...], flat) * conductance[1].reshape(rows, nz)
    along_z = mm(flat, kz_t[...]) * conductance[2].reshape(rows, nz)
    along_x = [g * conductance[0, x] for x, g in enumerate(derive(cheb, [source[x] for x in range(nx)]))]
    yz = mm(ky_t[...], along_y) + mm(along_z, kz[...])
    for x, value in enumerate(derive(cheb.T, along_x)):
        target[x] = mass[x] * source[x] + value + yz[x * ny : (x + 1) * ny]


def operator_kernel(ready, direction, conductance, mass, ky, ky_t, kz, kz_t, image):
    ready(0, 1, 2, 3, 4, 5, 6)
    operator(direction, conductance, mass, ky, ky_t, kz, kz_t, image)


def total_of(values):
    return jnp.sum(jnp.sum(values, axis=0, keepdims=True), axis=1, keepdims=True)


def correct_kernel(
    ready, blocks, coarse_inner, values, ids_wide, local_part, inner_local, direction, image_direction,
    conductance, mass, ky, ky_t, kz, kz_t,
    z_out, image_out, to_high, to_low, terms, square,
):
    nx, ny, nz = direction.shape
    rows = nx * ny
    n_stored, coarse, block = values.shape
    total = jnp.zeros((coarse, block), F32)
    for k in range(n_stored):
        total = total + values[k] * coarse_inner[pl.ds(blocks[k], 1), :]
    solution = jnp.sum(total, axis=1, keepdims=True)
    unknown = lax.broadcasted_iota(jnp.int32, (coarse, nz), 0).astype(F32)
    ey = ny // N
    for a in range(nx // N):
        for b in range(ey):
            q = a * ey + b
            hit = jnp.abs(unknown - ids_wide[q : q + 1, :]) < 0.5
            line = jnp.sum(jnp.where(hit, solution, 0.0), axis=0, keepdims=True)
            for x in range(N):
                at = (a * N + x) * ny + b * N
                z_out[a * N + x, b * N : b * N + N, :] = local_part[at : at + N, :] + line
    ready(10, 11)
    operator(z_out, conductance, mass, ky, ky_t, kz, kz_t, image_out)
    flat = z_out[...].reshape(rows, nz)
    image = image_out[...].reshape(rows, nz)
    to_high[0] = image_out[nx - 1]
    to_high[1] = image_direction[nx - 1]
    to_low[0] = image_out[0]
    to_low[1] = image_direction[0]
    old = direction[...].reshape(rows, nz)
    old_image = image_direction[...].reshape(rows, nz)
    first = total_of(flat * image)
    second = total_of(flat * old_image + old * image)
    third = total_of(old * old_image)
    lane = lax.broadcasted_iota(jnp.int32, (1, nz), 1)
    line = jnp.where(
        lane == 0,
        inner_local[...],
        jnp.where(lane == 1, first, jnp.where(lane == 2, second, jnp.where(lane == 3, third, 0.0))),
    )
    for i in range(terms.shape[0]):
        terms[i] = line
    square[...] = total_of(coarse_inner[...] * coarse_inner[...])


def assemble_length_kernel(
    ready, image, image_direction, low, high, parts, out, to_high, to_low, terms
):
    nx, ny, nz = image.shape
    total = jnp.sum(parts[...], axis=0)
    for i in range(terms.shape[0]):
        terms[i] = total
    for i, ref in ((0, image), (1, image_direction)):
        out[i] = ref[...]
        for x in range(nx):
            if x % N == N - 1:
                out[i, x] = ref[x] + (ref[x + 1] if x + 1 < nx else high[i])
            elif x % N == 0:
                out[i, x] = ref[x] + (ref[x - 1] if x else low[i])
        to_high[i] = out[i, :, ny - 1, :]
        to_low[i] = out[i, :, 0, :]


def assemble_across_kernel(ready, images, low, high, solution, out, to_high, to_low):
    _, nx, ny, nz = images.shape
    out[...] = images[...]
    for i in range(2):
        for y in range(ny):
            if y % N == N - 1:
                other = images[i, :, y + 1, :] if y + 1 < ny else high[i]
            elif y % N == 0:
                other = images[i, :, y - 1, :] if y else low[i]
            else:
                continue
            out[i, :, y, :] = images[i, :, y, :] + other
    row = lax.broadcasted_iota(jnp.int32, (8, nz), 0)
    lane = lax.broadcasted_iota(jnp.int32, (8, nz), 1)
    pick = ((row == 0) & (lane == nz - 1)) | ((row == 1) & (lane == 0))
    ends = mm(pick.astype(F32), out[...].reshape(2 * nx * ny, nz), 1, 1)
    to_high[...] = ends[0:1]
    to_low[...] = ends[1:2]


def update_kernel(
    ready, prior, terms, square, images, low, high, residual, solution, direction, z,
    new_solution, new_residual, new_direction,
):
    nx, ny, nz = residual.shape
    rows = nx * ny
    lane1 = lax.broadcasted_iota(jnp.int32, (1, nz), 1)
    sums = jnp.sum(terms[...], axis=0)

    def term(i):
        return jnp.sum(jnp.where(lane1 == i, sums, 0.0), axis=1, keepdims=True)

    inner = term(0) + square[...]
    ratio = inner / prior[0]
    alpha = inner / (term(1) + ratio * term(2) + ratio * ratio * term(3))
    new = z[...].reshape(rows, nz) + ratio * direction[...].reshape(rows, nz)
    new_direction[...] = new.reshape(nx, ny, nz)
    new_solution[...] = (solution[...].reshape(rows, nz) + alpha * new).reshape(nx, ny, nz)
    image = images[0].reshape(rows, nz) + ratio * images[1].reshape(rows, nz)
    row = lax.broadcasted_iota(jnp.int32, (8, rows), 0)
    low_line = low[:, :rows] + ratio * low[:, rows:]
    high_line = high[:, :rows] + ratio * high[:, rows:]
    ends = jnp.where(row == 0, low_line, jnp.where(row == 1, high_line, 0.0))
    row = lax.broadcasted_iota(jnp.int32, (8, nz), 0)
    lane = lax.broadcasted_iota(jnp.int32, (8, nz), 1)
    place = ((row == 0) & (lane == 0)) | ((row == 1) & (lane == nz - 1))
    outer = mm(jnp.transpose(ends), place.astype(F32))
    lane = lax.broadcasted_iota(jnp.int32, (rows, nz), 1)
    above = pltpu.roll(image, nz - 1, 1)
    below = pltpu.roll(image, 1, 1)
    above = jnp.where((lane % N == N - 1) & (lane < nz - 1), above, 0.0)
    below = jnp.where((lane % N == 0) & (lane > 0), below, 0.0)
    image = image + above + below + outer
    new_residual[...] = (residual[...].reshape(rows, nz) - alpha * image).reshape(nx, ny, nz)


def shifts(axis):
    count = lax.axis_size(axis)
    forward = [(i, i + 1) for i in range(count - 1)]
    return forward, [(b, a) for a, b in forward]


def exchange(to_high, to_low, axis):
    forward, backward = shifts(axis)
    return lax.ppermute(to_high, axis, forward), lax.ppermute(to_low, axis, backward)


def spread(values, axes):
    return lax.all_to_all(values, axes, 0, 0, tiled=False)


def body(
    residual,
    solution,
    direction,
    conductance,
    mass_term,
    eigen_basis,
    inverse_eigen_sums,
    element_coarse_index,
    xxt_values,
    xxt_blocks,
    prior_inner,
):
    nx, ny, nz = residual.shape
    ex, ey, ez = nx // N, ny // N, nz // N
    rows = nx * ny
    plane = ("gy", "gz")
    n_plane, n_line = lax.axis_size(plane), lax.axis_size("gx")
    coarse_count, block = xxt_values.shape[1:]
    n_blocks = coarse_count * n_plane * n_line // block
    own = n_blocks // n_plane

    ids = element_coarse_index.reshape(ex * ey, ez)
    me = lax.axis_index("gx").astype(jnp.int32).reshape(1)
    head = up8(xxt_values.shape[0] + 1)
    assert xxt_values.shape[0] * n_line <= nz
    payload, ids_wide, residual, xxt_values = call(
        coarse_kernel, "coarse_restrict", [(n_line, head + ny, nz), (ex * ey, nz)],
        xxt_blocks, me, residual, ids, xxt_values, smem=(0, 1), load=(3,), keep=(2, 4), pin=(1,),
    )
    parts = spread(payload, "gx")

    cheb = cheb_matrix()
    ky = np.kron(np.eye(nx, dtype=np.float32), np.kron(np.eye(ey, dtype=np.float32), cheb))
    kz = np.kron(np.eye(ez, dtype=np.float32), cheb)
    tables = [jnp.asarray(np.ascontiguousarray(t)) for t in (ky, ky.T, kz, kz.T)]
    image_direction, direction, conductance, mass_term, kz, kz_t = call(
        operator_kernel, "operator_direction", [direction.shape],
        direction, conductance, mass_term, *tables, load=(3, 4), keep=(0, 1, 2, 5, 6), pin=(0,),
    )

    face = up8(nx + 2)
    n_every = rows + 2 * ny + 2 * face
    pad = [-1] * (face - nx - 2)
    line = [*range(nx), nx, nx + 1, *pad]
    cols_x = np.array([*np.repeat(np.arange(nx), ny), *[nx] * ny, *[nx + 1] * ny, *line, *line])
    cols_y = np.array(
        [*np.tile(np.arange(ny), nx), *range(ny), *range(ny), *[ny] * face, *[ny + 1] * face]
    )
    n_x, n_y, n_z = inverse_eigen_sums.shape
    high_y = up8(n_y)
    place_y = np.tile(np.arange(high_y), n_x)
    row_x = one_hot(np.repeat(np.arange(n_x), high_y), n_x) * (place_y < n_y)[:, None]
    row_y = one_hot(place_y, n_y)
    col_x = (extended_positions(ex)[:, None] == cols_x[None, :]).astype(np.float32)
    col_y = (extended_positions(ey)[:, None] == cols_y[None, :]).astype(np.float32)
    assert ex == ey
    to_spectral, from_spectral, to_z, from_z = call(
        matrices_kernel, "basis_matrices",
        [(n_x * high_y, n_every), (rows, n_x * high_y), (nz + 8, n_z), (n_z, nz)],
        eigen_basis,
        *map(
            jnp.asarray,
            (
                np.tile(np.eye(E, dtype=np.float32), (ex, 1)),
                np.kron(np.eye(ex), np.ones((E, E))).astype(np.float32),
                np.tile(np.eye(E, dtype=np.float32), (ez, 1)),
                np.kron(np.eye(ez), np.ones((E, E))).astype(np.float32),
                row_x.astype(np.float32),
                row_y,
                col_x,
                col_y,
                one_hot(np.repeat(inside_positions(ex), ny), n_x),
                one_hot(np.tile(inside_positions(ey), nx), n_y),
                np.ascontiguousarray(one_hot(extended_positions(ez), nz + 8).T),
                np.ascontiguousarray(one_hot(inside_positions(ez), n_z).T),
            ),
        ),
        load=tuple(range(13)),
    )

    dense, x_low, x_high, to_high, to_low = call(
        line_kernel, "line_sum",
        [(n_plane, own, block), (ny, nz), (ny, nz), (face, nz), (face, nz)],
        me, parts, residual, image_direction, from_z, smem=(0,), pin=(1, 2),
    )
    parts = spread(dense, plane)
    y_low, y_high = exchange(to_high, to_low, "gy")
    owned, every, to_high, to_low = call(
        plane_kernel, "plane_sum",
        [(n_plane, own, block), (n_every, nz), (1, n_every), (1, n_every)],
        parts, residual, x_low, x_high, y_low, y_high, pin=(1,),
    )
    coarse_inner = spread(owned, plane).reshape(n_blocks, block)
    z_low, z_high = exchange(to_high, to_low, "gz")
    local_part, inner_local = call(
        solve_kernel, "element_solve", [(rows, nz), (1, 1)],
        every, z_low, z_high, to_spectral, from_spectral, to_z, from_z, inverse_eigen_sums,
        load=(3, 4, 5, 6, 7), pin=(0, 1), scratch=(pltpu.VMEM((n_x, high_y, n_z), F32),),
    )

    z, image, to_high, to_low, terms, square = call(
        correct_kernel, "coarse_correct",
        [direction.shape, direction.shape, (2, ny, nz), (2, ny, nz), (n_plane, 1, nz), (1, 1)],
        xxt_blocks, coarse_inner, xxt_values, ids_wide, local_part, inner_local, direction,
        image_direction, conductance, mass_term, *tables[:2], kz, kz_t, smem=(0,), load=(10, 11), pin=(0, 1, 5),
    )
    low, high = exchange(to_high, to_low, "gx")
    parts = spread(terms, plane)
    images, to_high, to_low, terms = call(
        assemble_length_kernel, "assemble_length",
        [(2, nx, ny, nz), (2, nx, nz), (2, nx, nz), (n_line, 1, nz)],
        image, image_direction, low, high, parts, pin=(0,),
    )
    parts = spread(terms, "gx")
    low, high = exchange(to_high, to_low, "gy")
    images, to_high, to_low, solution = call(
        assemble_across_kernel, "assemble_across", [(2, nx, ny, nz), (1, 2 * rows), (1, 2 * rows)],
        images, low, high, solution, keep=(3,), pin=(0,),
    )
    low, high = exchange(to_high, to_low, "gz")
    return tuple(
        call(
            update_kernel, "update", [direction.shape] * 3,
            prior_inner, parts, square, images, low, high, residual, solution, direction, z,
            smem=(0,),
        )
    )


def solution(mesh):
    whole = P("gx", "gy", "gz")
    in_specs = (
        whole,
        whole,
        whole,
        P(None, "gx", "gy", "gz"),
        whole,
        P(),
        whole,
        whole,
        P(("gx", "gy", "gz"), None, None),
        P(("gx", "gy", "gz")),
        P(),
    )
    return jax.shard_map(
        body, mesh=mesh, in_specs=in_specs, out_specs=(whole, whole, whole), check_vma=False
    )
```

```python
import functools

import jax
import jax.numpy as jnp
import numpy as np
from jax import lax
from jax.experimental import pallas as pl
from jax.experimental.pallas import tpu as pltpu
from jax.sharding import PartitionSpec as P

HIGH = lax.Precision.HIGHEST
N = 8
E = 10
F32 = jnp.float32


def cheb_matrix():
    count = 8
    points = np.cos(np.pi * np.arange(count) / (count - 1))
    signs = np.array([2.0, 1, 1, 1, 1, 1, 1, 2.0]) * (-1.0) ** np.arange(count)
    differ = points[:, None] - points[None, :] + np.eye(count)
    matrix = np.outer(signs, 1.0 / signs) / differ
    matrix = matrix - np.eye(count) * np.sum(matrix, axis=1)[:, None]
    return (0.25 * matrix).astype(np.float32)


def extended_positions(count):
    length = N * count
    result = []
    for element in range(count):
        for node in [N * element - 2, *range(N * element, N * element + N), N * element + N + 1]:
            result.append(length if node < 0 else length + 1 if node >= length else node)
    return np.array(result)


def inside_positions(count):
    return np.concatenate([np.arange(E * e + 1, E * e + N + 1) for e in range(count)])


def one_hot(index, size):
    return (np.asarray(index)[:, None] == np.arange(size)[None, :]).astype(np.float32)


def up8(count):
    return -(-count // 8) * 8


def mm(a, b, ca=1, cb=0):
    return lax.dot_general(
        a, b, (((ca,), (cb,)), ((), ())), precision=HIGH, preferred_element_type=F32
    )


def call(kernel, name, outs, *args, smem=(), load=(), keep=(), scratch=(), pin=(), store=(), idle=()):
    count, n_out, n_keep = len(args), len(outs), len(keep)
    moved = sorted((*load, *keep))
    vmem = pl.BlockSpec(memory_space=pltpu.VMEM)

    def whole(*refs):
        inside, results = list(refs[:count]), refs[count : count + n_out]
        kept = refs[count + n_out : count + n_out + n_keep]
        rest = list(refs[count + n_out + n_keep :])
        sems = rest.pop() if moved or store else None
        written = list(results)
        for i in store:
            written[i] = rest.pop()
        copies = {}
        for at, i in enumerate(moved):
            target = kept[keep.index(i)] if i in keep else rest.pop()
            copies[i] = pltpu.make_async_copy(inside[i], target, sems.at[at])
            copies[i].start()
            inside[i] = target
        waiting = dict(copies)

        def ready(*which):
            for i in which:
                if i in waiting:
                    waiting.pop(i).wait()

        kernel(ready, *inside, *written, *rest)
        ready(*moved)
        copies = [
            pltpu.make_async_copy(written[i], results[i], sems.at[len(moved) + at])
            for at, i in enumerate(store)
        ]
        for copy in copies:
            copy.start()
        for copy in copies:
            copy.wait()

    buffers = [pltpu.VMEM(args[i].shape, args[i].dtype) for i in moved if i not in keep]
    specs = []
    for i in range(count):
        space = pltpu.SMEM if i in smem else pltpu.HBM if i in (*moved, *idle) else pltpu.VMEM
        specs.append(pl.BlockSpec(memory_space=space))
    args = [
        pltpu.with_memory_space_constraint(a, pltpu.HBM) if i in (*moved, *idle) else a
        for i, a in enumerate(args)
    ]
    size = sum(int(np.prod(a.shape)) * 4 for a in args) + sum(int(np.prod(o)) * 4 for o in outs)
    return pl.pallas_call(
        whole,
        out_shape=[
            pltpu.VMEM(o, F32)
            if i in pin
            else pltpu.HBM(o, F32)
            if i in store
            else jax.ShapeDtypeStruct(o, F32)
            for i, o in enumerate(outs)
        ]
        + [pltpu.VMEM(args[i].shape, args[i].dtype) for i in keep],
        in_specs=specs,
        out_specs=[
            pl.BlockSpec(memory_space=pltpu.HBM) if i in store else vmem
            for i in range(n_out + n_keep)
        ],
        scratch_shapes=[
            *scratch,
            *buffers[::-1],
            *[pltpu.VMEM(outs[i], F32) for i in store[::-1]],
            *([pltpu.SemaphoreType.DMA((len(moved) + len(store),))] if moved or store else []),
        ],
        cost_estimate=pl.CostEstimate(flops=0, bytes_accessed=size, transcendentals=0),
        compiler_params=pltpu.CompilerParams(vmem_limit_bytes=24 * 2**20),
        name=name,
    )(*args)


def coarse_kernel(ready, blocks, me, residual, ids, values, payload, ids_wide):
    nx, ny, nz = residual.shape
    ex, ey = nx // N, ny // N
    ez = ids.shape[1]
    n_stored, coarse, _ = values.shape
    n_line, head = payload.shape[0], payload.shape[1] - ny
    widen = (
        lax.broadcasted_iota(jnp.int32, (ez, nz), 1) // N
        == lax.broadcasted_iota(jnp.int32, (ez, nz), 0)
    ).astype(F32)
    payload[...] = jnp.zeros_like(payload)
    at = me[0]
    lane = lax.broadcasted_iota(jnp.int32, (1, nz), 1)
    numbers = jnp.zeros((1, nz), F32)
    for k in range(n_stored):
        numbers = jnp.where(lane == n_stored * at + k, blocks[k].astype(F32), numbers)
    ready(3)
    wide = mm(ids[...].astype(F32), widen)
    ids_wide[...] = wide
    unknown = lax.broadcasted_iota(jnp.int32, (coarse, nz), 0).astype(F32)
    total = jnp.zeros((coarse, nz), F32)
    ready(2)

    @pl.when(at + 1 < n_line)
    def _():
        payload[at + 1, head:, :] = residual[nx - 2]

    @pl.when(at > 0)
    def _():
        payload[at - 1, head:, :] = residual[1]

    for a in range(ex):
        for b in range(ey):
            part = jnp.sum(residual[a * N : a * N + N, b * N : b * N + N, :], axis=(0, 1))[None]
            q = a * ey + b
            total = total + jnp.where(jnp.abs(unknown - wide[q : q + 1]) < 0.5, part, 0.0)
    coarse_residual = jnp.sum(total, axis=1, keepdims=True)
    ready(4)
    row = lax.broadcasted_iota(jnp.int32, (head, nz), 0)
    lines = jnp.where(row == n_stored, numbers, 0.0)
    for k in range(n_stored):
        lines = jnp.where(
            row == k, jnp.sum(values[k] * coarse_residual, axis=0, keepdims=True), lines
        )
    for i in range(n_line):
        payload[i, :head, :] = lines


def line_kernel(
    n_stored, ready, me, parts, residual, after1, after2, dense, x_low, x_high, to_high, to_low
):
    nx, ny, nz = residual.shape
    n_line = parts.shape[0]
    head = parts.shape[1] - ny
    at = me[0]
    rows = parts[:, :n_stored, :].reshape(n_line * n_stored, nz)
    if rows.shape[0] < nz:
        rows = jnp.concatenate([rows, jnp.zeros((nz - rows.shape[0], nz), F32)])
    numbers = jnp.sum(parts[:, n_stored : n_stored + 1, :], axis=0)
    n_blocks = dense.shape[0] * dense.shape[1]
    block = lax.broadcasted_iota(jnp.int32, (n_blocks, nz), 0).astype(F32)
    place = (jnp.abs(block - numbers) < 0.5).astype(F32)
    dense[...] = mm(place, rows).reshape(dense.shape)
    before, behind = jnp.maximum(at - 1, 0), jnp.minimum(at + 1, n_line - 1)
    x_low[...] = jnp.where(at > 0, parts[before, head:, :], 0.0)
    x_high[...] = jnp.where(at + 1 < n_line, parts[behind, head:, :], 0.0)
    for out, y in ((to_high, ny - 2), (to_low, 1)):
        out[...] = jnp.zeros_like(out)
        out[:nx] = residual[:, y, :]
        out[nx : nx + 1] = x_low[y : y + 1]
        out[nx + 1 : nx + 2] = x_high[y : y + 1]


def spread_sum_kernel(ready, parts, after, out):
    total = jnp.sum(parts[...], axis=0)
    for i in range(out.shape[0]):
        out[i] = total


def plane_kernel(
    ready, parts, residual, x_low, x_high, y_low, y_high, owned, every, to_high, to_low
):
    total = jnp.sum(parts[...], axis=0)
    for i in range(owned.shape[0]):
        owned[i] = total
    nx, ny, nz = residual.shape
    at = 0
    for ref in (None, x_low, x_high, y_low, y_high):
        block = residual[...].reshape(nx * ny, nz) if ref is None else ref[...]
        every[at : at + block.shape[0]] = block
        at += block.shape[0]
    row = lax.broadcasted_iota(jnp.int32, (8, nz), 0)
    lane = lax.broadcasted_iota(jnp.int32, (8, nz), 1)
    pick = ((row == 0) & (lane == nz - 2)) | ((row == 1) & (lane == 1))
    ends = mm(pick.astype(F32), every[...], 1, 1)
    to_high[...] = ends[0:1]
    to_low[...] = ends[1:2]


def matrices_kernel(
    ready, basis, tile2, mask2, tilez, maskz, row_x, row_y, col_x, col_y, out_x, out_y, col_z, in_z,
    to_spectral, from_spectral, to_z, from_z,
):
    ready(*range(13))
    flat2 = mm(mm(tile2[...], basis[...]), tile2[...], 1, 1) * mask2[...]
    flatz = mm(mm(tilez[...], basis[...]), tilez[...], 1, 1) * maskz[...]
    to_x = mm(row_x[...], mm(flat2, col_x[...], 0, 0))
    to_y = mm(row_y[...], mm(flat2, col_y[...], 0, 0))
    to_spectral[...] = to_x * to_y
    from_x = mm(mm(out_x[...], flat2), row_x[...], 1, 1)
    from_y = mm(mm(out_y[...], flat2), row_y[...], 1, 1)
    from_spectral[...] = from_x * from_y
    to_z[...] = mm(col_z[...], flatz)
    from_z[...] = mm(flatz, in_z[...], 0, 0)


def spectral_kernel(ready, every, to_spectral, to_z, spectral):
    ready(1, 2)
    spectral[...] = mm(mm(to_spectral[...], every[...]), to_z[: every.shape[1], :])


def solve_kernel(
    ready, inside, z_low, z_high, to_spectral, from_spectral, to_z, from_z, sums, local_part,
    inner, wide
):
    n_x, n_y, n_z = sums.shape
    wide[...] = jnp.zeros_like(wide)
    row = lax.broadcasted_iota(jnp.int32, (8, z_low.shape[1]), 0)
    ends = jnp.where(row == 0, z_low[...], jnp.where(row == 1, z_high[...], 0.0))
    ready(3, 5)
    spectral = inside[...] + mm(mm(to_spectral[...], ends, 1, 1), to_z[to_z.shape[0] - 8 :, :])
    ready(7)
    wide[:, :n_y, :] = sums[...]
    weighted = wide[...].reshape(-1, n_z) * spectral
    inner[...] = jnp.sum(jnp.sum(weighted * spectral, axis=0, keepdims=True), axis=1, keepdims=True)
    ready(4, 6)
    local_part[...] = mm(mm(from_spectral[...], weighted), from_z[...])


def derive(matrix, slabs):
    result = []
    for first in range(0, len(slabs), N):
        for i in range(N):
            terms = [float(matrix[i, j]) * slabs[first + j] for j in range(N)]
            while len(terms) > 1:
                terms = [a + b for a, b in zip(terms[::2], terms[1::2])]
            result.append(terms[0])
    return result


def operator(source, conductance, mass, ky, ky_t, kz, kz_t, target):
    nx, ny, nz = source.shape
    rows = nx * ny
    cheb = cheb_matrix()
    flat = source[...].reshape(rows, nz)
    along_y = mm(ky[...], flat) * conductance[1].reshape(rows, nz)
    along_z = mm(flat, kz_t[...]) * conductance[2].reshape(rows, nz)
    along_x = [g * conductance[0, x] for x, g in enumerate(derive(cheb, [source[x] for x in range(nx)]))]
    yz = mm(ky_t[...], along_y) + mm(along_z, kz[...])
    for x, value in enumerate(derive(cheb.T, along_x)):
        target[x] = mass[x] * source[x] + value + yz[x * ny : (x + 1) * ny]


def operator_kernel(ready, direction, conductance, mass, ky, ky_t, kz, kz_t, image):
    ready(0, 1, 2, 3, 4, 5, 6)
    operator(direction, conductance, mass, ky, ky_t, kz, kz_t, image)


def total_of(values):
    return jnp.sum(jnp.sum(values, axis=0, keepdims=True), axis=1, keepdims=True)


def correct_kernel(
    ready, blocks, coarse_inner, values, ids_wide, local_part, direction, image_direction,
    conductance, mass, ky, ky_t, kz, kz_t,
    z_out, image_out, to_high, to_low,
):
    nx, ny, nz = direction.shape
    rows = nx * ny
    n_stored, coarse, block = values.shape
    total = jnp.zeros((coarse, block), F32)
    for k in range(n_stored):
        total = total + values[k] * coarse_inner[pl.ds(blocks[k], 1), :]
    solution = jnp.sum(total, axis=1, keepdims=True)
    unknown = lax.broadcasted_iota(jnp.int32, (coarse, nz), 0).astype(F32)
    ey = ny // N
    for a in range(nx // N):
        for b in range(ey):
            q = a * ey + b
            hit = jnp.abs(unknown - ids_wide[q : q + 1, :]) < 0.5
            line = jnp.sum(jnp.where(hit, solution, 0.0), axis=0, keepdims=True)
            for x in range(N):
                at = (a * N + x) * ny + b * N
                z_out[a * N + x, b * N : b * N + N, :] = local_part[at : at + N, :] + line
    operator(z_out, conductance, mass, ky, ky_t, kz, kz_t, image_out)
    for out, x in ((to_high, nx - 1), (to_low, 0)):
        out[0, :ny] = image_out[x]
        out[1, :ny] = image_direction[x]


def terms_kernel(
    ready, z, image, direction, image_direction, inner_local, coarse_inner, after, terms, square
):
    first = jnp.sum(z[...] * image[...], axis=0)
    second = jnp.sum(z[...] * image_direction[...] + direction[...] * image[...], axis=0)
    third = jnp.sum(direction[...] * image_direction[...], axis=0)
    lane = lax.broadcasted_iota(jnp.int32, (1, terms.shape[2]), 1)
    line = jnp.where(lane == 0, inner_local[...], 0.0)
    for i, value in enumerate((first, second, third)):
        line = jnp.where(lane == i + 1, total_of(value), line)
    for i in range(terms.shape[0]):
        terms[i] = line
    square[...] = total_of(coarse_inner[...] * coarse_inner[...])


def assemble_length_kernel(
    ready, image, image_direction, low, high, out, to_high, to_low
):
    nx, ny, nz = image.shape
    for i, ref in ((0, image), (1, image_direction)):
        out[i] = ref[...]
        for x in range(nx):
            if x % N == N - 1:
                out[i, x] = ref[x] + (ref[x + 1] if x + 1 < nx else high[i, :ny])
            elif x % N == 0:
                out[i, x] = ref[x] + (ref[x - 1] if x else low[i, :ny])
        to_high[i, :nx] = out[i, :, ny - 1, :]
        to_low[i, :nx] = out[i, :, 0, :]


def assemble_across_kernel(ready, images, low, high, solution, out, to_high, to_low):
    _, nx, ny, nz = images.shape
    out[...] = images[...]
    for i in range(2):
        for y in range(ny):
            if y % N == N - 1:
                other = images[i, :, y + 1, :] if y + 1 < ny else high[i, :nx]
            elif y % N == 0:
                other = images[i, :, y - 1, :] if y else low[i, :nx]
            else:
                continue
            out[i, :, y, :] = images[i, :, y, :] + other
    row = lax.broadcasted_iota(jnp.int32, (8, nz), 0)
    lane = lax.broadcasted_iota(jnp.int32, (8, nz), 1)
    pick = ((row == 0) & (lane == nz - 1)) | ((row == 1) & (lane == 0))
    ends = mm(pick.astype(F32), out[...].reshape(2 * nx * ny, nz), 1, 1)
    to_high[...] = ends[0:1]
    to_low[...] = ends[1:2]


def update_kernel(
    ready, prior, terms, square, images, low, high, residual, solution, direction, z,
    new_solution, new_residual, new_direction,
):
    nx, ny, nz = residual.shape
    rows = nx * ny
    lane1 = lax.broadcasted_iota(jnp.int32, (1, nz), 1)
    sums = jnp.sum(terms[...], axis=0)

    def term(i):
        return jnp.sum(jnp.where(lane1 == i, sums, 0.0), axis=1, keepdims=True)

    inner = term(0) + square[...]
    ratio = inner / prior[0]
    alpha = inner / (term(1) + ratio * term(2) + ratio * ratio * term(3))
    new = z[...].reshape(rows, nz) + ratio * direction[...].reshape(rows, nz)
    new_direction[...] = new.reshape(nx, ny, nz)
    new_solution[...] = (solution[...].reshape(rows, nz) + alpha * new).reshape(nx, ny, nz)
    image = images[0].reshape(rows, nz) + ratio * images[1].reshape(rows, nz)
    row = lax.broadcasted_iota(jnp.int32, (8, rows), 0)
    low_line = low[:, :rows] + ratio * low[:, rows:]
    high_line = high[:, :rows] + ratio * high[:, rows:]
    ends = jnp.where(row == 0, low_line, jnp.where(row == 1, high_line, 0.0))
    row = lax.broadcasted_iota(jnp.int32, (8, nz), 0)
    lane = lax.broadcasted_iota(jnp.int32, (8, nz), 1)
    place = ((row == 0) & (lane == 0)) | ((row == 1) & (lane == nz - 1))
    outer = mm(jnp.transpose(ends), place.astype(F32))
    lane = lax.broadcasted_iota(jnp.int32, (rows, nz), 1)
    above = pltpu.roll(image, nz - 1, 1)
    below = pltpu.roll(image, 1, 1)
    above = jnp.where((lane % N == N - 1) & (lane < nz - 1), above, 0.0)
    below = jnp.where((lane % N == 0) & (lane > 0), below, 0.0)
    image = image + above + below + outer
    new_residual[...] = (residual[...].reshape(rows, nz) - alpha * image).reshape(nx, ny, nz)


def shifts(axis):
    count = lax.axis_size(axis)
    forward = [(i, i + 1) for i in range(count - 1)]
    return forward, [(b, a) for a, b in forward]


def exchange(to_high, to_low, axis):
    forward, backward = shifts(axis)
    return lax.ppermute(to_high, axis, forward), lax.ppermute(to_low, axis, backward)


def spread(values, axes):
    return lax.all_to_all(values, axes, 0, 0, tiled=False)


def body(
    residual,
    solution,
    direction,
    conductance,
    mass_term,
    eigen_basis,
    inverse_eigen_sums,
    element_coarse_index,
    xxt_values,
    xxt_blocks,
    prior_inner,
):
    nx, ny, nz = residual.shape
    ex, ey, ez = nx // N, ny // N, nz // N
    rows = nx * ny
    plane = ("gy", "gz")
    n_plane, n_line = lax.axis_size(plane), lax.axis_size("gx")
    coarse_count, block = xxt_values.shape[1:]
    n_blocks = coarse_count * n_plane * n_line // block
    own = n_blocks // n_plane

    ids = element_coarse_index.reshape(ex * ey, ez)
    me = lax.axis_index("gx").astype(jnp.int32).reshape(1)
    head = up8(xxt_values.shape[0] + 1)
    assert xxt_values.shape[0] * n_line <= nz
    payload, ids_wide, residual, xxt_values = call(
        coarse_kernel, "coarse_restrict", [(n_line, head + ny, nz), (ex * ey, nz)],
        xxt_blocks, me, residual, ids, xxt_values, smem=(0, 1), load=(3,), keep=(2, 4), pin=(1,),
    )
    parts = spread(payload, "gx")

    cheb = cheb_matrix()
    ky = np.kron(np.eye(nx, dtype=np.float32), np.kron(np.eye(ey, dtype=np.float32), cheb))
    kz = np.kron(np.eye(ez, dtype=np.float32), cheb)
    tables = [jnp.asarray(np.ascontiguousarray(t)) for t in (ky, ky.T, kz, kz.T)]
    image_direction, direction, conductance, mass_term, *tables = call(
        operator_kernel, "operator_direction", [direction.shape],
        direction, conductance, mass_term, *tables, keep=tuple(range(7)), pin=(0,),
    )

    face = up8(nx + 2)
    n_every = rows + 2 * ny + 2 * face
    pad = [-1] * (face - nx - 2)
    line = [*range(nx), nx, nx + 1, *pad]
    cols_x = np.array([*np.repeat(np.arange(nx), ny), *[nx] * ny, *[nx + 1] * ny, *line, *line])
    cols_y = np.array(
        [*np.tile(np.arange(ny), nx), *range(ny), *range(ny), *[ny] * face, *[ny + 1] * face]
    )
    n_x, n_y, n_z = inverse_eigen_sums.shape
    high_y = up8(n_y)
    place_y = np.tile(np.arange(high_y), n_x)
    row_x = one_hot(np.repeat(np.arange(n_x), high_y), n_x) * (place_y < n_y)[:, None]
    row_y = one_hot(place_y, n_y)
    col_x = (extended_positions(ex)[:, None] == cols_x[None, :]).astype(np.float32)
    col_y = (extended_positions(ey)[:, None] == cols_y[None, :]).astype(np.float32)
    assert ex == ey
    to_spectral, from_spectral, to_z, from_z = call(
        matrices_kernel, "basis_matrices",
        [(n_x * high_y, n_every), (rows, n_x * high_y), (nz + 8, n_z), (n_z, nz)],
        eigen_basis,
        *map(
            jnp.asarray,
            (
                np.tile(np.eye(E, dtype=np.float32), (ex, 1)),
                np.kron(np.eye(ex), np.ones((E, E))).astype(np.float32),
                np.tile(np.eye(E, dtype=np.float32), (ez, 1)),
                np.kron(np.eye(ez), np.ones((E, E))).astype(np.float32),
                row_x.astype(np.float32),
                row_y,
                col_x,
                col_y,
                one_hot(np.repeat(inside_positions(ex), ny), n_x),
                one_hot(np.tile(inside_positions(ey), nx), n_y),
                np.ascontiguousarray(one_hot(extended_positions(ez), nz + 8).T),
                np.ascontiguousarray(one_hot(inside_positions(ez), n_z).T),
            ),
        ),
        load=tuple(range(13)), store=(0, 1, 2, 3),
    )

    dense, x_low, x_high, to_high, to_low = call(
        functools.partial(line_kernel, xxt_values.shape[0]), "line_sum",
        [(n_plane, own, block), (ny, nz), (ny, nz), (face, nz), (face, nz)],
        me, parts, residual, image_direction, from_z, smem=(0,), pin=(1, 2), idle=(4,),
    )
    parts = spread(dense, plane)
    y_low, y_high = exchange(to_high, to_low, "gy")
    owned, every, to_high, to_low = call(
        plane_kernel, "plane_sum",
        [(n_plane, own, block), (n_every, nz), (1, n_every), (1, n_every)],
        parts, residual, x_low, x_high, y_low, y_high, pin=(1,),
    )
    coarse_inner = spread(owned, plane).reshape(n_blocks, block)
    z_low, z_high = exchange(to_high, to_low, "gz")
    (spectral,) = call(
        spectral_kernel, "element_spectral", [(n_x * high_y, n_z)],
        every, to_spectral, to_z, load=(1, 2), pin=(0,),
    )
    local_part, inner_local = call(
        solve_kernel, "element_solve", [(rows, nz), (1, 1)],
        spectral, z_low, z_high, to_spectral, from_spectral, to_z, from_z, inverse_eigen_sums,
        load=(3, 4, 5, 6, 7), pin=(0, 1), scratch=(pltpu.VMEM((n_x, high_y, n_z), F32),),
    )

    z, image, to_high, to_low = call(
        correct_kernel, "coarse_correct",
        [direction.shape, direction.shape, (2, 4 * ny, nz), (2, 4 * ny, nz)],
        xxt_blocks, coarse_inner, xxt_values, ids_wide, local_part, direction,
        image_direction, conductance, mass_term, *tables, smem=(0,), pin=(0, 1),
    )
    low, high = exchange(to_high, to_low, "gx")
    terms, square = call(
        terms_kernel, "terms", [(n_plane, 1, nz), (1, 1)],
        z, image, direction, image_direction, inner_local, coarse_inner, low, pin=(1,),
    )
    parts = spread(terms, plane)
    images, to_high, to_low = call(
        assemble_length_kernel, "assemble_length", [(2, nx, ny, nz), (2, 2 * nx, nz), (2, 2 * nx, nz)],
        image, image_direction, low, high, pin=(0,),
    )
    low, high = exchange(to_high, to_low, "gy")
    (terms,) = call(spread_sum_kernel, "sum_terms", [(n_line, 1, nz)], parts, low)
    parts = spread(terms, "gx")
    images, to_high, to_low, solution = call(
        assemble_across_kernel, "assemble_across", [(2, nx, ny, nz), (1, 2 * rows), (1, 2 * rows)],
        images, low, high, solution, keep=(3,), pin=(0,),
    )
    low, high = exchange(to_high, to_low, "gz")
    return tuple(
        call(
            update_kernel, "update", [direction.shape] * 3,
            prior_inner, parts, square, images, low, high, residual, solution, direction, z,
            smem=(0,),
        )
    )


def solution(mesh):
    whole = P("gx", "gy", "gz")
    in_specs = (
        whole,
        whole,
        whole,
        P(None, "gx", "gy", "gz"),
        whole,
        P(),
        whole,
        whole,
        P(("gx", "gy", "gz"), None, None),
        P(("gx", "gy", "gz")),
        P(),
    )
    return jax.shard_map(
        body, mesh=mesh, in_specs=in_specs, out_specs=(whole, whole, whole), check_vma=False
    )
```

```python
import jax
import jax.numpy as jnp
import numpy as np
from jax import lax
from jax.experimental import pallas as pl
from jax.experimental.pallas import tpu as pltpu
from jax.sharding import PartitionSpec as P

HIGH = lax.Precision.HIGHEST
N = 8
E = 10
F32 = jnp.float32


def cheb_matrix():
    count = 8
    points = np.cos(np.pi * np.arange(count) / (count - 1))
    signs = np.array([2.0, 1, 1, 1, 1, 1, 1, 2.0]) * (-1.0) ** np.arange(count)
    differ = points[:, None] - points[None, :] + np.eye(count)
    matrix = np.outer(signs, 1.0 / signs) / differ
    matrix = matrix - np.eye(count) * np.sum(matrix, axis=1)[:, None]
    return (0.25 * matrix).astype(np.float32)


def extended_positions(count):
    length = N * count
    result = []
    for element in range(count):
        for node in [N * element - 2, *range(N * element, N * element + N), N * element + N + 1]:
            result.append(length if node < 0 else length + 1 if node >= length else node)
    return np.array(result)


def inside_positions(count):
    return np.concatenate([np.arange(E * e + 1, E * e + N + 1) for e in range(count)])


def one_hot(index, size):
    return (np.asarray(index)[:, None] == np.arange(size)[None, :]).astype(np.float32)


def up8(count):
    return -(-count // 8) * 8


def mm(a, b, ca=1, cb=0):
    return lax.dot_general(
        a, b, (((ca,), (cb,)), ((), ())), precision=HIGH, preferred_element_type=F32
    )


def call(kernel, name, outs, *args, smem=(), load=(), keep=(), scratch=(), pin=(), store=(), idle=()):
    count, n_out, n_keep = len(args), len(outs), len(keep)
    moved = sorted((*load, *keep))
    vmem = pl.BlockSpec(memory_space=pltpu.VMEM)

    def whole(*refs):
        inside, results = list(refs[:count]), refs[count : count + n_out]
        kept = refs[count + n_out : count + n_out + n_keep]
        rest = list(refs[count + n_out + n_keep :])
        sems = rest.pop() if moved or store else None
        written = list(results)
        for i in store:
            written[i] = rest.pop()
        copies = {}
        for at, i in enumerate(moved):
            target = kept[keep.index(i)] if i in keep else rest.pop()
            copies[i] = pltpu.make_async_copy(inside[i], target, sems.at[at])
            copies[i].start()
            inside[i] = target
        waiting = dict(copies)

        def ready(*which):
            for i in which:
                if i in waiting:
                    waiting.pop(i).wait()

        kernel(ready, *inside, *written, *rest)
        ready(*moved)
        copies = [
            pltpu.make_async_copy(written[i], results[i], sems.at[len(moved) + at])
            for at, i in enumerate(store)
        ]
        for copy in copies:
            copy.start()
        for copy in copies:
            copy.wait()

    buffers = [pltpu.VMEM(args[i].shape, args[i].dtype) for i in moved if i not in keep]
    specs = []
    for i in range(count):
        space = pltpu.SMEM if i in smem else pltpu.HBM if i in (*moved, *idle) else pltpu.VMEM
        specs.append(pl.BlockSpec(memory_space=space))
    args = [
        pltpu.with_memory_space_constraint(a, pltpu.HBM) if i in (*moved, *idle) else a
        for i, a in enumerate(args)
    ]
    size = sum(int(np.prod(a.shape)) * 4 for a in args) + sum(int(np.prod(o)) * 4 for o in outs)
    return pl.pallas_call(
        whole,
        out_shape=[
            pltpu.VMEM(o, F32)
            if i in pin
            else pltpu.HBM(o, F32)
            if i in store
            else jax.ShapeDtypeStruct(o, F32)
            for i, o in enumerate(outs)
        ]
        + [pltpu.VMEM(args[i].shape, args[i].dtype) for i in keep],
        in_specs=specs,
        out_specs=[
            pl.BlockSpec(memory_space=pltpu.HBM) if i in store else vmem
            for i in range(n_out + n_keep)
        ],
        scratch_shapes=[
            *scratch,
            *buffers[::-1],
            *[pltpu.VMEM(outs[i], F32) for i in store[::-1]],
            *([pltpu.SemaphoreType.DMA((len(moved) + len(store),))] if moved or store else []),
        ],
        cost_estimate=pl.CostEstimate(flops=0, bytes_accessed=size, transcendentals=0),
        compiler_params=pltpu.CompilerParams(vmem_limit_bytes=24 * 2**20),
        name=name,
    )(*args)


def coarse_kernel(ready, blocks, residual, ids, values, dense, ids_wide, to_high, to_low):
    nx, ny, nz = residual.shape
    ex, ey = nx // N, ny // N
    ez = ids.shape[1]
    n_stored, coarse, _ = values.shape
    widen = (
        lax.broadcasted_iota(jnp.int32, (ez, nz), 1) // N
        == lax.broadcasted_iota(jnp.int32, (ez, nz), 0)
    ).astype(F32)
    dense[...] = jnp.zeros_like(dense)
    ready(2)
    wide = mm(ids[...].astype(F32), widen)
    ids_wide[...] = wide
    unknown = lax.broadcasted_iota(jnp.int32, (coarse, nz), 0).astype(F32)
    total = jnp.zeros((coarse, nz), F32)
    ready(1)
    to_high[...] = residual[nx - 2]
    to_low[...] = residual[1]
    for a in range(ex):
        for b in range(ey):
            part = jnp.sum(residual[a * N : a * N + N, b * N : b * N + N, :], axis=(0, 1))[None]
            q = a * ey + b
            total = total + jnp.where(jnp.abs(unknown - wide[q : q + 1]) < 0.5, part, 0.0)
    coarse_residual = jnp.sum(total, axis=1, keepdims=True)
    ready(3)
    for k in range(n_stored):
        at = pl.ds(blocks[k], 1)
        row = jnp.sum(values[k] * coarse_residual, axis=0, keepdims=True)
        dense[at, :] = dense[at, :] + row


def spread_sum(parts, out):
    total = jnp.sum(parts[...], axis=0)
    for i in range(out.shape[0]):
        out[i] = total


def across_kernel(ready, parts, residual, low, high, after1, after2, owned, to_high, to_low):
    spread_sum(parts, owned)
    nx, ny, nz = residual.shape
    for out, y in ((to_high, ny - 2), (to_low, 1)):
        out[...] = jnp.zeros_like(out)
        out[:nx] = residual[:, y, :]
        out[nx : nx + 1] = low[y : y + 1]
        out[nx + 1 : nx + 2] = high[y : y + 1]


def spread_sum_kernel(ready, parts, after, out):
    spread_sum(parts, out)


def depth_kernel(
    ready, parts, residual, x_low, x_high, y_low, y_high, after, owned, every, to_high, to_low
):
    spread_sum(parts, owned)
    nx, ny, nz = residual.shape
    at = 0
    for ref in (None, x_low, x_high, y_low, y_high):
        block = residual[...].reshape(nx * ny, nz) if ref is None else ref[...]
        every[at : at + block.shape[0]] = block
        at += block.shape[0]
    row = lax.broadcasted_iota(jnp.int32, (8, nz), 0)
    lane = lax.broadcasted_iota(jnp.int32, (8, nz), 1)
    pick = ((row == 0) & (lane == nz - 2)) | ((row == 1) & (lane == 1))
    ends = mm(pick.astype(F32), every[...], 1, 1)
    to_high[...] = ends[0:1]
    to_low[...] = ends[1:2]


def tiled(tile, basis, mask):
    return mm(mm(tile[...], basis[...]), tile[...], 1, 1) * mask[...]


def to_spectral_kernel(
    ready, basis, tile2, mask2, tilez, maskz, row_x, row_y, col_x, col_y, col_z, to_spectral, to_z
):
    ready(*range(10))
    flat2 = tiled(tile2, basis, mask2)
    to_x = mm(row_x[...], mm(flat2, col_x[...], 0, 0))
    to_y = mm(row_y[...], mm(flat2, col_y[...], 0, 0))
    to_spectral[...] = to_x * to_y
    to_z[...] = mm(col_z[...], tiled(tilez, basis, maskz))


def from_spectral_kernel(
    ready, basis, tile2, mask2, tilez, maskz, row_x, row_y, out_x, out_y, in_z, from_spectral,
    from_z,
):
    ready(*range(10))
    flat2 = tiled(tile2, basis, mask2)
    from_x = mm(mm(out_x[...], flat2), row_x[...], 1, 1)
    from_y = mm(mm(out_y[...], flat2), row_y[...], 1, 1)
    from_spectral[...] = from_x * from_y
    from_z[...] = mm(tiled(tilez, basis, maskz), in_z[...], 0, 0)


def spectral_kernel(ready, every, to_spectral, to_z, spectral):
    ready(1, 2)
    spectral[...] = mm(mm(to_spectral[...], every[...]), to_z[: every.shape[1], :])


def solve_kernel(
    ready, inside, z_low, z_high, to_spectral, from_spectral, to_z, from_z, sums, local_part,
    inner, wide
):
    n_x, n_y, n_z = sums.shape
    wide[...] = jnp.zeros_like(wide)
    row = lax.broadcasted_iota(jnp.int32, (8, z_low.shape[1]), 0)
    ends = jnp.where(row == 0, z_low[...], jnp.where(row == 1, z_high[...], 0.0))
    ready(3, 5)
    spectral = inside[...] + mm(mm(to_spectral[...], ends, 1, 1), to_z[to_z.shape[0] - 8 :, :])
    ready(7)
    wide[:, :n_y, :] = sums[...]
    weighted = wide[...].reshape(-1, n_z) * spectral
    inner[...] = jnp.sum(jnp.sum(weighted * spectral, axis=0, keepdims=True), axis=1, keepdims=True)
    ready(4, 6)
    local_part[...] = mm(mm(from_spectral[...], weighted), from_z[...])


def derive(matrix, slabs):
    result = []
    for first in range(0, len(slabs), N):
        for i in range(N):
            terms = [float(matrix[i, j]) * slabs[first + j] for j in range(N)]
            while len(terms) > 1:
                terms = [a + b for a, b in zip(terms[::2], terms[1::2])]
            result.append(terms[0])
    return result


def operator(source, conductance, mass, ky, ky_t, kz, kz_t, target):
    nx, ny, nz = source.shape
    rows = nx * ny
    cheb = cheb_matrix()
    flat = source[...].reshape(rows, nz)
    along_y = mm(ky[...], flat) * conductance[1].reshape(rows, nz)
    along_z = mm(flat, kz_t[...]) * conductance[2].reshape(rows, nz)
    along_x = [g * conductance[0, x] for x, g in enumerate(derive(cheb, [source[x] for x in range(nx)]))]
    yz = mm(ky_t[...], along_y) + mm(along_z, kz[...])
    for x, value in enumerate(derive(cheb.T, along_x)):
        target[x] = mass[x] * source[x] + value + yz[x * ny : (x + 1) * ny]


def operator_kernel(ready, direction, conductance, mass, ky, ky_t, kz, kz_t, image, third):
    ready(0, 1, 2, 3, 4, 5, 6)
    operator(direction, conductance, mass, ky, ky_t, kz, kz_t, image)
    third[...] = total_of(jnp.sum(direction[...] * image[...], axis=0))


def total_of(values):
    return jnp.sum(jnp.sum(values, axis=0, keepdims=True), axis=1, keepdims=True)


def correct_kernel(
    ready, blocks, coarse_inner, values, ids_wide, local_part, direction, image_direction,
    conductance, mass, ky, ky_t, kz, kz_t,
    z_out, image_out, to_high, to_low,
):
    nx, ny, nz = direction.shape
    rows = nx * ny
    n_stored, coarse, block = values.shape
    total = jnp.zeros((coarse, block), F32)
    for k in range(n_stored):
        total = total + values[k] * coarse_inner[pl.ds(blocks[k], 1), :]
    solution = jnp.sum(total, axis=1, keepdims=True)
    unknown = lax.broadcasted_iota(jnp.int32, (coarse, nz), 0).astype(F32)
    ey = ny // N
    for a in range(nx // N):
        for b in range(ey):
            q = a * ey + b
            hit = jnp.abs(unknown - ids_wide[q : q + 1, :]) < 0.5
            line = jnp.sum(jnp.where(hit, solution, 0.0), axis=0, keepdims=True)
            for x in range(N):
                at = (a * N + x) * ny + b * N
                z_out[a * N + x, b * N : b * N + N, :] = local_part[at : at + N, :] + line
    operator(z_out, conductance, mass, ky, ky_t, kz, kz_t, image_out)
    for out, x in ((to_high, nx - 1), (to_low, 0)):
        out[0, :ny] = image_out[x]
        out[1, :ny] = image_direction[x]


def terms_kernel(
    ready, z, image, direction, image_direction, inner_local, third, after, terms
):
    first = total_of(jnp.sum(z[...] * image[...], axis=0))
    second = z[...] * image_direction[...] + direction[...] * image[...]
    second = total_of(jnp.sum(second, axis=0))
    lane = lax.broadcasted_iota(jnp.int32, (1, terms.shape[2]), 1)
    line = jnp.where(lane == 0, inner_local[...], 0.0)
    for i, value in enumerate((first, second, third[...])):
        line = jnp.where(lane == i + 1, value, line)
    for i in range(terms.shape[0]):
        terms[i] = line


def assemble_length_kernel(
    ready, image, image_direction, low, high, coarse_inner, out, to_high, to_low, square
):
    square[...] = total_of(coarse_inner[...] * coarse_inner[...])
    nx, ny, nz = image.shape
    for i, ref in ((0, image), (1, image_direction)):
        out[i] = ref[...]
        for x in range(nx):
            if x % N == N - 1:
                out[i, x] = ref[x] + (ref[x + 1] if x + 1 < nx else high[i, :ny])
            elif x % N == 0:
                out[i, x] = ref[x] + (ref[x - 1] if x else low[i, :ny])
        to_high[i, :nx] = out[i, :, ny - 1, :]
        to_low[i, :nx] = out[i, :, 0, :]


def assemble_across_kernel(ready, images, low, high, solution, out, to_high, to_low):
    _, nx, ny, nz = images.shape
    out[...] = images[...]
    for i in range(2):
        for y in range(ny):
            if y % N == N - 1:
                other = images[i, :, y + 1, :] if y + 1 < ny else high[i, :nx]
            elif y % N == 0:
                other = images[i, :, y - 1, :] if y else low[i, :nx]
            else:
                continue
            out[i, :, y, :] = images[i, :, y, :] + other
    row = lax.broadcasted_iota(jnp.int32, (8, nz), 0)
    lane = lax.broadcasted_iota(jnp.int32, (8, nz), 1)
    pick = ((row == 0) & (lane == nz - 1)) | ((row == 1) & (lane == 0))
    ends = mm(pick.astype(F32), out[...].reshape(2 * nx * ny, nz), 1, 1)
    to_high[...] = ends[0:1]
    to_low[...] = ends[1:2]


def assemble_depth_kernel(ready, images, low, high, out):
    _, nx, ny, nz = images.shape
    rows = 2 * nx * ny
    image = images[...].reshape(rows, nz)
    row = lax.broadcasted_iota(jnp.int32, (8, rows), 0)
    ends = jnp.where(row == 0, low[...], jnp.where(row == 1, high[...], 0.0))
    row = lax.broadcasted_iota(jnp.int32, (8, nz), 0)
    lane = lax.broadcasted_iota(jnp.int32, (8, nz), 1)
    place = ((row == 0) & (lane == 0)) | ((row == 1) & (lane == nz - 1))
    outer = mm(jnp.transpose(ends), place.astype(F32))
    lane = lax.broadcasted_iota(jnp.int32, (rows, nz), 1)
    above = jnp.where((lane % N == N - 1) & (lane < nz - 1), pltpu.roll(image, nz - 1, 1), 0.0)
    below = jnp.where((lane % N == 0) & (lane > 0), pltpu.roll(image, 1, 1), 0.0)
    out[...] = (image + above + below + outer).reshape(out.shape)


def update_kernel(
    ready, prior, terms, square, images, residual, solution, direction, z,
    new_solution, new_residual, new_direction,
):
    lane = lax.broadcasted_iota(jnp.int32, (1, terms.shape[2]), 1)
    sums = jnp.sum(terms[...], axis=0)

    def term(i):
        return jnp.sum(jnp.where(lane == i, sums, 0.0), axis=1, keepdims=True)

    inner = term(0) + square[...]
    ratio = inner / prior[0]
    alpha = inner / (term(1) + ratio * term(2) + ratio * ratio * term(3))
    ratio, alpha = ratio[None], alpha[None]
    new = z[...] + ratio * direction[...]
    new_direction[...] = new
    new_solution[...] = solution[...] + alpha * new
    new_residual[...] = residual[...] - alpha * (images[0] + ratio * images[1])


def shifts(axis):
    count = lax.axis_size(axis)
    forward = [(i, i + 1) for i in range(count - 1)]
    return forward, [(b, a) for a, b in forward]


def exchange(to_high, to_low, axis):
    forward, backward = shifts(axis)
    return lax.ppermute(to_high, axis, forward), lax.ppermute(to_low, axis, backward)


def spread(values, axes):
    return lax.all_to_all(values, axes, 0, 0, tiled=False)


def body(
    residual,
    solution,
    direction,
    conductance,
    mass_term,
    eigen_basis,
    inverse_eigen_sums,
    element_coarse_index,
    xxt_values,
    xxt_blocks,
    prior_inner,
):
    nx, ny, nz = residual.shape
    ex, ey, ez = nx // N, ny // N, nz // N
    rows = nx * ny
    plane = ("gy", "gz")
    n_plane, n_line = lax.axis_size(plane), lax.axis_size("gx")
    coarse_count, block = xxt_values.shape[1:]
    n_blocks = coarse_count * n_plane * n_line // block
    own = n_blocks // n_plane

    ids = element_coarse_index.reshape(ex * ey, ez)
    dense, ids_wide, to_high, to_low, residual, xxt_values = call(
        coarse_kernel, "coarse_restrict", [(n_blocks, block), (ex * ey, nz), (ny, nz), (ny, nz)],
        xxt_blocks, residual, ids, xxt_values, smem=(0,), load=(2,), keep=(1, 3), pin=(1,),
    )
    parts = spread(dense.reshape(n_plane, own, block), plane)
    x_low, x_high = exchange(to_high, to_low, "gx")

    cheb = cheb_matrix()
    ky = np.kron(np.eye(nx, dtype=np.float32), np.kron(np.eye(ey, dtype=np.float32), cheb))
    kz = np.kron(np.eye(ez, dtype=np.float32), cheb)
    tables = [jnp.asarray(np.ascontiguousarray(t)) for t in (ky, ky.T, kz, kz.T)]
    image_direction, third, direction, conductance, mass_term, *tables = call(
        operator_kernel, "operator_direction", [direction.shape, (1, 1)],
        direction, conductance, mass_term, *tables, keep=tuple(range(7)), pin=(0, 1),
    )

    face = up8(nx + 2)
    n_every = rows + 2 * ny + 2 * face
    pad = [-1] * (face - nx - 2)
    line = [*range(nx), nx, nx + 1, *pad]
    cols_x = np.array([*np.repeat(np.arange(nx), ny), *[nx] * ny, *[nx + 1] * ny, *line, *line])
    cols_y = np.array(
        [*np.tile(np.arange(ny), nx), *range(ny), *range(ny), *[ny] * face, *[ny + 1] * face]
    )
    n_x, n_y, n_z = inverse_eigen_sums.shape
    high_y = up8(n_y)
    place_y = np.tile(np.arange(high_y), n_x)
    row_x = one_hot(np.repeat(np.arange(n_x), high_y), n_x) * (place_y < n_y)[:, None]
    row_y = one_hot(place_y, n_y)
    col_x = (extended_positions(ex)[:, None] == cols_x[None, :]).astype(np.float32)
    col_y = (extended_positions(ey)[:, None] == cols_y[None, :]).astype(np.float32)
    assert ex == ey
    shared = [
        np.tile(np.eye(E, dtype=np.float32), (ex, 1)),
        np.kron(np.eye(ex), np.ones((E, E))).astype(np.float32),
        np.tile(np.eye(E, dtype=np.float32), (ez, 1)),
        np.kron(np.eye(ez), np.ones((E, E))).astype(np.float32),
        row_x.astype(np.float32),
        row_y,
    ]
    shared = [eigen_basis, *map(jnp.asarray, shared)]
    to_spectral, to_z = call(
        to_spectral_kernel, "to_spectral", [(n_x * high_y, n_every), (nz + 8, n_z)],
        *shared, jnp.asarray(col_x), jnp.asarray(col_y),
        jnp.asarray(np.ascontiguousarray(one_hot(extended_positions(ez), nz + 8).T)),
        load=tuple(range(10)), store=(0, 1),
    )
    from_spectral, from_z = call(
        from_spectral_kernel, "from_spectral", [(rows, n_x * high_y), (n_z, nz)],
        *shared, jnp.asarray(one_hot(np.repeat(inside_positions(ex), ny), n_x)),
        jnp.asarray(one_hot(np.tile(inside_positions(ey), nx), n_y)),
        jnp.asarray(np.ascontiguousarray(one_hot(inside_positions(ez), n_z).T)),
        load=tuple(range(10)), store=(0, 1),
    )
    owned, to_high, to_low = call(
        across_kernel, "plane_sum", [(n_line, own, block), (face, nz), (face, nz)],
        parts, residual, x_low, x_high, image_direction, to_z, idle=(5,),
    )
    parts = spread(owned, "gx")
    y_low, y_high = exchange(to_high, to_low, "gy")
    owned, every, to_high, to_low = call(
        depth_kernel, "line_sum",
        [(n_plane, own, block), (n_every, nz), (1, n_every), (1, n_every)],
        parts, residual, x_low, x_high, y_low, y_high, from_z, pin=(1,), idle=(6,),
    )
    coarse_inner = spread(owned, plane).reshape(n_blocks, block)
    z_low, z_high = exchange(to_high, to_low, "gz")
    (spectral,) = call(
        spectral_kernel, "element_spectral", [(n_x * high_y, n_z)],
        every, to_spectral, to_z, load=(1, 2), pin=(0,),
    )
    local_part, inner_local = call(
        solve_kernel, "element_solve", [(rows, nz), (1, 1)],
        spectral, z_low, z_high, to_spectral, from_spectral, to_z, from_z, inverse_eigen_sums,
        load=(3, 4, 5, 6, 7), pin=(0, 1), scratch=(pltpu.VMEM((n_x, high_y, n_z), F32),),
    )

    z, image, to_high, to_low = call(
        correct_kernel, "coarse_correct",
        [direction.shape, direction.shape, (2, 4 * ny, nz), (2, 4 * ny, nz)],
        xxt_blocks, coarse_inner, xxt_values, ids_wide, local_part, direction,
        image_direction, conductance, mass_term, *tables, smem=(0,), pin=(0, 1),
    )
    low, high = exchange(to_high, to_low, "gx")
    (terms,) = call(
        terms_kernel, "terms", [(n_plane, 1, nz)],
        z, image, direction, image_direction, inner_local, third, low,
    )
    parts = spread(terms, plane)
    images, to_high, to_low, square = call(
        assemble_length_kernel, "assemble_length",
        [(2, nx, ny, nz), (2, 2 * nx, nz), (2, 2 * nx, nz), (1, 1)],
        image, image_direction, low, high, coarse_inner, pin=(0, 3),
    )
    low, high = exchange(to_high, to_low, "gy")
    (terms,) = call(spread_sum_kernel, "sum_terms", [(n_line, 1, nz)], parts, low)
    parts = spread(terms, "gx")
    images, to_high, to_low, solution = call(
        assemble_across_kernel, "assemble_across", [(2, nx, ny, nz), (1, 2 * rows), (1, 2 * rows)],
        images, low, high, solution, keep=(3,), pin=(0,),
    )
    low, high = exchange(to_high, to_low, "gz")
    (images,) = call(
        assemble_depth_kernel, "assemble_depth", [images.shape], images, low, high, pin=(0,)
    )
    return tuple(
        call(
            update_kernel, "update", [direction.shape] * 3,
            prior_inner, parts, square, images, residual, solution, direction, z, smem=(0,),
        )
    )


def solution(mesh):
    whole = P("gx", "gy", "gz")
    in_specs = (
        whole,
        whole,
        whole,
        P(None, "gx", "gy", "gz"),
        whole,
        P(),
        whole,
        whole,
        P(("gx", "gy", "gz"), None, None),
        P(("gx", "gy", "gz")),
        P(),
    )
    return jax.shard_map(
        body, mesh=mesh, in_specs=in_specs, out_specs=(whole, whole, whole), check_vma=False
    )
```

```python
import functools

import jax
import jax.numpy as jnp
import numpy as np
from jax import lax
from jax.experimental import pallas as pl
from jax.experimental.pallas import tpu as pltpu
from jax.sharding import PartitionSpec as P

HIGH = lax.Precision.HIGHEST
N = 8
E = 10
F32 = jnp.float32


def cheb_matrix():
    count = 8
    points = np.cos(np.pi * np.arange(count) / (count - 1))
    signs = np.array([2.0, 1, 1, 1, 1, 1, 1, 2.0]) * (-1.0) ** np.arange(count)
    differ = points[:, None] - points[None, :] + np.eye(count)
    matrix = np.outer(signs, 1.0 / signs) / differ
    matrix = matrix - np.eye(count) * np.sum(matrix, axis=1)[:, None]
    return (0.25 * matrix).astype(np.float32)


def extended_positions(count):
    length = N * count
    result = []
    for element in range(count):
        for node in [N * element - 2, *range(N * element, N * element + N), N * element + N + 1]:
            result.append(length if node < 0 else length + 1 if node >= length else node)
    return np.array(result)


def inside_positions(count):
    return np.concatenate([np.arange(E * e + 1, E * e + N + 1) for e in range(count)])


def one_hot(index, size):
    return (np.asarray(index)[:, None] == np.arange(size)[None, :]).astype(np.float32)


def up8(count):
    return -(-count // 8) * 8


def mm(a, b, ca=1, cb=0):
    return lax.dot_general(
        a, b, (((ca,), (cb,)), ((), ())), precision=HIGH, preferred_element_type=F32
    )


def halves(a):
    high = a.astype(jnp.bfloat16)
    return high, (a - high.astype(F32)).astype(jnp.bfloat16)


def mm3(a, b):
    (a_high, a_low), (b_high, b_low) = halves(a), halves(b)

    def product(x, y):
        return jnp.dot(x, y, preferred_element_type=F32)

    return product(a_high, b_high) + (product(a_high, b_low) + product(a_low, b_high))


def call(kernel, name, outs, *args, smem=(), load=(), keep=(), scratch=(), pin=(), store=(), idle=(), numbers=()):
    count, n_out, n_keep = len(args), len(outs), len(keep)
    moved = sorted((*load, *keep, *numbers))
    vmem = pl.BlockSpec(memory_space=pltpu.VMEM)

    def whole(*refs):
        inside, results = list(refs[:count]), refs[count : count + n_out]
        kept = refs[count + n_out : count + n_out + n_keep]
        rest = list(refs[count + n_out + n_keep :])
        sems = rest.pop() if moved or store else None
        written = list(results)
        for i in store:
            written[i] = rest.pop()
        copies = {}
        for at, i in enumerate(moved):
            target = kept[keep.index(i)] if i in keep else rest.pop()
            copies[i] = pltpu.make_async_copy(inside[i], target, sems.at[at])
            copies[i].start()
            inside[i] = target
        waiting = dict(copies)

        def ready(*which):
            for i in which:
                if i in waiting:
                    waiting.pop(i).wait()

        kernel(ready, *inside, *written, *rest)
        ready(*moved)
        copies = [
            pltpu.make_async_copy(written[i], results[i], sems.at[len(moved) + at])
            for at, i in enumerate(store)
        ]
        for copy in copies:
            copy.start()
        for copy in copies:
            copy.wait()

    buffers = [
        (pltpu.SMEM if i in numbers else pltpu.VMEM)(args[i].shape, args[i].dtype)
        for i in moved
        if i not in keep
    ]
    specs = []
    for i in range(count):
        space = pltpu.SMEM if i in smem else pltpu.HBM if i in (*moved, *idle) else pltpu.VMEM
        specs.append(pl.BlockSpec(memory_space=space))
    args = [
        pltpu.with_memory_space_constraint(a, pltpu.HBM) if i in (*moved, *idle) else a
        for i, a in enumerate(args)
    ]
    size = sum(int(np.prod(a.shape)) * 4 for a in args) + sum(int(np.prod(o)) * 4 for o in outs)
    return pl.pallas_call(
        whole,
        out_shape=[
            pltpu.VMEM(o, F32)
            if i in pin
            else pltpu.HBM(o, F32)
            if i in store
            else jax.ShapeDtypeStruct(o, F32)
            for i, o in enumerate(outs)
        ]
        + [pltpu.VMEM(args[i].shape, args[i].dtype) for i in keep],
        in_specs=specs,
        out_specs=[
            pl.BlockSpec(memory_space=pltpu.HBM) if i in store else vmem
            for i in range(n_out + n_keep)
        ],
        scratch_shapes=[
            *scratch,
            *buffers[::-1],
            *[pltpu.VMEM(outs[i], F32) for i in store[::-1]],
            *([pltpu.SemaphoreType.DMA((len(moved) + len(store),))] if moved or store else []),
        ],
        cost_estimate=pl.CostEstimate(flops=0, bytes_accessed=size, transcendentals=0),
        compiler_params=pltpu.CompilerParams(vmem_limit_bytes=24 * 2**20),
        name=name,
    )(*args)


def coarse_kernel(ready, blocks, me, residual, ids, values, kept, payload, ids_wide):
    nx, ny, nz = residual.shape
    ex, ey = nx // N, ny // N
    ez = ids.shape[1]
    n_stored, coarse, _ = values.shape
    n_line, head = payload.shape[0], payload.shape[1] - ny
    widen = (
        lax.broadcasted_iota(jnp.int32, (ez, nz), 1) // N
        == lax.broadcasted_iota(jnp.int32, (ez, nz), 0)
    ).astype(F32)
    payload[...] = jnp.zeros_like(payload)
    at = me[0]
    ready(3)
    wide = mm(ids[...].astype(F32), widen)
    ids_wide[...] = wide
    unknown = lax.broadcasted_iota(jnp.int32, (coarse, nz), 0).astype(F32)
    total = jnp.zeros((coarse, nz), F32)
    ready(2)

    @pl.when(at + 1 < n_line)
    def _():
        payload[at + 1, head:, :] = residual[nx - 2]

    @pl.when(at > 0)
    def _():
        payload[at - 1, head:, :] = residual[1]

    for a in range(ex):
        for b in range(ey):
            part = jnp.sum(residual[a * N : a * N + N, b * N : b * N + N, :], axis=(0, 1))[None]
            q = a * ey + b
            total = total + jnp.where(jnp.abs(unknown - wide[q : q + 1]) < 0.5, part, 0.0)
    coarse_residual = jnp.sum(total, axis=1, keepdims=True)
    ready(4)
    ready(0)
    lane = lax.broadcasted_iota(jnp.int32, (1, nz), 1)
    numbers = jnp.zeros((1, nz), F32)
    for k in range(n_stored):
        numbers = jnp.where(lane == n_stored * at + k, blocks[k].astype(F32), numbers)
    row = lax.broadcasted_iota(jnp.int32, (head, nz), 0)
    lines = jnp.where(row == n_stored, numbers, 0.0)
    for k in range(n_stored):
        lines = jnp.where(
            row == k, jnp.sum(values[k] * coarse_residual, axis=0, keepdims=True), lines
        )
    for i in range(n_line):
        payload[i, :head, :] = lines


def line_kernel(
    n_stored, ready, me, parts, residual, after1, after2, dense, x_low, x_high, to_high, to_low
):
    nx, ny, nz = residual.shape
    n_line = parts.shape[0]
    head = parts.shape[1] - ny
    at = me[0]
    rows = parts[:, :n_stored, :].reshape(n_line * n_stored, nz)
    if rows.shape[0] < nz:
        rows = jnp.concatenate([rows, jnp.zeros((nz - rows.shape[0], nz), F32)])
    numbers = jnp.sum(parts[:, n_stored : n_stored + 1, :], axis=0)
    n_blocks = dense.shape[0] * dense.shape[1]
    block = lax.broadcasted_iota(jnp.int32, (n_blocks, nz), 0).astype(F32)
    place = (jnp.abs(block - numbers) < 0.5).astype(F32)
    dense[...] = mm(place, rows).reshape(dense.shape)
    before, behind = jnp.maximum(at - 1, 0), jnp.minimum(at + 1, n_line - 1)
    x_low[...] = jnp.where(at > 0, parts[before, head:, :], 0.0)
    x_high[...] = jnp.where(at + 1 < n_line, parts[behind, head:, :], 0.0)
    for out, y in ((to_high, ny - 2), (to_low, 1)):
        out[...] = jnp.zeros_like(out)
        out[:nx] = residual[:, y, :]
        out[nx : nx + 1] = x_low[y : y + 1]
        out[nx + 1 : nx + 2] = x_high[y : y + 1]


def spread_sum_kernel(ready, parts, after, out):
    total = jnp.sum(parts[...], axis=0)
    for i in range(out.shape[0]):
        out[i] = total


def plane_kernel(
    ready, parts, residual, x_low, x_high, y_low, y_high, owned, every, to_high, to_low
):
    total = jnp.sum(parts[...], axis=0)
    for i in range(owned.shape[0]):
        owned[i] = total
    nx, ny, nz = residual.shape
    at = 0
    for ref in (None, x_low, x_high, y_low, y_high):
        block = residual[...].reshape(nx * ny, nz) if ref is None else ref[...]
        every[at : at + block.shape[0]] = block
        at += block.shape[0]
    row = lax.broadcasted_iota(jnp.int32, (8, nz), 0)
    lane = lax.broadcasted_iota(jnp.int32, (8, nz), 1)
    pick = ((row == 0) & (lane == nz - 2)) | ((row == 1) & (lane == 1))
    ends = mm(pick.astype(F32), every[...], 1, 1)
    to_high[...] = ends[0:1]
    to_low[...] = ends[1:2]


def matrices_kernel(
    ready, basis, tile2, mask2, tilez, maskz, row_x, row_y, col_x, col_y, out_x, out_y, col_z, in_z,
    to_spectral, from_spectral, to_z, from_z,
):
    ready(*range(13))
    flat2 = mm(mm(tile2[...], basis[...]), tile2[...], 1, 1) * mask2[...]
    flatz = mm(mm(tilez[...], basis[...]), tilez[...], 1, 1) * maskz[...]
    to_x = mm(row_x[...], mm(flat2, col_x[...], 0, 0))
    to_y = mm(row_y[...], mm(flat2, col_y[...], 0, 0))
    to_spectral[...] = to_x * to_y
    from_x = mm(mm(out_x[...], flat2), row_x[...], 1, 1)
    from_y = mm(mm(out_y[...], flat2), row_y[...], 1, 1)
    from_spectral[...] = from_x * from_y
    to_z[...] = mm(col_z[...], flatz)
    from_z[...] = mm(flatz, in_z[...], 0, 0)


def spectral_kernel(ready, every, to_spectral, to_z, spectral):
    ready(1, 2)
    spectral[...] = mm3(mm3(to_spectral[...], every[...]), to_z[: every.shape[1], :])


def solve_kernel(
    ready, inside, z_low, z_high, to_spectral, from_spectral, to_z, from_z, sums, local_part,
    inner, wide
):
    n_x, n_y, n_z = sums.shape
    wide[...] = jnp.zeros_like(wide)
    row = lax.broadcasted_iota(jnp.int32, (8, z_low.shape[1]), 0)
    ends = jnp.where(row == 0, z_low[...], jnp.where(row == 1, z_high[...], 0.0))
    ready(3, 5)
    spectral = inside[...] + mm(mm(to_spectral[...], ends, 1, 1), to_z[to_z.shape[0] - 8 :, :])
    ready(7)
    wide[:, :n_y, :] = sums[...]
    weighted = wide[...].reshape(-1, n_z) * spectral
    line = jnp.sum(weighted * spectral, axis=0, keepdims=True)
    wide_line = jnp.concatenate([line, jnp.zeros((1, 256 - n_z), F32)], axis=1)
    inner[...] = folded((wide_line[:, :128] + wide_line[:, 128:])[None])
    ready(4, 6)
    local_part[...] = mm3(mm3(from_spectral[...], weighted), from_z[...])


def derive(matrix, slabs):
    result = []
    for first in range(0, len(slabs), N):
        for i in range(N):
            terms = [float(matrix[i, j]) * slabs[first + j] for j in range(N)]
            while len(terms) > 1:
                terms = [a + b for a, b in zip(terms[::2], terms[1::2])]
            result.append(terms[0])
    return result


def operator(source, conductance, mass, ky, ky_t, kz, kz_t, target):
    nx, ny, nz = source.shape
    rows = nx * ny
    cheb = cheb_matrix()
    flat = source[...].reshape(rows, nz)
    along_y = mm(ky[...], flat) * conductance[1].reshape(rows, nz)
    along_z = mm(flat, kz_t[...]) * conductance[2].reshape(rows, nz)
    along_x = [g * conductance[0, x] for x, g in enumerate(derive(cheb, [source[x] for x in range(nx)]))]
    yz = mm(ky_t[...], along_y) + mm(along_z, kz[...])
    for x, value in enumerate(derive(cheb.T, along_x)):
        target[x] = mass[x] * source[x] + value + yz[x * ny : (x + 1) * ny]


def operator_kernel(ready, direction, conductance, mass, ky, ky_t, kz, kz_t, image, third):
    ready(0, 1, 2, 3, 4, 5, 6)
    operator(direction, conductance, mass, ky, ky_t, kz, kz_t, image)
    third[...] = folded(direction[...] * image[...])


def total_of(values):
    return jnp.sum(jnp.sum(values, axis=0, keepdims=True), axis=1, keepdims=True)


def correct_kernel(
    ready, blocks, coarse_inner, values, ids_wide, local_part, direction, image_direction,
    conductance, mass, ky, ky_t, kz, kz_t,
    z_out, image_out, to_high, to_low,
):
    nx, ny, nz = direction.shape
    rows = nx * ny
    n_stored, coarse, block = values.shape
    total = jnp.zeros((coarse, block), F32)
    for k in range(n_stored):
        total = total + values[k] * coarse_inner[pl.ds(blocks[k], 1), :]
    solution = jnp.sum(total, axis=1, keepdims=True)
    unknown = lax.broadcasted_iota(jnp.int32, (coarse, nz), 0).astype(F32)
    ey = ny // N
    for a in range(nx // N):
        for b in range(ey):
            q = a * ey + b
            hit = jnp.abs(unknown - ids_wide[q : q + 1, :]) < 0.5
            line = jnp.sum(jnp.where(hit, solution, 0.0), axis=0, keepdims=True)
            for x in range(N):
                at = (a * N + x) * ny + b * N
                z_out[a * N + x, b * N : b * N + N, :] = local_part[at : at + N, :] + line
    operator(z_out, conductance, mass, ky, ky_t, kz, kz_t, image_out)
    for out, x in ((to_high, nx - 1), (to_low, 0)):
        out[0, :ny] = image_out[x]
        out[1, :ny] = image_direction[x]


def folded(values):
    line = jnp.sum(jnp.sum(values, axis=0), axis=0, keepdims=True)
    line = line + pltpu.roll(line, 64, 1)
    return line + pltpu.roll(line, 32, 1)


def terms_kernel(ready, z, image, direction, image_direction, inner_local, third, after, terms):
    first = folded(z[...] * image[...])
    second = folded(z[...] * image_direction[...] + direction[...] * image[...])
    group = lax.broadcasted_iota(jnp.int32, (1, terms.shape[2]), 1) // 32
    line = jnp.where(group == 0, inner_local[...], third[...])
    line = jnp.where(group == 1, first, jnp.where(group == 2, second, line))
    for i in range(terms.shape[0]):
        terms[i] = line


def assemble_length_kernel(
    ready, image, image_direction, low, high, coarse_inner, out, to_high, to_low, square
):
    square[...] = total_of(coarse_inner[...] * coarse_inner[...])
    nx, ny, nz = image.shape
    for i, ref in ((0, image), (1, image_direction)):
        out[i] = ref[...]
        for x in range(nx):
            if x % N == N - 1:
                out[i, x] = ref[x] + (ref[x + 1] if x + 1 < nx else high[i, :ny])
            elif x % N == 0:
                out[i, x] = ref[x] + (ref[x - 1] if x else low[i, :ny])
        to_high[i, :nx] = out[i, :, ny - 1, :]
        to_low[i, :nx] = out[i, :, 0, :]


def assemble_across_kernel(ready, images, low, high, solution, out, to_high, to_low):
    _, nx, ny, nz = images.shape
    out[...] = images[...]
    for i in range(2):
        for y in range(ny):
            if y % N == N - 1:
                other = images[i, :, y + 1, :] if y + 1 < ny else high[i, :nx]
            elif y % N == 0:
                other = images[i, :, y - 1, :] if y else low[i, :nx]
            else:
                continue
            out[i, :, y, :] = images[i, :, y, :] + other
    row = lax.broadcasted_iota(jnp.int32, (8, nz), 0)
    lane = lax.broadcasted_iota(jnp.int32, (8, nz), 1)
    pick = ((row == 0) & (lane == nz - 1)) | ((row == 1) & (lane == 0))
    ends = mm(pick.astype(F32), out[...].reshape(2 * nx * ny, nz), 1, 1)
    to_high[...] = ends[0:1]
    to_low[...] = ends[1:2]


def assemble_depth_kernel(ready, images, low, high, out):
    _, nx, ny, nz = images.shape
    rows = 2 * nx * ny
    image = images[...].reshape(rows, nz)
    row = lax.broadcasted_iota(jnp.int32, (8, rows), 0)
    ends = jnp.where(row == 0, low[...], jnp.where(row == 1, high[...], 0.0))
    row = lax.broadcasted_iota(jnp.int32, (8, nz), 0)
    lane = lax.broadcasted_iota(jnp.int32, (8, nz), 1)
    place = ((row == 0) & (lane == 0)) | ((row == 1) & (lane == nz - 1))
    outer = mm(jnp.transpose(ends), place.astype(F32))
    lane = lax.broadcasted_iota(jnp.int32, (rows, nz), 1)
    above = jnp.where((lane % N == N - 1) & (lane < nz - 1), pltpu.roll(image, nz - 1, 1), 0.0)
    below = jnp.where((lane % N == 0) & (lane > 0), pltpu.roll(image, 1, 1), 0.0)
    out[...] = (image + above + below + outer).reshape(out.shape)


def update_kernel(
    ready, prior, terms, square, images, residual, solution, direction, z,
    new_solution, new_residual, new_direction,
):
    lane = lax.broadcasted_iota(jnp.int32, (1, terms.shape[2]), 1)
    sums = jnp.sum(terms[...], axis=0)

    def term(i):
        return jnp.sum(jnp.where(lane // 32 == i, sums, 0.0), axis=1, keepdims=True)

    inner = term(0) + square[...]
    ratio = inner / prior[0]
    alpha = inner / (term(1) + ratio * term(2) + ratio * ratio * term(3))
    ratio, alpha = ratio[None], alpha[None]
    new = z[...] + ratio * direction[...]
    new_direction[...] = new
    new_solution[...] = solution[...] + alpha * new
    new_residual[...] = residual[...] - alpha * (images[0] + ratio * images[1])


def shifts(axis):
    count = lax.axis_size(axis)
    forward = [(i, i + 1) for i in range(count - 1)]
    return forward, [(b, a) for a, b in forward]


def exchange(to_high, to_low, axis):
    forward, backward = shifts(axis)
    return lax.ppermute(to_high, axis, forward), lax.ppermute(to_low, axis, backward)


def spread(values, axes):
    return lax.all_to_all(values, axes, 0, 0, tiled=False)


def body(
    residual,
    solution,
    direction,
    conductance,
    mass_term,
    eigen_basis,
    inverse_eigen_sums,
    element_coarse_index,
    xxt_values,
    xxt_blocks,
    prior_inner,
):
    nx, ny, nz = residual.shape
    ex, ey, ez = nx // N, ny // N, nz // N
    rows = nx * ny
    plane = ("gy", "gz")
    n_plane, n_line = lax.axis_size(plane), lax.axis_size("gx")
    coarse_count, block = xxt_values.shape[1:]
    n_blocks = coarse_count * n_plane * n_line // block
    own = n_blocks // n_plane

    ids = element_coarse_index.reshape(ex * ey, ez)
    me = lax.axis_index("gx").astype(jnp.int32).reshape(1)
    head = up8(xxt_values.shape[0] + 1)
    assert xxt_values.shape[0] * n_line <= nz
    payload, ids_wide, residual, xxt_values, block_numbers = call(
        coarse_kernel, "coarse_restrict", [(n_line, head + ny, nz), (ex * ey, nz)],
        xxt_blocks, me, residual, ids, xxt_values, xxt_blocks, smem=(1,), load=(3,), keep=(2, 4, 5),
        pin=(1,),
        numbers=(0,),
    )
    parts = spread(payload, "gx")

    cheb = cheb_matrix()
    ky = np.kron(np.eye(nx, dtype=np.float32), np.kron(np.eye(ey, dtype=np.float32), cheb))
    kz = np.kron(np.eye(ez, dtype=np.float32), cheb)
    tables = [jnp.asarray(np.ascontiguousarray(t)) for t in (ky, ky.T, kz, kz.T)]
    image_direction, third, direction, conductance, mass_term, *tables = call(
        operator_kernel, "operator_direction", [direction.shape, (1, nz)],
        direction, conductance, mass_term, *tables, keep=tuple(range(7)), pin=(0, 1),
    )

    face = up8(nx + 2)
    n_every = rows + 2 * ny + 2 * face
    pad = [-1] * (face - nx - 2)
    line = [*range(nx), nx, nx + 1, *pad]
    cols_x = np.array([*np.repeat(np.arange(nx), ny), *[nx] * ny, *[nx + 1] * ny, *line, *line])
    cols_y = np.array(
        [*np.tile(np.arange(ny), nx), *range(ny), *range(ny), *[ny] * face, *[ny + 1] * face]
    )
    n_x, n_y, n_z = inverse_eigen_sums.shape
    high_y = up8(n_y)
    place_y = np.tile(np.arange(high_y), n_x)
    row_x = one_hot(np.repeat(np.arange(n_x), high_y), n_x) * (place_y < n_y)[:, None]
    row_y = one_hot(place_y, n_y)
    col_x = (extended_positions(ex)[:, None] == cols_x[None, :]).astype(np.float32)
    col_y = (extended_positions(ey)[:, None] == cols_y[None, :]).astype(np.float32)
    assert ex == ey
    to_spectral, from_spectral, to_z, from_z = call(
        matrices_kernel, "basis_matrices",
        [(n_x * high_y, n_every), (rows, n_x * high_y), (nz + 8, n_z), (n_z, nz)],
        eigen_basis,
        *map(
            jnp.asarray,
            (
                np.tile(np.eye(E, dtype=np.float32), (ex, 1)),
                np.kron(np.eye(ex), np.ones((E, E))).astype(np.float32),
                np.tile(np.eye(E, dtype=np.float32), (ez, 1)),
                np.kron(np.eye(ez), np.ones((E, E))).astype(np.float32),
                row_x.astype(np.float32),
                row_y,
                col_x,
                col_y,
                one_hot(np.repeat(inside_positions(ex), ny), n_x),
                one_hot(np.tile(inside_positions(ey), nx), n_y),
                np.ascontiguousarray(one_hot(extended_positions(ez), nz + 8).T),
                np.ascontiguousarray(one_hot(inside_positions(ez), n_z).T),
            ),
        ),
        load=tuple(range(13)), store=(0, 1, 2, 3),
    )

    dense, x_low, x_high, to_high, to_low = call(
        functools.partial(line_kernel, xxt_values.shape[0]), "line_sum",
        [(n_plane, own, block), (ny, nz), (ny, nz), (face, nz), (face, nz)],
        me, parts, residual, image_direction, from_z, smem=(0,), pin=(1, 2), idle=(4,),
    )
    parts = spread(dense, plane)
    y_low, y_high = exchange(to_high, to_low, "gy")
    owned, every, to_high, to_low = call(
        plane_kernel, "plane_sum",
        [(n_plane, own, block), (n_every, nz), (1, n_every), (1, n_every)],
        parts, residual, x_low, x_high, y_low, y_high, pin=(1,),
    )
    coarse_inner = spread(owned, plane).reshape(n_blocks, block)
    z_low, z_high = exchange(to_high, to_low, "gz")
    (spectral,) = call(
        spectral_kernel, "element_spectral", [(n_x * high_y, n_z)],
        every, to_spectral, to_z, load=(1, 2), pin=(0,),
    )
    local_part, inner_local = call(
        solve_kernel, "element_solve", [(rows, nz), (1, nz)],
        spectral, z_low, z_high, to_spectral, from_spectral, to_z, from_z, inverse_eigen_sums,
        load=(3, 4, 5, 6, 7), pin=(0, 1), scratch=(pltpu.VMEM((n_x, high_y, n_z), F32),),
    )

    z, image, to_high, to_low = call(
        correct_kernel, "coarse_correct",
        [direction.shape, direction.shape, (2, 4 * ny, nz), (2, 4 * ny, nz)],
        block_numbers, coarse_inner, xxt_values, ids_wide, local_part, direction,
        image_direction, conductance, mass_term, *tables, smem=(0,), pin=(0, 1),
    )
    low, high = exchange(to_high, to_low, "gx")
    (terms,) = call(
        terms_kernel, "terms", [(n_plane, 1, nz)],
        z, image, direction, image_direction, inner_local, third, low,
    )
    parts = spread(terms, plane)
    images, to_high, to_low, square = call(
        assemble_length_kernel, "assemble_length",
        [(2, nx, ny, nz), (2, 2 * nx, nz), (2, 2 * nx, nz), (1, 1)],
        image, image_direction, low, high, coarse_inner, pin=(0, 3),
    )
    low, high = exchange(to_high, to_low, "gy")
    (terms,) = call(spread_sum_kernel, "sum_terms", [(n_line, 1, nz)], parts, low)
    parts = spread(terms, "gx")
    images, to_high, to_low, solution = call(
        assemble_across_kernel, "assemble_across", [(2, nx, ny, nz), (1, 2 * rows), (1, 2 * rows)],
        images, low, high, solution, keep=(3,), pin=(0,),
    )
    low, high = exchange(to_high, to_low, "gz")
    (images,) = call(
        assemble_depth_kernel, "assemble_depth", [images.shape], images, low, high, pin=(0,)
    )
    return tuple(
        call(
            update_kernel, "update", [direction.shape] * 3,
            prior_inner, parts, square, images, residual, solution, direction, z, smem=(0,),
        )
    )


def solution(mesh):
    whole = P("gx", "gy", "gz")
    in_specs = (
        whole,
        whole,
        whole,
        P(None, "gx", "gy", "gz"),
        whole,
        P(),
        whole,
        whole,
        P(("gx", "gy", "gz"), None, None),
        P(("gx", "gy", "gz")),
        P(),
    )
    return jax.shard_map(
        body, mesh=mesh, in_specs=in_specs, out_specs=(whole, whole, whole), check_vma=False
    )
```

```python
import functools

import jax
import jax.numpy as jnp
import numpy as np
from jax import lax
from jax.experimental import pallas as pl
from jax.experimental.pallas import tpu as pltpu
from jax.sharding import PartitionSpec as P

HIGH = lax.Precision.HIGHEST
N = 8
E = 10
F32 = jnp.float32


def cheb_matrix():
    count = 8
    points = np.cos(np.pi * np.arange(count) / (count - 1))
    signs = np.array([2.0, 1, 1, 1, 1, 1, 1, 2.0]) * (-1.0) ** np.arange(count)
    differ = points[:, None] - points[None, :] + np.eye(count)
    matrix = np.outer(signs, 1.0 / signs) / differ
    matrix = matrix - np.eye(count) * np.sum(matrix, axis=1)[:, None]
    return (0.25 * matrix).astype(np.float32)


def extended_positions(count):
    length = N * count
    result = []
    for element in range(count):
        for node in [N * element - 2, *range(N * element, N * element + N), N * element + N + 1]:
            result.append(length if node < 0 else length + 1 if node >= length else node)
    return np.array(result)


def inside_positions(count):
    return np.concatenate([np.arange(E * e + 1, E * e + N + 1) for e in range(count)])


def one_hot(index, size):
    return (np.asarray(index)[:, None] == np.arange(size)[None, :]).astype(np.float32)


def up8(count):
    return -(-count // 8) * 8


def mm(a, b, ca=1, cb=0):
    return lax.dot_general(
        a, b, (((ca,), (cb,)), ((), ())), precision=HIGH, preferred_element_type=F32
    )


def halves(a):
    high = a.astype(jnp.bfloat16)
    return high, (a - high.astype(F32)).astype(jnp.bfloat16)


def mm3(a, b):
    (a_high, a_low), (b_high, b_low) = halves(a), halves(b)

    def product(x, y):
        return jnp.dot(x, y, preferred_element_type=F32)

    return product(a_high, b_high) + (product(a_high, b_low) + product(a_low, b_high))


def call(kernel, name, outs, *args, smem=(), load=(), keep=(), scratch=(), pin=(), store=(), idle=(), numbers=()):
    count, n_out, n_keep = len(args), len(outs), len(keep)
    moved = sorted((*load, *keep, *numbers))
    vmem = pl.BlockSpec(memory_space=pltpu.VMEM)

    def whole(*refs):
        inside, results = list(refs[:count]), refs[count : count + n_out]
        kept = refs[count + n_out : count + n_out + n_keep]
        rest = list(refs[count + n_out + n_keep :])
        sems = rest.pop() if moved or store else None
        written = list(results)
        for i in store:
            written[i] = rest.pop()
        copies = {}
        for at, i in enumerate(moved):
            target = kept[keep.index(i)] if i in keep else rest.pop()
            copies[i] = pltpu.make_async_copy(inside[i], target, sems.at[at])
            copies[i].start()
            inside[i] = target
        waiting = dict(copies)

        def ready(*which):
            for i in which:
                if i in waiting:
                    waiting.pop(i).wait()

        kernel(ready, *inside, *written, *rest)
        ready(*moved)
        copies = [
            pltpu.make_async_copy(written[i], results[i], sems.at[len(moved) + at])
            for at, i in enumerate(store)
        ]
        for copy in copies:
            copy.start()
        for copy in copies:
            copy.wait()

    buffers = [
        (pltpu.SMEM if i in numbers else pltpu.VMEM)(args[i].shape, args[i].dtype)
        for i in moved
        if i not in keep
    ]
    specs = []
    for i in range(count):
        space = pltpu.SMEM if i in smem else pltpu.HBM if i in (*moved, *idle) else pltpu.VMEM
        specs.append(pl.BlockSpec(memory_space=space))
    args = [
        pltpu.with_memory_space_constraint(a, pltpu.HBM) if i in (*moved, *idle) else a
        for i, a in enumerate(args)
    ]
    size = sum(int(np.prod(a.shape)) * 4 for a in args) + sum(int(np.prod(o)) * 4 for o in outs)
    return pl.pallas_call(
        whole,
        out_shape=[
            pltpu.VMEM(o, F32)
            if i in pin
            else pltpu.HBM(o, F32)
            if i in store
            else jax.ShapeDtypeStruct(o, F32)
            for i, o in enumerate(outs)
        ]
        + [pltpu.VMEM(args[i].shape, args[i].dtype) for i in keep],
        in_specs=specs,
        out_specs=[
            pl.BlockSpec(memory_space=pltpu.HBM) if i in store else vmem
            for i in range(n_out + n_keep)
        ],
        scratch_shapes=[
            *scratch,
            *buffers[::-1],
            *[pltpu.VMEM(outs[i], F32) for i in store[::-1]],
            *([pltpu.SemaphoreType.DMA((len(moved) + len(store),))] if moved or store else []),
        ],
        cost_estimate=pl.CostEstimate(flops=0, bytes_accessed=size, transcendentals=0),
        compiler_params=pltpu.CompilerParams(vmem_limit_bytes=24 * 2**20),
        name=name,
    )(*args)


def coarse_kernel(ready, blocks, me, residual, ids, values, kept, payload, ids_wide, to_high, to_low):
    nx, ny, nz = residual.shape
    ex, ey = nx // N, ny // N
    ez = ids.shape[1]
    n_stored, coarse, _ = values.shape
    n_line, head = payload.shape[:2]
    widen = (
        lax.broadcasted_iota(jnp.int32, (ez, nz), 1) // N
        == lax.broadcasted_iota(jnp.int32, (ez, nz), 0)
    ).astype(F32)
    at = me[0]
    ready(3)
    wide = mm(ids[...].astype(F32), widen)
    ids_wide[...] = wide
    unknown = lax.broadcasted_iota(jnp.int32, (coarse, nz), 0).astype(F32)
    total = jnp.zeros((coarse, nz), F32)
    ready(2)

    to_high[...] = residual[nx - 2]
    to_low[...] = residual[1]
    for a in range(ex):
        for b in range(ey):
            part = jnp.sum(residual[a * N : a * N + N, b * N : b * N + N, :], axis=(0, 1))[None]
            q = a * ey + b
            total = total + jnp.where(jnp.abs(unknown - wide[q : q + 1]) < 0.5, part, 0.0)
    coarse_residual = jnp.sum(total, axis=1, keepdims=True)
    ready(4)
    ready(0)
    lane = lax.broadcasted_iota(jnp.int32, (1, nz), 1)
    numbers = jnp.zeros((1, nz), F32)
    for k in range(n_stored):
        numbers = jnp.where(lane == n_stored * at + k, blocks[k].astype(F32), numbers)
    row = lax.broadcasted_iota(jnp.int32, (head, nz), 0)
    lines = jnp.where(row == n_stored, numbers, 0.0)
    for k in range(n_stored):
        lines = jnp.where(
            row == k, jnp.sum(values[k] * coarse_residual, axis=0, keepdims=True), lines
        )
    for i in range(n_line):
        payload[i] = lines


def line_kernel(
    n_stored, ready, parts, residual, x_low, x_high, after1, after2, dense, to_high, to_low
):
    nx, ny, nz = residual.shape
    n_line = parts.shape[0]
    rows = parts[:, :n_stored, :].reshape(n_line * n_stored, nz)
    if rows.shape[0] < nz:
        rows = jnp.concatenate([rows, jnp.zeros((nz - rows.shape[0], nz), F32)])
    numbers = jnp.sum(parts[:, n_stored : n_stored + 1, :], axis=0)
    n_blocks = dense.shape[0] * dense.shape[1]
    block = lax.broadcasted_iota(jnp.int32, (n_blocks, nz), 0).astype(F32)
    place = (jnp.abs(block - numbers) < 0.5).astype(F32)
    dense[...] = mm(place, rows).reshape(dense.shape)
    for out, y in ((to_high, ny - 2), (to_low, 1)):
        out[...] = jnp.zeros_like(out)
        out[:nx] = residual[:, y, :]
        out[nx : nx + 1] = x_low[y : y + 1]
        out[nx + 1 : nx + 2] = x_high[y : y + 1]


def spread_sum_kernel(ready, parts, after, out):
    total = jnp.sum(parts[...], axis=0)
    for i in range(out.shape[0]):
        out[i] = total


def plane_kernel(
    ready, parts, residual, x_low, x_high, y_low, y_high, owned, every, to_high, to_low
):
    total = jnp.sum(parts[...], axis=0)
    for i in range(owned.shape[0]):
        owned[i] = total
    nx, ny, nz = residual.shape
    at = 0
    for ref in (None, x_low, x_high, y_low, y_high):
        block = residual[...].reshape(nx * ny, nz) if ref is None else ref[...]
        every[at : at + block.shape[0]] = block
        at += block.shape[0]
    row = lax.broadcasted_iota(jnp.int32, (8, nz), 0)
    lane = lax.broadcasted_iota(jnp.int32, (8, nz), 1)
    pick = ((row == 0) & (lane == nz - 2)) | ((row == 1) & (lane == 1))
    ends = mm(pick.astype(F32), every[...], 1, 1)
    to_high[...] = ends[0:1]
    to_low[...] = ends[1:2]


def matrices_kernel(
    ready, basis, tile2, mask2, tilez, maskz, row_x, row_y, col_x, col_y, out_x, out_y, col_z, in_z,
    to_spectral, from_spectral, to_z, from_z,
):
    ready(*range(13))
    flat2 = mm(mm(tile2[...], basis[...]), tile2[...], 1, 1) * mask2[...]
    flatz = mm(mm(tilez[...], basis[...]), tilez[...], 1, 1) * maskz[...]
    to_x = mm(row_x[...], mm(flat2, col_x[...], 0, 0))
    to_y = mm(row_y[...], mm(flat2, col_y[...], 0, 0))
    to_spectral[...] = to_x * to_y
    from_x = mm(mm(out_x[...], flat2), row_x[...], 1, 1)
    from_y = mm(mm(out_y[...], flat2), row_y[...], 1, 1)
    from_spectral[...] = from_x * from_y
    to_z[...] = mm(col_z[...], flatz)
    from_z[...] = mm(flatz, in_z[...], 0, 0)


def spectral_kernel(ready, every, to_spectral, to_z, spectral):
    ready(1, 2)
    spectral[...] = mm3(mm3(to_spectral[...], every[...]), to_z[: every.shape[1], :])


def solve_kernel(
    ready, inside, z_low, z_high, to_spectral, from_spectral, to_z, from_z, sums, local_part,
    inner, wide
):
    n_x, n_y, n_z = sums.shape
    wide[...] = jnp.zeros_like(wide)
    row = lax.broadcasted_iota(jnp.int32, (8, z_low.shape[1]), 0)
    ends = jnp.where(row == 0, z_low[...], jnp.where(row == 1, z_high[...], 0.0))
    ready(3, 5)
    spectral = inside[...] + mm(mm(to_spectral[...], ends, 1, 1), to_z[to_z.shape[0] - 8 :, :])
    ready(7)
    wide[:, :n_y, :] = sums[...]
    weighted = wide[...].reshape(-1, n_z) * spectral
    line = jnp.sum(weighted * spectral, axis=0, keepdims=True)
    wide_line = jnp.concatenate([line, jnp.zeros((1, 256 - n_z), F32)], axis=1)
    inner[...] = folded((wide_line[:, :128] + wide_line[:, 128:])[None])
    ready(4, 6)
    local_part[...] = mm3(mm3(from_spectral[...], weighted), from_z[...])


def derive(matrix, slabs):
    result = []
    for first in range(0, len(slabs), N):
        for i in range(N):
            terms = [float(matrix[i, j]) * slabs[first + j] for j in range(N)]
            while len(terms) > 1:
                terms = [a + b for a, b in zip(terms[::2], terms[1::2])]
            result.append(terms[0])
    return result


def operator(source, conductance, mass, ky, ky_t, kz, kz_t, target):
    nx, ny, nz = source.shape
    rows = nx * ny
    cheb = cheb_matrix()
    flat = source[...].reshape(rows, nz)
    along_y = mm(ky[...], flat) * conductance[1].reshape(rows, nz)
    along_z = mm(flat, kz_t[...]) * conductance[2].reshape(rows, nz)
    along_x = [g * conductance[0, x] for x, g in enumerate(derive(cheb, [source[x] for x in range(nx)]))]
    yz = mm(ky_t[...], along_y) + mm(along_z, kz[...])
    for x, value in enumerate(derive(cheb.T, along_x)):
        target[x] = mass[x] * source[x] + value + yz[x * ny : (x + 1) * ny]


def operator_kernel(ready, direction, conductance, mass, ky, ky_t, kz, kz_t, image, third):
    ready(0, 1, 2, 3, 4, 5, 6)
    operator(direction, conductance, mass, ky, ky_t, kz, kz_t, image)
    third[...] = folded(direction[...] * image[...])


def total_of(values):
    return jnp.sum(jnp.sum(values, axis=0, keepdims=True), axis=1, keepdims=True)


def correct_kernel(
    ready, blocks, coarse_inner, values, ids_wide, local_part, direction, image_direction,
    conductance, mass, ky, ky_t, kz, kz_t,
    z_out, image_out, to_high, to_low,
):
    nx, ny, nz = direction.shape
    rows = nx * ny
    n_stored, coarse, block = values.shape
    total = jnp.zeros((coarse, block), F32)
    for k in range(n_stored):
        total = total + values[k] * coarse_inner[pl.ds(blocks[k], 1), :]
    solution = jnp.sum(total, axis=1, keepdims=True)
    unknown = lax.broadcasted_iota(jnp.int32, (coarse, nz), 0).astype(F32)
    ey = ny // N
    for a in range(nx // N):
        for b in range(ey):
            q = a * ey + b
            hit = jnp.abs(unknown - ids_wide[q : q + 1, :]) < 0.5
            line = jnp.sum(jnp.where(hit, solution, 0.0), axis=0, keepdims=True)
            for x in range(N):
                at = (a * N + x) * ny + b * N
                z_out[a * N + x, b * N : b * N + N, :] = local_part[at : at + N, :] + line
    operator(z_out, conductance, mass, ky, ky_t, kz, kz_t, image_out)
    for out, x in ((to_high, nx - 1), (to_low, 0)):
        out[0, :ny] = image_out[x]
        out[1, :ny] = image_direction[x]


def folded(values):
    line = jnp.sum(jnp.sum(values, axis=0), axis=0, keepdims=True)
    line = line + pltpu.roll(line, 64, 1)
    return line + pltpu.roll(line, 32, 1)


def terms_kernel(ready, z, image, direction, image_direction, inner_local, third, after, terms):
    first = folded(z[...] * image[...])
    second = folded(z[...] * image_direction[...] + direction[...] * image[...])
    group = lax.broadcasted_iota(jnp.int32, (1, terms.shape[2]), 1) // 32
    line = jnp.where(group == 0, inner_local[...], third[...])
    line = jnp.where(group == 1, first, jnp.where(group == 2, second, line))
    for i in range(terms.shape[0]):
        terms[i] = line


def assemble_length_kernel(
    ready, image, image_direction, low, high, coarse_inner, out, to_high, to_low, square
):
    square[...] = total_of(coarse_inner[...] * coarse_inner[...])
    nx, ny, nz = image.shape
    for i, ref in ((0, image), (1, image_direction)):
        out[i] = ref[...]
        for x in range(nx):
            if x % N == N - 1:
                out[i, x] = ref[x] + (ref[x + 1] if x + 1 < nx else high[i, :ny])
            elif x % N == 0:
                out[i, x] = ref[x] + (ref[x - 1] if x else low[i, :ny])
        to_high[i, :nx] = out[i, :, ny - 1, :]
        to_low[i, :nx] = out[i, :, 0, :]


def assemble_across_kernel(ready, images, low, high, solution, out, to_high, to_low):
    _, nx, ny, nz = images.shape
    out[...] = images[...]
    for i in range(2):
        for y in range(ny):
            if y % N == N - 1:
                other = images[i, :, y + 1, :] if y + 1 < ny else high[i, :nx]
            elif y % N == 0:
                other = images[i, :, y - 1, :] if y else low[i, :nx]
            else:
                continue
            out[i, :, y, :] = images[i, :, y, :] + other
    row = lax.broadcasted_iota(jnp.int32, (8, nz), 0)
    lane = lax.broadcasted_iota(jnp.int32, (8, nz), 1)
    pick = ((row == 0) & (lane == nz - 1)) | ((row == 1) & (lane == 0))
    ends = mm(pick.astype(F32), out[...].reshape(2 * nx * ny, nz), 1, 1)
    to_high[...] = ends[0:1]
    to_low[...] = ends[1:2]


def assemble_depth_kernel(ready, images, low, high, out):
    _, nx, ny, nz = images.shape
    rows = 2 * nx * ny
    image = images[...].reshape(rows, nz)
    row = lax.broadcasted_iota(jnp.int32, (8, rows), 0)
    ends = jnp.where(row == 0, low[...], jnp.where(row == 1, high[...], 0.0))
    row = lax.broadcasted_iota(jnp.int32, (8, nz), 0)
    lane = lax.broadcasted_iota(jnp.int32, (8, nz), 1)
    place = ((row == 0) & (lane == 0)) | ((row == 1) & (lane == nz - 1))
    outer = mm(jnp.transpose(ends), place.astype(F32))
    lane = lax.broadcasted_iota(jnp.int32, (rows, nz), 1)
    above = jnp.where((lane % N == N - 1) & (lane < nz - 1), pltpu.roll(image, nz - 1, 1), 0.0)
    below = jnp.where((lane % N == 0) & (lane > 0), pltpu.roll(image, 1, 1), 0.0)
    out[...] = (image + above + below + outer).reshape(out.shape)


def update_kernel(
    ready, prior, terms, square, images, residual, solution, direction, z,
    new_solution, new_residual, new_direction,
):
    lane = lax.broadcasted_iota(jnp.int32, (1, terms.shape[2]), 1)
    sums = jnp.sum(terms[...], axis=0)

    def term(i):
        return jnp.sum(jnp.where(lane // 32 == i, sums, 0.0), axis=1, keepdims=True)

    inner = term(0) + square[...]
    ratio = inner / prior[0]
    alpha = inner / (term(1) + ratio * term(2) + ratio * ratio * term(3))
    ratio, alpha = ratio[None], alpha[None]
    new = z[...] + ratio * direction[...]
    new_direction[...] = new
    new_solution[...] = solution[...] + alpha * new
    new_residual[...] = residual[...] - alpha * (images[0] + ratio * images[1])


def shifts(axis):
    count = lax.axis_size(axis)
    forward = [(i, i + 1) for i in range(count - 1)]
    return forward, [(b, a) for a, b in forward]


def exchange(to_high, to_low, axis):
    forward, backward = shifts(axis)
    return lax.ppermute(to_high, axis, forward), lax.ppermute(to_low, axis, backward)


def spread(values, axes):
    return lax.all_to_all(values, axes, 0, 0, tiled=False)


def body(
    residual,
    solution,
    direction,
    conductance,
    mass_term,
    eigen_basis,
    inverse_eigen_sums,
    element_coarse_index,
    xxt_values,
    xxt_blocks,
    prior_inner,
):
    nx, ny, nz = residual.shape
    ex, ey, ez = nx // N, ny // N, nz // N
    rows = nx * ny
    plane = ("gy", "gz")
    n_plane, n_line = lax.axis_size(plane), lax.axis_size("gx")
    coarse_count, block = xxt_values.shape[1:]
    n_blocks = coarse_count * n_plane * n_line // block
    own = n_blocks // n_plane

    ids = element_coarse_index.reshape(ex * ey, ez)
    me = lax.axis_index("gx").astype(jnp.int32).reshape(1)
    head = up8(xxt_values.shape[0] + 1)
    assert xxt_values.shape[0] * n_line <= nz
    payload, ids_wide, to_high, to_low, residual, xxt_values, block_numbers = call(
        coarse_kernel, "coarse_restrict",
        [(n_line, head, nz), (ex * ey, nz), (ny, nz), (ny, nz)],
        xxt_blocks, me, residual, ids, xxt_values, xxt_blocks, smem=(1,), load=(3,), keep=(2, 4, 5),
        pin=(1,),
        numbers=(0,),
    )
    parts = spread(payload, "gx")
    x_low, x_high = exchange(to_high, to_low, "gx")

    cheb = cheb_matrix()
    ky = np.kron(np.eye(nx, dtype=np.float32), np.kron(np.eye(ey, dtype=np.float32), cheb))
    kz = np.kron(np.eye(ez, dtype=np.float32), cheb)
    tables = [jnp.asarray(np.ascontiguousarray(t)) for t in (ky, ky.T, kz, kz.T)]
    image_direction, third, direction, conductance, mass_term, *tables = call(
        operator_kernel, "operator_direction", [direction.shape, (1, nz)],
        direction, conductance, mass_term, *tables, keep=tuple(range(7)), pin=(0, 1),
    )

    face = up8(nx + 2)
    n_every = rows + 2 * ny + 2 * face
    pad = [-1] * (face - nx - 2)
    line = [*range(nx), nx, nx + 1, *pad]
    cols_x = np.array([*np.repeat(np.arange(nx), ny), *[nx] * ny, *[nx + 1] * ny, *line, *line])
    cols_y = np.array(
        [*np.tile(np.arange(ny), nx), *range(ny), *range(ny), *[ny] * face, *[ny + 1] * face]
    )
    n_x, n_y, n_z = inverse_eigen_sums.shape
    high_y = up8(n_y)
    place_y = np.tile(np.arange(high_y), n_x)
    row_x = one_hot(np.repeat(np.arange(n_x), high_y), n_x) * (place_y < n_y)[:, None]
    row_y = one_hot(place_y, n_y)
    col_x = (extended_positions(ex)[:, None] == cols_x[None, :]).astype(np.float32)
    col_y = (extended_positions(ey)[:, None] == cols_y[None, :]).astype(np.float32)
    assert ex == ey
    to_spectral, from_spectral, to_z, from_z = call(
        matrices_kernel, "basis_matrices",
        [(n_x * high_y, n_every), (rows, n_x * high_y), (nz + 8, n_z), (n_z, nz)],
        eigen_basis,
        *map(
            jnp.asarray,
            (
                np.tile(np.eye(E, dtype=np.float32), (ex, 1)),
                np.kron(np.eye(ex), np.ones((E, E))).astype(np.float32),
                np.tile(np.eye(E, dtype=np.float32), (ez, 1)),
                np.kron(np.eye(ez), np.ones((E, E))).astype(np.float32),
                row_x.astype(np.float32),
                row_y,
                col_x,
                col_y,
                one_hot(np.repeat(inside_positions(ex), ny), n_x),
                one_hot(np.tile(inside_positions(ey), nx), n_y),
                np.ascontiguousarray(one_hot(extended_positions(ez), nz + 8).T),
                np.ascontiguousarray(one_hot(inside_positions(ez), n_z).T),
            ),
        ),
        load=tuple(range(13)), store=(0, 1, 2, 3),
    )

    dense, to_high, to_low = call(
        functools.partial(line_kernel, xxt_values.shape[0]), "line_sum",
        [(n_plane, own, block), (face, nz), (face, nz)],
        parts, residual, x_low, x_high, image_direction, from_z, idle=(5,),
    )
    parts = spread(dense, plane)
    y_low, y_high = exchange(to_high, to_low, "gy")
    owned, every, to_high, to_low = call(
        plane_kernel, "plane_sum",
        [(n_plane, own, block), (n_every, nz), (1, n_every), (1, n_every)],
        parts, residual, x_low, x_high, y_low, y_high, pin=(1,),
    )
    coarse_inner = spread(owned, plane).reshape(n_blocks, block)
    z_low, z_high = exchange(to_high, to_low, "gz")
    (spectral,) = call(
        spectral_kernel, "element_spectral", [(n_x * high_y, n_z)],
        every, to_spectral, to_z, load=(1, 2), pin=(0,),
    )
    local_part, inner_local = call(
        solve_kernel, "element_solve", [(rows, nz), (1, nz)],
        spectral, z_low, z_high, to_spectral, from_spectral, to_z, from_z, inverse_eigen_sums,
        load=(3, 4, 5, 6, 7), pin=(0, 1), scratch=(pltpu.VMEM((n_x, high_y, n_z), F32),),
    )

    z, image, to_high, to_low = call(
        correct_kernel, "coarse_correct",
        [direction.shape, direction.shape, (2, 4 * ny, nz), (2, 4 * ny, nz)],
        block_numbers, coarse_inner, xxt_values, ids_wide, local_part, direction,
        image_direction, conductance, mass_term, *tables, smem=(0,), pin=(0, 1),
    )
    low, high = exchange(to_high, to_low, "gx")
    (terms,) = call(
        terms_kernel, "terms", [(n_plane, 1, nz)],
        z, image, direction, image_direction, inner_local, third, low,
    )
    parts = spread(terms, plane)
    images, to_high, to_low, square = call(
        assemble_length_kernel, "assemble_length",
        [(2, nx, ny, nz), (2, 2 * nx, nz), (2, 2 * nx, nz), (1, 1)],
        image, image_direction, low, high, coarse_inner, pin=(0, 3),
    )
    low, high = exchange(to_high, to_low, "gy")
    (terms,) = call(spread_sum_kernel, "sum_terms", [(n_line, 1, nz)], parts, low)
    parts = spread(terms, "gx")
    images, to_high, to_low, solution = call(
        assemble_across_kernel, "assemble_across", [(2, nx, ny, nz), (1, 2 * rows), (1, 2 * rows)],
        images, low, high, solution, keep=(3,), pin=(0,),
    )
    low, high = exchange(to_high, to_low, "gz")
    (images,) = call(
        assemble_depth_kernel, "assemble_depth", [images.shape], images, low, high, pin=(0,)
    )
    return tuple(
        call(
            update_kernel, "update", [direction.shape] * 3,
            prior_inner, parts, square, images, residual, solution, direction, z, smem=(0,),
        )
    )


def solution(mesh):
    whole = P("gx", "gy", "gz")
    in_specs = (
        whole,
        whole,
        whole,
        P(None, "gx", "gy", "gz"),
        whole,
        P(),
        whole,
        whole,
        P(("gx", "gy", "gz"), None, None),
        P(("gx", "gy", "gz")),
        P(),
    )
    return jax.shard_map(
        body, mesh=mesh, in_specs=in_specs, out_specs=(whole, whole, whole), check_vma=False
    )
```

```python
import functools

import jax
import jax.numpy as jnp
import numpy as np
from jax import lax
from jax.experimental import pallas as pl
from jax.experimental.pallas import tpu as pltpu
from jax.sharding import PartitionSpec as P

HIGH = lax.Precision.HIGHEST
N = 8
E = 10
F32 = jnp.float32


def cheb_matrix():
    count = 8
    points = np.cos(np.pi * np.arange(count) / (count - 1))
    signs = np.array([2.0, 1, 1, 1, 1, 1, 1, 2.0]) * (-1.0) ** np.arange(count)
    differ = points[:, None] - points[None, :] + np.eye(count)
    matrix = np.outer(signs, 1.0 / signs) / differ
    matrix = matrix - np.eye(count) * np.sum(matrix, axis=1)[:, None]
    return (0.25 * matrix).astype(np.float32)


def extended_positions(count):
    length = N * count
    result = []
    for element in range(count):
        for node in [N * element - 2, *range(N * element, N * element + N), N * element + N + 1]:
            result.append(length if node < 0 else length + 1 if node >= length else node)
    return np.array(result)


def inside_positions(count):
    return np.concatenate([np.arange(E * e + 1, E * e + N + 1) for e in range(count)])


def one_hot(index, size):
    return (np.asarray(index)[:, None] == np.arange(size)[None, :]).astype(np.float32)


def up8(count):
    return -(-count // 8) * 8


def mm(a, b, ca=1, cb=0):
    return lax.dot_general(
        a, b, (((ca,), (cb,)), ((), ())), precision=HIGH, preferred_element_type=F32
    )


def halves(a):
    high = a.astype(jnp.bfloat16)
    return high, (a - high.astype(F32)).astype(jnp.bfloat16)


def mm3(a, b):
    (a_high, a_low), (b_high, b_low) = halves(a), halves(b)

    def product(x, y):
        return jnp.dot(x, y, preferred_element_type=F32)

    return product(a_high, b_high) + (product(a_high, b_low) + product(a_low, b_high))


def call(kernel, name, outs, *args, smem=(), load=(), keep=(), scratch=(), pin=(), store=(), idle=(), numbers=()):
    count, n_out, n_keep = len(args), len(outs), len(keep)
    moved = sorted((*load, *keep, *numbers))
    vmem = pl.BlockSpec(memory_space=pltpu.VMEM)

    def whole(*refs):
        inside, results = list(refs[:count]), refs[count : count + n_out]
        kept = refs[count + n_out : count + n_out + n_keep]
        rest = list(refs[count + n_out + n_keep :])
        sems = rest.pop() if moved or store else None
        written = list(results)
        for i in store:
            written[i] = rest.pop()
        copies = {}
        for at, i in enumerate(moved):
            target = kept[keep.index(i)] if i in keep else rest.pop()
            copies[i] = pltpu.make_async_copy(inside[i], target, sems.at[at])
            copies[i].start()
            inside[i] = target
        waiting = dict(copies)

        def ready(*which):
            for i in which:
                if i in waiting:
                    waiting.pop(i).wait()

        kernel(ready, *inside, *written, *rest)
        ready(*moved)
        copies = [
            pltpu.make_async_copy(written[i], results[i], sems.at[len(moved) + at])
            for at, i in enumerate(store)
        ]
        for copy in copies:
            copy.start()
        for copy in copies:
            copy.wait()

    buffers = [
        (pltpu.SMEM if i in numbers else pltpu.VMEM)(args[i].shape, args[i].dtype)
        for i in moved
        if i not in keep
    ]
    specs = []
    for i in range(count):
        space = pltpu.SMEM if i in smem else pltpu.HBM if i in (*moved, *idle) else pltpu.VMEM
        specs.append(pl.BlockSpec(memory_space=space))
    args = [
        pltpu.with_memory_space_constraint(a, pltpu.HBM) if i in (*moved, *idle) else a
        for i, a in enumerate(args)
    ]
    size = sum(int(np.prod(a.shape)) * 4 for a in args) + sum(int(np.prod(o)) * 4 for o in outs)
    return pl.pallas_call(
        whole,
        out_shape=[
            pltpu.VMEM(o, F32)
            if i in pin
            else pltpu.HBM(o, F32)
            if i in store
            else jax.ShapeDtypeStruct(o, F32)
            for i, o in enumerate(outs)
        ]
        + [pltpu.VMEM(args[i].shape, args[i].dtype) for i in keep],
        in_specs=specs,
        out_specs=[
            pl.BlockSpec(memory_space=pltpu.HBM) if i in store else vmem
            for i in range(n_out + n_keep)
        ],
        scratch_shapes=[
            *scratch,
            *buffers[::-1],
            *[pltpu.VMEM(outs[i], F32) for i in store[::-1]],
            *([pltpu.SemaphoreType.DMA((len(moved) + len(store),))] if moved or store else []),
        ],
        cost_estimate=pl.CostEstimate(flops=0, bytes_accessed=size, transcendentals=0),
        compiler_params=pltpu.CompilerParams(vmem_limit_bytes=24 * 2**20),
        name=name,
    )(*args)


def coarse_kernel(ready, blocks, me, residual, ids, values, kept, payload, ids_wide):
    nx, ny, nz = residual.shape
    ex, ey = nx // N, ny // N
    ez = ids.shape[1]
    n_stored, coarse, _ = values.shape
    head = n_stored + 1
    n_line = payload.shape[0] // (head + ny)
    widen = (
        lax.broadcasted_iota(jnp.int32, (ez, nz), 1) // N
        == lax.broadcasted_iota(jnp.int32, (ez, nz), 0)
    ).astype(F32)
    at = me[0]
    ready(3)
    wide = mm(ids[...].astype(F32), widen)
    ids_wide[...] = wide
    unknown = lax.broadcasted_iota(jnp.int32, (coarse, nz), 0).astype(F32)
    total = jnp.zeros((coarse, nz), F32)
    ready(2)

    @pl.when(at + 1 < n_line)
    def _():
        for y in range(ny):
            payload[(at + 1) * (head + ny) + head + y] = residual[nx - 2, y : y + 1, :]

    @pl.when(at > 0)
    def _():
        for y in range(ny):
            payload[(at - 1) * (head + ny) + head + y] = residual[1, y : y + 1, :]

    for a in range(ex):
        for b in range(ey):
            part = jnp.sum(residual[a * N : a * N + N, b * N : b * N + N, :], axis=(0, 1))[None]
            q = a * ey + b
            total = total + jnp.where(jnp.abs(unknown - wide[q : q + 1]) < 0.5, part, 0.0)
    coarse_residual = jnp.sum(total, axis=1, keepdims=True)
    ready(4)
    ready(0)
    lane = lax.broadcasted_iota(jnp.int32, (1, nz), 1)
    numbers = jnp.zeros((1, nz), F32)
    for k in range(n_stored):
        numbers = jnp.where(lane == n_stored * at + k, blocks[k].astype(F32), numbers)
    for k in range(head):
        if k < n_stored:
            line = jnp.sum(values[k] * coarse_residual, axis=0, keepdims=True)
        else:
            line = numbers
        for i in range(n_line):
            payload[i * (head + ny) + k] = line


def line_kernel(
    n_stored, ready, me, parts, residual, after1, after2, dense, x_low, x_high, to_high, to_low, rows
):
    nx, ny, nz = residual.shape
    head = n_stored + 1
    size = head + ny
    n_line = parts.shape[0] // size
    at = me[0]
    numbers = jnp.zeros((1, nz), F32)
    if n_line * n_stored < nz:
        rows[n_line * n_stored :, :] = jnp.zeros((nz - n_line * n_stored, nz), F32)
    for i in range(n_line):
        numbers = numbers + parts[i * size + n_stored]
        for k in range(n_stored):
            rows[i * n_stored + k : i * n_stored + k + 1, :] = parts[i * size + k]
    n_blocks = dense.shape[0] * dense.shape[1]
    block = lax.broadcasted_iota(jnp.int32, (n_blocks, nz), 0).astype(F32)
    place = (jnp.abs(block - numbers) < 0.5).astype(F32)
    dense[...] = mm(place, rows[...]).reshape(dense.shape)
    before, behind = jnp.maximum(at - 1, 0), jnp.minimum(at + 1, n_line - 1)
    for y in range(ny):
        x_low[y : y + 1] = jnp.where(at > 0, parts[before * size + head + y], 0.0)
        x_high[y : y + 1] = jnp.where(at + 1 < n_line, parts[behind * size + head + y], 0.0)
    for out, y in ((to_high, ny - 2), (to_low, 1)):
        out[...] = jnp.zeros_like(out)
        out[:nx] = residual[:, y, :]
        out[nx : nx + 1] = x_low[y : y + 1]
        out[nx + 1 : nx + 2] = x_high[y : y + 1]


def spread_sum_kernel(ready, parts, after, out):
    total = jnp.sum(parts[...], axis=0)
    for i in range(out.shape[0]):
        out[i] = total


def plane_kernel(
    ready, parts, residual, x_low, x_high, y_low, y_high, owned, every, to_high, to_low
):
    total = jnp.sum(parts[...], axis=0)
    for i in range(owned.shape[0]):
        owned[i] = total
    nx, ny, nz = residual.shape
    at = 0
    for ref in (None, x_low, x_high, y_low, y_high):
        block = residual[...].reshape(nx * ny, nz) if ref is None else ref[...]
        every[at : at + block.shape[0]] = block
        at += block.shape[0]
    row = lax.broadcasted_iota(jnp.int32, (8, nz), 0)
    lane = lax.broadcasted_iota(jnp.int32, (8, nz), 1)
    pick = ((row == 0) & (lane == nz - 2)) | ((row == 1) & (lane == 1))
    ends = mm(pick.astype(F32), every[...], 1, 1)
    to_high[...] = ends[0:1]
    to_low[...] = ends[1:2]


def matrices_kernel(
    ready, basis, tile2, mask2, tilez, maskz, row_x, row_y, col_x, col_y, out_x, out_y, col_z, in_z,
    to_spectral, from_spectral, to_z, from_z,
):
    ready(*range(13))
    flat2 = mm(mm(tile2[...], basis[...]), tile2[...], 1, 1) * mask2[...]
    flatz = mm(mm(tilez[...], basis[...]), tilez[...], 1, 1) * maskz[...]
    to_x = mm(row_x[...], mm(flat2, col_x[...], 0, 0))
    to_y = mm(row_y[...], mm(flat2, col_y[...], 0, 0))
    to_spectral[...] = to_x * to_y
    from_x = mm(mm(out_x[...], flat2), row_x[...], 1, 1)
    from_y = mm(mm(out_y[...], flat2), row_y[...], 1, 1)
    from_spectral[...] = from_x * from_y
    to_z[...] = mm(col_z[...], flatz)
    from_z[...] = mm(flatz, in_z[...], 0, 0)


def spectral_kernel(ready, every, to_spectral, to_z, spectral):
    ready(1, 2)
    spectral[...] = mm3(mm3(to_spectral[...], every[...]), to_z[: every.shape[1], :])


def solve_kernel(
    ready, inside, z_low, z_high, to_spectral, from_spectral, to_z, from_z, sums, local_part,
    inner, wide
):
    n_x, n_y, n_z = sums.shape
    wide[...] = jnp.zeros_like(wide)
    row = lax.broadcasted_iota(jnp.int32, (8, z_low.shape[1]), 0)
    ends = jnp.where(row == 0, z_low[...], jnp.where(row == 1, z_high[...], 0.0))
    ready(3, 5)
    spectral = inside[...] + mm(mm(to_spectral[...], ends, 1, 1), to_z[to_z.shape[0] - 8 :, :])
    ready(7)
    wide[:, :n_y, :] = sums[...]
    weighted = wide[...].reshape(-1, n_z) * spectral
    line = jnp.sum(weighted * spectral, axis=0, keepdims=True)
    wide_line = jnp.concatenate([line, jnp.zeros((1, 256 - n_z), F32)], axis=1)
    inner[...] = folded((wide_line[:, :128] + wide_line[:, 128:])[None])
    ready(4, 6)
    local_part[...] = mm3(mm3(from_spectral[...], weighted), from_z[...])


def derive(matrix, slabs):
    result = []
    for first in range(0, len(slabs), N):
        for i in range(N):
            terms = [float(matrix[i, j]) * slabs[first + j] for j in range(N)]
            while len(terms) > 1:
                terms = [a + b for a, b in zip(terms[::2], terms[1::2])]
            result.append(terms[0])
    return result


def operator(source, conductance, mass, ky, ky_t, kz, kz_t, target):
    nx, ny, nz = source.shape
    rows = nx * ny
    cheb = cheb_matrix()
    flat = source[...].reshape(rows, nz)
    along_y = mm(ky[...], flat) * conductance[1].reshape(rows, nz)
    along_z = mm(flat, kz_t[...]) * conductance[2].reshape(rows, nz)
    along_x = [g * conductance[0, x] for x, g in enumerate(derive(cheb, [source[x] for x in range(nx)]))]
    yz = mm(ky_t[...], along_y) + mm(along_z, kz[...])
    for x, value in enumerate(derive(cheb.T, along_x)):
        target[x] = mass[x] * source[x] + value + yz[x * ny : (x + 1) * ny]


def operator_kernel(ready, direction, conductance, mass, ky, ky_t, kz, kz_t, image, third):
    ready(0, 1, 2, 3, 4, 5, 6)
    operator(direction, conductance, mass, ky, ky_t, kz, kz_t, image)
    third[...] = folded(direction[...] * image[...])


def total_of(values):
    return jnp.sum(jnp.sum(values, axis=0, keepdims=True), axis=1, keepdims=True)


def correct_kernel(
    ready, blocks, coarse_inner, values, ids_wide, local_part, direction, image_direction,
    conductance, mass, ky, ky_t, kz, kz_t,
    z_out, image_out, to_high, to_low,
):
    nx, ny, nz = direction.shape
    rows = nx * ny
    n_stored, coarse, block = values.shape
    total = jnp.zeros((coarse, block), F32)
    for k in range(n_stored):
        total = total + values[k] * coarse_inner[pl.ds(blocks[k], 1), :]
    solution = jnp.sum(total, axis=1, keepdims=True)
    unknown = lax.broadcasted_iota(jnp.int32, (coarse, nz), 0).astype(F32)
    ey = ny // N
    for a in range(nx // N):
        for b in range(ey):
            q = a * ey + b
            hit = jnp.abs(unknown - ids_wide[q : q + 1, :]) < 0.5
            line = jnp.sum(jnp.where(hit, solution, 0.0), axis=0, keepdims=True)
            for x in range(N):
                at = (a * N + x) * ny + b * N
                z_out[a * N + x, b * N : b * N + N, :] = local_part[at : at + N, :] + line
    operator(z_out, conductance, mass, ky, ky_t, kz, kz_t, image_out)
    for out, x in ((to_high, nx - 1), (to_low, 0)):
        out[0, :ny] = image_out[x]
        out[1, :ny] = image_direction[x]


def folded(values):
    line = jnp.sum(jnp.sum(values, axis=0), axis=0, keepdims=True)
    line = line + pltpu.roll(line, 64, 1)
    return line + pltpu.roll(line, 32, 1)


def terms_kernel(ready, z, image, direction, image_direction, inner_local, third, after, terms):
    first = folded(z[...] * image[...])
    second = folded(z[...] * image_direction[...] + direction[...] * image[...])
    group = lax.broadcasted_iota(jnp.int32, (1, terms.shape[2]), 1) // 32
    line = jnp.where(group == 0, inner_local[...], third[...])
    line = jnp.where(group == 1, first, jnp.where(group == 2, second, line))
    for i in range(terms.shape[0]):
        terms[i] = line


def assemble_length_kernel(
    ready, image, image_direction, low, high, coarse_inner, out, to_high, to_low, square
):
    square[...] = total_of(coarse_inner[...] * coarse_inner[...])
    nx, ny, nz = image.shape
    for i, ref in ((0, image), (1, image_direction)):
        out[i] = ref[...]
        for x in range(nx):
            if x % N == N - 1:
                out[i, x] = ref[x] + (ref[x + 1] if x + 1 < nx else high[i, :ny])
            elif x % N == 0:
                out[i, x] = ref[x] + (ref[x - 1] if x else low[i, :ny])
        to_high[i, :nx] = out[i, :, ny - 1, :]
        to_low[i, :nx] = out[i, :, 0, :]


def assemble_across_kernel(ready, images, low, high, solution, out, to_high, to_low):
    _, nx, ny, nz = images.shape
    out[...] = images[...]
    for i in range(2):
        for y in range(ny):
            if y % N == N - 1:
                other = images[i, :, y + 1, :] if y + 1 < ny else high[i, :nx]
            elif y % N == 0:
                other = images[i, :, y - 1, :] if y else low[i, :nx]
            else:
                continue
            out[i, :, y, :] = images[i, :, y, :] + other
    row = lax.broadcasted_iota(jnp.int32, (8, nz), 0)
    lane = lax.broadcasted_iota(jnp.int32, (8, nz), 1)
    pick = ((row == 0) & (lane == nz - 1)) | ((row == 1) & (lane == 0))
    ends = mm(pick.astype(F32), out[...].reshape(2 * nx * ny, nz), 1, 1)
    to_high[...] = ends[0:1]
    to_low[...] = ends[1:2]


def assemble_depth_kernel(ready, images, low, high, out):
    _, nx, ny, nz = images.shape
    rows = 2 * nx * ny
    image = images[...].reshape(rows, nz)
    row = lax.broadcasted_iota(jnp.int32, (8, rows), 0)
    ends = jnp.where(row == 0, low[...], jnp.where(row == 1, high[...], 0.0))
    row = lax.broadcasted_iota(jnp.int32, (8, nz), 0)
    lane = lax.broadcasted_iota(jnp.int32, (8, nz), 1)
    place = ((row == 0) & (lane == 0)) | ((row == 1) & (lane == nz - 1))
    outer = mm(jnp.transpose(ends), place.astype(F32))
    lane = lax.broadcasted_iota(jnp.int32, (rows, nz), 1)
    above = jnp.where((lane % N == N - 1) & (lane < nz - 1), pltpu.roll(image, nz - 1, 1), 0.0)
    below = jnp.where((lane % N == 0) & (lane > 0), pltpu.roll(image, 1, 1), 0.0)
    out[...] = (image + above + below + outer).reshape(out.shape)


def update_kernel(
    ready, prior, terms, square, images, residual, solution, direction, z,
    new_solution, new_residual, new_direction,
):
    lane = lax.broadcasted_iota(jnp.int32, (1, terms.shape[2]), 1)
    sums = jnp.sum(terms[...], axis=0)

    def term(i):
        return jnp.sum(jnp.where(lane // 32 == i, sums, 0.0), axis=1, keepdims=True)

    inner = term(0) + square[...]
    ratio = inner / prior[0]
    alpha = inner / (term(1) + ratio * term(2) + ratio * ratio * term(3))
    ratio, alpha = ratio[None], alpha[None]
    new = z[...] + ratio * direction[...]
    new_direction[...] = new
    new_solution[...] = solution[...] + alpha * new
    new_residual[...] = residual[...] - alpha * (images[0] + ratio * images[1])


def shifts(axis):
    count = lax.axis_size(axis)
    forward = [(i, i + 1) for i in range(count - 1)]
    return forward, [(b, a) for a, b in forward]


def exchange(to_high, to_low, axis):
    forward, backward = shifts(axis)
    return lax.ppermute(to_high, axis, forward), lax.ppermute(to_low, axis, backward)


def spread(values, axes):
    return lax.all_to_all(values, axes, 0, 0, tiled=False)


def body(
    residual,
    solution,
    direction,
    conductance,
    mass_term,
    eigen_basis,
    inverse_eigen_sums,
    element_coarse_index,
    xxt_values,
    xxt_blocks,
    prior_inner,
):
    nx, ny, nz = residual.shape
    ex, ey, ez = nx // N, ny // N, nz // N
    rows = nx * ny
    plane = ("gy", "gz")
    n_plane, n_line = lax.axis_size(plane), lax.axis_size("gx")
    coarse_count, block = xxt_values.shape[1:]
    n_blocks = coarse_count * n_plane * n_line // block
    own = n_blocks // n_plane

    ids = element_coarse_index.reshape(ex * ey, ez)
    me = lax.axis_index("gx").astype(jnp.int32).reshape(1)
    head = xxt_values.shape[0] + 1
    assert xxt_values.shape[0] * n_line <= nz
    payload, ids_wide, residual, xxt_values, block_numbers = call(
        coarse_kernel, "coarse_restrict",
        [(n_line * (head + ny), 1, nz), (ex * ey, nz)],
        xxt_blocks, me, residual, ids, xxt_values, xxt_blocks, smem=(1,), load=(3,), keep=(2, 4, 5),
        pin=(1,),
        numbers=(0,),
    )
    parts = spread(payload.reshape(n_line, head + ny, 1, nz), "gx").reshape(payload.shape)

    cheb = cheb_matrix()
    ky = np.kron(np.eye(nx, dtype=np.float32), np.kron(np.eye(ey, dtype=np.float32), cheb))
    kz = np.kron(np.eye(ez, dtype=np.float32), cheb)
    tables = [jnp.asarray(np.ascontiguousarray(t)) for t in (ky, ky.T, kz, kz.T)]
    image_direction, third, direction, conductance, mass_term, *tables = call(
        operator_kernel, "operator_direction", [direction.shape, (1, nz)],
        direction, conductance, mass_term, *tables, keep=tuple(range(7)), pin=(0, 1),
    )

    face = up8(nx + 2)
    n_every = rows + 2 * ny + 2 * face
    pad = [-1] * (face - nx - 2)
    line = [*range(nx), nx, nx + 1, *pad]
    cols_x = np.array([*np.repeat(np.arange(nx), ny), *[nx] * ny, *[nx + 1] * ny, *line, *line])
    cols_y = np.array(
        [*np.tile(np.arange(ny), nx), *range(ny), *range(ny), *[ny] * face, *[ny + 1] * face]
    )
    n_x, n_y, n_z = inverse_eigen_sums.shape
    high_y = up8(n_y)
    place_y = np.tile(np.arange(high_y), n_x)
    row_x = one_hot(np.repeat(np.arange(n_x), high_y), n_x) * (place_y < n_y)[:, None]
    row_y = one_hot(place_y, n_y)
    col_x = (extended_positions(ex)[:, None] == cols_x[None, :]).astype(np.float32)
    col_y = (extended_positions(ey)[:, None] == cols_y[None, :]).astype(np.float32)
    assert ex == ey
    to_spectral, from_spectral, to_z, from_z = call(
        matrices_kernel, "basis_matrices",
        [(n_x * high_y, n_every), (rows, n_x * high_y), (nz + 8, n_z), (n_z, nz)],
        eigen_basis,
        *map(
            jnp.asarray,
            (
                np.tile(np.eye(E, dtype=np.float32), (ex, 1)),
                np.kron(np.eye(ex), np.ones((E, E))).astype(np.float32),
                np.tile(np.eye(E, dtype=np.float32), (ez, 1)),
                np.kron(np.eye(ez), np.ones((E, E))).astype(np.float32),
                row_x.astype(np.float32),
                row_y,
                col_x,
                col_y,
                one_hot(np.repeat(inside_positions(ex), ny), n_x),
                one_hot(np.tile(inside_positions(ey), nx), n_y),
                np.ascontiguousarray(one_hot(extended_positions(ez), nz + 8).T),
                np.ascontiguousarray(one_hot(inside_positions(ez), n_z).T),
            ),
        ),
        load=tuple(range(13)), store=(0, 1, 2, 3),
    )

    dense, x_low, x_high, to_high, to_low = call(
        functools.partial(line_kernel, xxt_values.shape[0]), "line_sum",
        [(n_plane, own, block), (ny, nz), (ny, nz), (face, nz), (face, nz)],
        me, parts, residual, image_direction, from_z, smem=(0,), pin=(1, 2), idle=(4,),
        scratch=(pltpu.VMEM((nz, nz), F32),),
    )
    parts = spread(dense, plane)
    y_low, y_high = exchange(to_high, to_low, "gy")
    owned, every, to_high, to_low = call(
        plane_kernel, "plane_sum",
        [(n_plane, own, block), (n_every, nz), (1, n_every), (1, n_every)],
        parts, residual, x_low, x_high, y_low, y_high, pin=(1,),
    )
    coarse_inner = spread(owned, plane).reshape(n_blocks, block)
    z_low, z_high = exchange(to_high, to_low, "gz")
    (spectral,) = call(
        spectral_kernel, "element_spectral", [(n_x * high_y, n_z)],
        every, to_spectral, to_z, load=(1, 2), pin=(0,),
    )
    local_part, inner_local = call(
        solve_kernel, "element_solve", [(rows, nz), (1, nz)],
        spectral, z_low, z_high, to_spectral, from_spectral, to_z, from_z, inverse_eigen_sums,
        load=(3, 4, 5, 6, 7), pin=(0, 1), scratch=(pltpu.VMEM((n_x, high_y, n_z), F32),),
    )

    z, image, to_high, to_low = call(
        correct_kernel, "coarse_correct",
        [direction.shape, direction.shape, (2, 4 * ny, nz), (2, 4 * ny, nz)],
        block_numbers, coarse_inner, xxt_values, ids_wide, local_part, direction,
        image_direction, conductance, mass_term, *tables, smem=(0,), pin=(0, 1),
    )
    low, high = exchange(to_high, to_low, "gx")
    (terms,) = call(
        terms_kernel, "terms", [(n_plane, 1, nz)],
        z, image, direction, image_direction, inner_local, third, low,
    )
    parts = spread(terms, plane)
    images, to_high, to_low, square = call(
        assemble_length_kernel, "assemble_length",
        [(2, nx, ny, nz), (2, 2 * nx, nz), (2, 2 * nx, nz), (1, 1)],
        image, image_direction, low, high, coarse_inner, pin=(0, 3),
    )
    low, high = exchange(to_high, to_low, "gy")
    (terms,) = call(spread_sum_kernel, "sum_terms", [(n_line, 1, nz)], parts, low)
    parts = spread(terms, "gx")
    images, to_high, to_low, solution = call(
        assemble_across_kernel, "assemble_across", [(2, nx, ny, nz), (1, 2 * rows), (1, 2 * rows)],
        images, low, high, solution, keep=(3,), pin=(0,),
    )
    low, high = exchange(to_high, to_low, "gz")
    (images,) = call(
        assemble_depth_kernel, "assemble_depth", [images.shape], images, low, high, pin=(0,)
    )
    return tuple(
        call(
            update_kernel, "update", [direction.shape] * 3,
            prior_inner, parts, square, images, residual, solution, direction, z, smem=(0,),
        )
    )


def solution(mesh):
    whole = P("gx", "gy", "gz")
    in_specs = (
        whole,
        whole,
        whole,
        P(None, "gx", "gy", "gz"),
        whole,
        P(),
        whole,
        whole,
        P(("gx", "gy", "gz"), None, None),
        P(("gx", "gy", "gz")),
        P(),
    )
    return jax.shard_map(
        body, mesh=mesh, in_specs=in_specs, out_specs=(whole, whole, whole), check_vma=False
    )
```
